128 devices in a mesh: req: 8 (over y, core), unit: 16 (over x, z).
Axes of the slice: x: 4, y: 4, z: 4, core: 2. Of those that a mesh axis runs over, the one named last changes fastest.
Arguments:
- hidden: bfloat16 [6144, 2048], P(('req', 'unit')), may hold values from -6 to 6
- tree_q: bfloat16 [6144, 2048], P(('req', 'unit')), may hold values from -1.5 to 1.5
- tree_kv: bfloat16 [6144, 2, 512], P(('req', 'unit')), may hold values from -1.5 to 1.5
- kv_cache: bfloat16 [128, 2, 2, 2048, 256], P(('req', 'unit')), may hold values from -1.5 to 1.5
- cache_lengths: int32 [128], P(('req', 'unit')), may hold values from 1 to 2048, as said below
- tree_parents: int32 [128, 48], P(('req', 'unit')), may hold values from 0 to 46, as said below
- accepted: int32 [128, 4], P(('req', 'unit')), may hold values from 0 to 47, as said below
- tenant_ranges: int32 [128, 2], replicated, may hold values from 0 to 262144, as said below
- out_weight: bfloat16 [2048, 2048], P(None, 'unit'), may hold values from -0.125 to 0.125
- mlp_weights: bfloat16 [3, 2048, 8192], P(None, None, ('req', 'unit')), may hold values from -0.125 to 0.125
- draft_weights: bfloat16 [4, 2048, 2048], P(None, None, 'unit'), may hold values from -0.125 to 0.125
- embedding: bfloat16 [262144, 2048], P(('req', 'unit')), may hold values from -1.1269514 to 1.1269514
- attn_post_gain: bfloat16 [2048], replicated, may hold values from 0.25 to 1.75
- ff_pre_gain: bfloat16 [2048], replicated, may hold values from 0.25 to 1.75
- ff_post_gain: bfloat16 [2048], replicated, may hold values from 0.25 to 1.75
- final_gain: bfloat16 [2048], replicated, may hold values from 0.25 to 1.75
Outputs:
- tree_out: bfloat16 [6144, 2048], P(('req', 'unit'))
- draft_logprobs: bfloat16 [4, 512, 262144], P(None, None, ('req', 'unit'))
The draws below stay inside these ranges and needn't reach their ends.
Inputs may be any that keep to these rules, and one draw needn't show every extreme that they name: A request's cache holds live entries in its first cache_lengths slots; some request fills all 2048. `tree_parents`: node 0 is the root and its own parent; every other node's parent has a smaller index. `accepted`: rising nodes starting at the root 0, each the parent of the next. `tenant_ranges`: column 0 is the first allowed id, column 1 one past the last; each request allows 262144 // 2 ids or more; some request allows all.
All inputs are finite; a program needn't handle non-finite values.
Results may differ from the reference program's by a relative error of at most 0.008.
Values may be sent and summed in bfloat16 or wider, within the bound.
No kernel may reach another device: no remote copies, remote signals or barrier semaphores. Data moves between devices by JAX's collectives and lax.ppermute only.
A program may use at most 128 MiB of HBM per device.

```python
import math
import jax
import jax.numpy as jnp
from jax import lax

D = 2048
QH = 8
KVH = 2
HD = 256
FF = 8192
V = 262144
HEADS = 4
TREE = 48
ACC = 4
CACHE = 2048
REQUESTS = 128
TOKENS = 6144


def tree_shapes(key):
    base_key = jax.random.fold_in(key, 7)
    request_keys = jax.random.split(base_key, REQUESTS)

    def one_request(request_key):
        parent_key, path_key = jax.random.split(request_key)
        node_ids = jnp.arange(TREE, dtype=jnp.int32)
        parents = jax.random.randint(parent_key, (TREE,), 0, jnp.maximum(node_ids, 1))
        chosen = jnp.sort(jax.random.permutation(path_key, TREE - 1)[:ACC - 1] + 1)
        path_nodes = jnp.concatenate([jnp.zeros((1,), jnp.int32), chosen.astype(jnp.int32)])
        parents = parents.at[path_nodes[1:]].set(path_nodes[:-1])
        return (parents.astype(jnp.int32), path_nodes.astype(jnp.int32))
    return jax.vmap(one_request)(request_keys)


def draw_tree_parents(key, part):
    return tree_shapes(key)[0]


def draw_accepted(key, part):
    return tree_shapes(key)[1]


def draw_cache_lengths(key, part):
    first_key, second_key = jax.random.split(jax.random.fold_in(key, 3))
    lengths = jax.random.randint(first_key, (REQUESTS,), 1, CACHE // 2 + 1)
    longest = jax.random.randint(second_key, (), 0, REQUESTS)
    return lengths.at[longest].set(CACHE).astype(jnp.int32)


def draw_tenant_ranges(key, part):
    span_key, start_key, full_key = jax.random.split(jax.random.fold_in(key, 5), 3)
    spans = jax.random.randint(span_key, (REQUESTS,), V // 2, V + 1)
    starts = jax.random.randint(start_key, (REQUESTS,), 0, V - spans + 1)
    widest = jax.random.randint(full_key, (), 0, REQUESTS)
    spans = spans.at[widest].set(V)
    starts = starts.at[widest].set(0)
    return jnp.stack([starts, starts + spans], axis=1).astype(jnp.int32)


def draw_embedding(key, part):
    first_key, second_key = jax.random.split(jax.random.fold_in(key, 11))
    vocab_pos = jnp.arange(V, dtype=jnp.float32)[:, None]
    rising = 1.0 + 2.0 * vocab_pos / V
    spread = jnp.exp(jax.random.uniform(second_key, (V, 1), minval=math.log(0.7), maxval=math.log(1.4)))
    base = jnp.clip(jax.random.normal(first_key, (V, D)), -4.0, 4.0)
    return (base * rising * spread * (3.0 / math.sqrt(D))).astype(jnp.bfloat16)


def level_of(rng, shape, cuts, least, top_value):
    level, own = 1.0, jax.random.fold_in(rng, 6)
    for position, blocks in cuts:
        steps = jnp.exp(jax.random.uniform(jax.random.fold_in(own, position), (blocks,), jnp.float32, least / len(cuts), top_value / len(cuts)))
        level = level * jnp.repeat(steps, shape[position] // blocks).reshape([-1 if axis == position else 1 for axis in range(len(shape))])
    return level


def bell_draw(rng, shape, scale, limit, shards=(), kind=jnp.bfloat16):
    values = jax.random.normal(rng, shape, jnp.float32) * scale
    if len(shards) > 0:
        values = level_of(rng, shape, shards, -0.22, 0.18) * values
    return jnp.clip(values, min=-limit, max=limit).astype(kind)


def setup_inputs(seed: int = 0) -> dict:
    keys = jax.random.split(jax.random.key(seed), 17)
    return {
        "hidden": bell_draw(keys[0], (TOKENS, D), 1.0, 6.0, ((0, 128),)),
        "tree_q": jnp.clip(jax.random.uniform(keys[1], (TOKENS, QH * HD), jnp.float32, -1.5, 1.5) * level_of(keys[1], (TOKENS, QH * HD), ((0, 128),), -0.4, 0.0), -1.5, 1.5).astype(jnp.bfloat16),
        "tree_kv": jnp.clip(jax.random.uniform(keys[2], (TOKENS, 2, KVH * HD), jnp.float32, -1.5, 1.5) * level_of(keys[2], (TOKENS, 2, KVH * HD), ((0, 128),), -0.4, 0.0), -1.5, 1.5).astype(jnp.bfloat16),
        "kv_cache": jnp.clip(jax.random.uniform(keys[3], (REQUESTS, 2, KVH, CACHE, HD), jnp.float32, -1.5, 1.5) * level_of(keys[3], (REQUESTS, 2, KVH, CACHE, HD), ((0, 128),), -0.4, 0.0), -1.5, 1.5).astype(jnp.bfloat16),
        "cache_lengths": draw_cache_lengths(jax.random.fold_in(keys[16], 71), 0),
        "tree_parents": draw_tree_parents(jax.random.fold_in(keys[16], 71), 0),
        "accepted": draw_accepted(jax.random.fold_in(keys[16], 71), 0),
        "tenant_ranges": draw_tenant_ranges(jax.random.fold_in(keys[16], 71), 0),
        "out_weight": bell_draw(keys[8], (QH * HD, D), (QH * HD) ** -0.5, 0.125, ((1, 16),)),
        "mlp_weights": bell_draw(keys[9], (3, D, FF), D ** -0.5, 0.125, ((2, 128),)),
        "draft_weights": bell_draw(keys[10], (HEADS, D, D), D ** -0.5, 0.125, ((2, 16),)),
        "embedding": draw_embedding(jax.random.fold_in(keys[16], 71), 0),
        "attn_post_gain": jnp.clip(1.0 + 0.15 * jax.random.normal(keys[12], (D,), jnp.float32), 0.25, 1.75).astype(jnp.bfloat16),
        "ff_pre_gain": jnp.clip(1.0 + 0.15 * jax.random.normal(keys[13], (D,), jnp.float32), 0.25, 1.75).astype(jnp.bfloat16),
        "ff_post_gain": jnp.clip(1.0 + 0.15 * jax.random.normal(keys[14], (D,), jnp.float32), 0.25, 1.75).astype(jnp.bfloat16),
        "final_gain": jnp.clip(1.0 + 0.15 * jax.random.normal(keys[15], (D,), jnp.float32), 0.25, 1.75).astype(jnp.bfloat16),
    }


EPS = 1e-06
SOFTCAP = 30.0

def rms_scale(values, gain):
    floats = values.astype(jnp.float32)
    return floats * lax.rsqrt(lax.optimization_barrier(jnp.mean(floats * floats, axis=-1, keepdims=True)) + EPS) * gain.astype(jnp.float32)

def ancestor_table(parents):
    tree_size = parents.shape[-1]
    node_ids = jnp.arange(tree_size, dtype=jnp.int32)
    reachable = jnp.maximum((parents[:, None] == node_ids[None, :]).astype(jnp.float32), (node_ids[:, None] == node_ids[None, :]).astype(jnp.float32))
    for doubling in range(max(1, (tree_size - 1).bit_length())):
        reachable = jnp.minimum(jnp.dot(reachable, reachable, precision=lax.Precision.HIGHEST), 1.0)
    return reachable

def rounded_weights(values):
    return lax.optimization_barrier(values.astype(jnp.bfloat16)).astype(jnp.float32)

def attend_request(query, tree_pairs, cache, length, parents):
    tree_size = query.shape[0]
    group_size = QH // KVH
    score_scale = HD ** (-0.5)
    queries = query.astype(jnp.float32).reshape(tree_size, KVH, group_size, HD)
    cache_keys = cache[0].astype(jnp.float32)
    cache_values = cache[1].astype(jnp.float32)
    cache_scores = jnp.exp(jnp.einsum('tkgd,ksd->kgts', queries, cache_keys) * score_scale)
    slot_ids = jnp.arange(CACHE, dtype=jnp.int32)
    cache_probs = jnp.where(slot_ids < length, cache_scores, 0.0)
    tree_keys = tree_pairs[:, 0].astype(jnp.float32).reshape(tree_size, KVH, HD)
    tree_values = tree_pairs[:, 1].astype(jnp.float32).reshape(tree_size, KVH, HD)
    tree_scores = jnp.exp(jnp.einsum('tkgd,skd->kgts', queries, tree_keys) * score_scale)
    tree_probs = tree_scores * ancestor_table(parents)
    denominator = lax.optimization_barrier(jnp.sum(cache_probs, axis=3)) + lax.optimization_barrier(jnp.sum(tree_probs, axis=3))
    numerator = jnp.einsum('kgts,ksd->tkgd', rounded_weights(cache_probs), cache_values)
    numerator = numerator + jnp.einsum('kgts,skd->tkgd', rounded_weights(tree_probs), tree_values)
    result = numerator / jnp.transpose(denominator, (2, 0, 1))[..., None]
    return result.reshape(tree_size, QH * HD).astype(jnp.bfloat16)

def reference(hidden, tree_q, tree_kv, kv_cache, cache_lengths, tree_parents, accepted, tenant_ranges, out_weight, mlp_weights, draft_weights, embedding, attn_post_gain, ff_pre_gain, ff_post_gain, final_gain):
    queries = tree_q.reshape(REQUESTS, TREE, QH * HD)
    tree_pairs = tree_kv.reshape(REQUESTS, TREE, 2, KVH * HD)
    attended = lax.map(lambda items: attend_request(*items), (queries, tree_pairs, kv_cache, cache_lengths, tree_parents))
    attended = attended.reshape(TOKENS, QH * HD)
    projected = jnp.dot(attended, out_weight, preferred_element_type=jnp.float32).astype(jnp.bfloat16)
    first = (hidden.astype(jnp.float32) + rms_scale(projected, attn_post_gain)).astype(jnp.bfloat16)
    normed = rms_scale(first, ff_pre_gain).astype(jnp.bfloat16)
    gate_part = jnp.dot(normed, mlp_weights[0], preferred_element_type=jnp.float32)
    upward = jnp.dot(normed, mlp_weights[1], preferred_element_type=jnp.float32)
    active = (jax.nn.gelu(gate_part, approximate=True) * upward).astype(jnp.bfloat16)
    mlp_sum = lax.dot_general(active, mlp_weights[2], (((1,), (1,)), ((), ())), preferred_element_type=jnp.float32)
    tree_out = (first.astype(jnp.float32) + rms_scale(mlp_sum, ff_post_gain)).astype(jnp.bfloat16)
    row_ids = (jnp.arange(REQUESTS, dtype=jnp.int32)[:, None] * TREE + accepted).reshape(-1)
    path_rows = tree_out[row_ids]
    path_normed = rms_scale(path_rows, final_gain).astype(jnp.bfloat16)
    before = jnp.einsum('rd,hde->rhe', path_normed.astype(jnp.float32), draft_weights.astype(jnp.float32))
    drafts = (path_normed.astype(jnp.float32)[:, None, :] + jax.nn.silu(before)).astype(jnp.bfloat16)
    starts = jnp.repeat(tenant_ranges[:, 0], ACC)
    range_ends = jnp.repeat(tenant_ranges[:, 1], ACC)
    vocab_ids = jnp.arange(V, dtype=jnp.int32)
    allowed = (vocab_ids[None, :] >= starts[:, None]) & (vocab_ids[None, :] < range_ends[:, None])

    def one_head(head_rows):
        logits = SOFTCAP * jnp.tanh(jnp.dot(head_rows, embedding.T, preferred_element_type=jnp.float32) / SOFTCAP)
        totals = lax.optimization_barrier(jnp.sum(jnp.where(allowed, jnp.exp(logits), 0.0), axis=1, keepdims=True))
        return jnp.where(allowed, logits - jnp.log(totals), 0.0).astype(jnp.bfloat16)
    draft_logprobs = lax.map(one_head, jnp.transpose(drafts, (1, 0, 2)))
    return (tree_out, draft_logprobs)
```

```python
import jax
import jax.numpy as jnp
from jax import lax
from jax.sharding import Mesh, PartitionSpec as P

QH = 8
KVH = 2
HD = 256
HEADS = 4
ACC = 4

EPS = 1e-06
SOFTCAP = 30.0
BLOCK_SLOTS = 512

Y, CORE, X, Z = 4, 2, 4, 4
XZ = ("x", "z")
YC = ("y", "core")
ALL = ("y", "core", "x", "z")
BF = jnp.bfloat16
F32 = jnp.float32


def rms_scale(values, gain):
    floats = values.astype(F32)
    return (
        floats
        * lax.rsqrt(jnp.mean(floats * floats, axis=-1, keepdims=True) + EPS)
        * gain.astype(F32)
    )


def ancestor_table(parents):
    tree_size = parents.shape[-1]
    node_ids = jnp.arange(tree_size, dtype=jnp.int32)
    reachable = jnp.maximum(
        (parents[:, None] == node_ids[None, :]).astype(BF),
        (node_ids[:, None] == node_ids[None, :]).astype(BF),
    )
    for doubling in range(max(1, (tree_size - 1).bit_length())):
        reachable = jnp.minimum(
            jnp.dot(reachable, reachable, preferred_element_type=F32), 1.0
        ).astype(BF)
    return reachable.astype(F32)


def cache_attention(queries, cache, length):
    slots_total = cache.shape[2]
    block_width = min(BLOCK_SLOTS, slots_total)
    blocks = slots_total // block_width
    score_scale = HD ** (-0.5)
    tree_size = queries.shape[0]
    group_size = queries.shape[2]

    def add_block(block_index, running):
        numerator, denominator = running
        offset = block_index * block_width
        key_block = lax.dynamic_slice_in_dim(cache[0], offset, block_width, 1)
        value_block = lax.dynamic_slice_in_dim(cache[1], offset, block_width, 1)
        scores = jnp.exp(
            jnp.einsum("tkgd,ksd->kgts", queries, key_block, preferred_element_type=F32)
            * score_scale
        )
        slot_ids = offset + jnp.arange(block_width, dtype=jnp.int32)
        weights_now = jnp.where(slot_ids < length, scores, 0.0)
        numerator = numerator + jnp.einsum(
            "kgts,ksd->tkgd",
            weights_now.astype(BF),
            value_block,
            preferred_element_type=F32,
        )
        return (numerator, denominator + jnp.sum(weights_now, axis=3))

    start_state = (
        jnp.zeros((tree_size, KVH, group_size, HD), F32),
        jnp.zeros((KVH, group_size, tree_size), F32),
    )
    return lax.fori_loop(0, blocks, add_block, start_state)


def attention(tree_q, tree_kv, kv_cache, cache_lengths, tree_parents):
    tree_size = tree_q.shape[0]
    group_size = QH // KVH
    queries = tree_q.reshape(tree_size, KVH, group_size, HD)
    numerator, denominator = cache_attention(queries, kv_cache[0], cache_lengths[0])
    tree_keys = tree_kv[:, 0].reshape(tree_size, KVH, HD)
    tree_values = tree_kv[:, 1].reshape(tree_size, KVH, HD)
    tree_scores = jnp.exp(
        jnp.einsum("tkgd,skd->kgts", queries, tree_keys, preferred_element_type=F32)
        * HD ** (-0.5)
    )
    tree_weights = tree_scores * ancestor_table(tree_parents[0])
    numerator = numerator + jnp.einsum(
        "kgts,skd->tkgd", tree_weights.astype(BF), tree_values, preferred_element_type=F32
    )
    denominator = denominator + jnp.sum(tree_weights, axis=3)
    attended = numerator / jnp.transpose(denominator, (2, 0, 1))[..., None]
    return attended.reshape(tree_size, QH * HD).astype(BF)


def ring(values, axis, size, shift):
    return lax.ppermute(values, axis, [((i + shift) % size, i) for i in range(size)])


def spread(values, axes, size):
    copies = lax.optimization_barrier(jnp.broadcast_to(values[None], (size,) + values.shape))
    return lax.all_to_all(copies, axes, split_axis=0, concat_axis=0, tiled=True)


def out_projection(attended, out_weight):
    rows, depth = attended.shape
    width = out_weight.shape[1]
    half = depth // 2
    core, x = lax.axis_index("core"), lax.axis_index("x")
    own_half = lax.dynamic_slice_in_dim(out_weight, core * half, half, 0)
    halves = [own_half] + [ring(own_half, "x", X, shift) for shift in range(1, X)]
    own_weight = jnp.concatenate(halves, axis=1)
    other_weight = ring(own_weight, "core", CORE, 1)
    group = lax.all_gather(attended, "z", axis=0, tiled=True)
    own_part = lax.dynamic_slice_in_dim(group, core * half, half, 1)
    other_part = lax.dynamic_slice_in_dim(group, (1 - core) * half, half, 1)
    columns = (
        jnp.dot(own_part, own_weight, preferred_element_type=F32)
        + jnp.dot(other_part, other_weight, preferred_element_type=F32)
    ).astype(BF)
    back = lax.all_to_all(
        columns.reshape(Z, rows, X * width), "z", split_axis=0, concat_axis=0, tiled=True
    )
    back = back.reshape(Z, rows, X, width)
    placed = []
    for column_x in range(X):
        shift = (column_x - x) % X
        piece = back[:, :, 0]
        for candidate in range(1, X):
            piece = jnp.where(shift == candidate, back[:, :, candidate], piece)
        placed.append(piece)
    return jnp.concatenate([p[z] for p in placed for z in range(Z)], axis=1)


def unit_terms(mlp_rows, weights):
    gate_part = jnp.dot(mlp_rows, weights[0], preferred_element_type=F32)
    upward = jnp.dot(mlp_rows, weights[1], preferred_element_type=F32)
    active = (jax.nn.gelu(gate_part, approximate=True) * upward).astype(BF)
    return lax.dot_general(
        active, weights[2], (((1,), (1,)), ((), ())), preferred_element_type=F32
    ).astype(BF)


def shared_sum(partial, size):
    rows = partial.shape[0] // size
    pieces = lax.all_to_all(
        partial.reshape(size, rows, -1), XZ, split_axis=0, concat_axis=0, tiled=True
    )
    return jnp.sum(pieces.astype(F32), axis=0)


def per_device(
    hidden,
    tree_q,
    tree_kv,
    kv_cache,
    cache_lengths,
    tree_parents,
    accepted,
    tenant_ranges,
    out_weight,
    mlp_weights,
    draft_weights,
    embedding,
    attn_post_gain,
    ff_pre_gain,
    ff_post_gain,
    final_gain,
):
    units = X * Z
    core = lax.axis_index("core")
    unit = lax.axis_index(XZ)
    weights = lax.all_gather(mlp_weights, YC, axis=2, tiled=True)
    attended = attention(tree_q, tree_kv, kv_cache, cache_lengths, tree_parents)
    projected = out_projection(attended, out_weight)
    first = (hidden.astype(F32) + rms_scale(projected, attn_post_gain)).astype(BF)
    normed = rms_scale(first, ff_pre_gain).astype(BF)

    chosen = (
        accepted[0][:, None] == jnp.arange(first.shape[0], dtype=jnp.int32)[None, :]
    ).astype(BF)
    first_path = jnp.dot(chosen, first, preferred_element_type=F32)
    normed_path = jnp.dot(chosen, normed, preferred_element_type=F32).astype(BF)
    path_rows = spread(normed_path, XZ, units).reshape(units * ACC, -1)
    path_sum = shared_sum(unit_terms(path_rows, weights), units)
    path = (first_path + rms_scale(path_sum, ff_post_gain)).astype(BF)
    path_normed = rms_scale(path, final_gain).astype(BF)
    group_path = spread(path_normed, XZ, units).reshape(units * ACC, -1)

    column_width = draft_weights.shape[2]
    before = jnp.einsum("rd,hde->hre", group_path, draft_weights, preferred_element_type=F32)
    own_columns = lax.dynamic_slice_in_dim(group_path, unit * column_width, column_width, 1)
    drafts = (own_columns.astype(F32)[None] + jax.nn.silu(before)).astype(BF)
    drafts = spread(drafts, "y", Y)
    drafts = jnp.transpose(drafts, (1, 0, 2, 3)).reshape(HEADS, Y * units * ACC, column_width)
    own_drafts = lax.all_gather(drafts, XZ, axis=2, tiled=True)
    other_drafts = ring(own_drafts, "core", CORE, 1)

    mlp_rows = lax.all_gather(normed, XZ, axis=0, tiled=True)
    partial = unit_terms(mlp_rows, weights)
    partial, own_drafts = lax.optimization_barrier((partial, own_drafts))
    mlp_sum = shared_sum(partial, units)
    tree_out = (first.astype(F32) + rms_scale(mlp_sum, ff_post_gain)).astype(BF)

    low = jnp.where(core == 0, own_drafts, other_drafts)
    high = jnp.where(core == 0, other_drafts, own_drafts)
    rows = units * ACC
    every = jnp.stack(
        [low.reshape(HEADS, Y, rows, -1), high.reshape(HEADS, Y, rows, -1)], axis=2
    ).reshape(HEADS, Y * CORE * rows, -1)

    vocab_width = embedding.shape[0]
    vocab_ids = lax.axis_index(ALL) * vocab_width + jnp.arange(vocab_width, dtype=jnp.int32)
    starts = jnp.repeat(tenant_ranges[:, 0], ACC)
    range_ends = jnp.repeat(tenant_ranges[:, 1], ACC)
    allowed = (vocab_ids[None, :] >= starts[:, None]) & (vocab_ids[None, :] < range_ends[:, None])
    head_logits = []
    head_totals = []
    for head_index in range(HEADS):
        products = lax.dot_general(
            every[head_index], embedding, (((1,), (1,)), ((), ())), preferred_element_type=F32
        )
        logits = SOFTCAP * jnp.tanh(products / SOFTCAP)
        head_logits.append(logits)
        head_totals.append(jnp.sum(jnp.where(allowed, jnp.exp(logits), 0.0), axis=1))
    totals = jnp.stack(head_totals)
    totals = jnp.sum(spread(totals, YC, Y * CORE), axis=0)
    totals = jnp.sum(spread(totals, XZ, units), axis=0)
    draft_logprobs = jnp.stack(
        [
            jnp.where(allowed, head_logits[head_index] - jnp.log(totals[head_index])[:, None], 0.0)
            for head_index in range(HEADS)
        ]
    ).astype(BF)
    return (tree_out, draft_logprobs)


def solution(mesh):
    fine = Mesh(mesh.devices.reshape(Y, CORE, X, Z), ALL)
    return jax.shard_map(
        per_device,
        mesh=fine,
        in_specs=(
            P(ALL, None),
            P(ALL, None),
            P(ALL, None, None),
            P(ALL, None, None, None, None),
            P(ALL),
            P(ALL, None),
            P(ALL, None),
            P(),
            P(None, XZ),
            P(None, None, ALL),
            P(None, None, XZ),
            P(ALL, None),
            P(),
            P(),
            P(),
            P(),
        ),
        out_specs=(P(ALL, None), P(None, None, ALL)),
        check_vma=False,
    )
```

```python
import jax
import jax.numpy as jnp
from jax import lax
from jax.experimental import pallas as pl
from jax.experimental.pallas import tpu as pltpu
from jax.sharding import Mesh, PartitionSpec as P

BF = jnp.bfloat16
F32 = jnp.float32
QH = 8
KVH = 2
HD = 256
HEADS = 4
SOFTCAP = 30.0
Y, CORE, X, Z = 4, 2, 4, 4
EPS = 1e-06
ACC = 4
XZ = ("x", "z")
YC = ("y", "core")
ALL = ("y", "core", "x", "z")
PIECE_PLACES = tuple(
    place
    for kind in range(2)
    for place in (
        (kind, 0, 2 * kind, 2 * kind + 2),
        (kind, 1, 2 * kind, 2 * kind + 2),
        (kind, 3, 2 * kind, 2 * kind + 2),
        (kind, 2, 2 * kind, 2 * kind + 1),
        (kind, 2, 2 * kind + 1, 2 * kind + 2),
    )
)
PIECES = len(PIECE_PLACES)
CONTRACT_LAST = (((1,), (1,)), ((), ()))


def attention_kernel(length_ref, q_ref, kv_ref, parents_ref, keys_ref, values_ref, out_ref, top, bottom, tree):
    rows = q_ref.shape[0]
    group = QH // KVH
    head, block = pl.program_id(0), pl.program_id(1)
    width = keys_ref.shape[0]
    queries = jnp.concatenate([q_ref[:, g * HD : (g + 1) * HD] for g in range(group)], axis=0)
    scale = HD ** (-0.5)

    @pl.when((head == 0) & (block == 0))
    def _():
        lanes = lax.broadcasted_iota(jnp.int32, (rows, rows), 1)
        subs = lax.broadcasted_iota(jnp.int32, (rows, rows), 0)
        reach = jnp.where((parents_ref[...] == lanes) | (subs == lanes), 1.0, 0.0)
        for _ in range(max(1, (rows - 1).bit_length())):
            half = reach.astype(BF)
            reach = jnp.minimum(jnp.dot(half, half, preferred_element_type=F32), 1.0)
        tree[...] = reach

    @pl.when(block == 0)
    def _():
        keys = kv_ref[0]
        scores = lax.dot_general(queries, keys, CONTRACT_LAST, preferred_element_type=F32)
        reach = tree[...]
        weights = jnp.exp(scores * scale) * jnp.concatenate([reach] * group, axis=0)
        bottom[...] = jnp.sum(weights, axis=1, keepdims=True)
        top[...] = jnp.dot(weights.astype(BF), kv_ref[1], preferred_element_type=F32)

    scores = lax.dot_general(queries, keys_ref[...], CONTRACT_LAST, preferred_element_type=F32)
    slots = block * width + lax.broadcasted_iota(jnp.int32, scores.shape, 1)
    weights = jnp.where(slots < length_ref[0], jnp.exp(scores * scale), 0.0)
    bottom[...] += jnp.sum(weights, axis=1, keepdims=True)
    top[...] += jnp.dot(weights.astype(BF), values_ref[...], preferred_element_type=F32)

    @pl.when(block == pl.num_programs(1) - 1)
    def _():
        attended = (top[...] / bottom[...]).astype(BF)
        for g in range(group):
            out_ref[:, g * HD : (g + 1) * HD] = attended[g * rows : (g + 1) * rows]


def attention(tree_q, tree_kv, kv_cache, cache_lengths, tree_parents):
    rows = tree_q.shape[0]
    group = QH // KVH
    slots = kv_cache.shape[3]
    block = min(1024, slots)
    kv = jnp.transpose(tree_kv, (1, 0, 2))
    spec = pl.BlockSpec
    return pl.pallas_call(
        attention_kernel,
        out_shape=jax.ShapeDtypeStruct((rows, QH * HD), BF),
        grid_spec=pltpu.PrefetchScalarGridSpec(
            num_scalar_prefetch=1,
            grid=(KVH, slots // block),
            in_specs=[
                spec((rows, group * HD), lambda k, b, n: (0, k)),
                spec((2, rows, HD), lambda k, b, n: (0, 0, k)),
                spec((rows, 1), lambda k, b, n: (0, 0)),
                spec((None, None, None, block, HD), lambda k, b, n: (0, 0, k, b, 0)),
                spec((None, None, None, block, HD), lambda k, b, n: (0, 1, k, b, 0)),
            ],
            out_specs=spec((rows, group * HD), lambda k, b, n: (0, k)),
            scratch_shapes=[
                pltpu.VMEM((group * rows, HD), F32),
                pltpu.VMEM((group * rows, 1), F32),
                pltpu.VMEM((rows, rows), F32),
            ],
        ),
        compiler_params=pltpu.CompilerParams(
            dimension_semantics=("arbitrary", "arbitrary"), vmem_limit_bytes=24 << 20
        ),
        cost_estimate=pl.CostEstimate(
            flops=4 * rows * QH * HD * slots,
            bytes_accessed=4 * KVH * slots * HD,
            transcendentals=rows * QH * slots,
        ),
    )(cache_lengths, tree_q, kv, tree_parents.reshape(rows, 1), kv_cache, kv_cache)


def logits_kernel(place_ref, *refs):
    pieces = refs[:PIECES]
    bounds_ref, embedding_ref = refs[PIECES : PIECES + 2]
    out_ref, totals_ref, rows_ref, running, sems = refs[-5:]
    step, steps = pl.program_id(0), pl.num_programs(0)
    heads, depth = rows_ref.shape[0], rows_ref.shape[2]
    count = rows_ref.shape[1]
    width = depth // (X * Z)
    x, z, start = place_ref[1], place_ref[2], place_ref[3]
    vocab = embedding_ref.shape[0]

    def copies():
        found = []
        for piece, (kind, d, first, last) in zip(pieces, PIECE_PLACES):
            for e in range(Z):
                dx, dz = (d, e) if kind == 0 else (e, d)
                column = (lax.rem(x + dx, X) * Z + lax.rem(z + dz, Z)) * width
                column = pl.multiple_of(column, width)
                found.append(
                    pltpu.make_async_copy(
                        piece.at[:, :, e * width : (e + 1) * width],
                        rows_ref.at[first:last, :, pl.ds(column, width)],
                        sems.at[len(found)],
                    )
                )
        return found

    @pl.when(step == 0)
    def _():
        started = copies()
        for copy in started:
            copy.start()
        for copy in started:
            copy.wait()
        running[...] = jnp.zeros_like(running)

    ids = start + step * vocab + lax.broadcasted_iota(jnp.int32, (count, vocab), 1)
    allowed = (ids >= bounds_ref[:, 0:1]) & (ids < bounds_ref[:, 1:2])
    for head in range(heads):
        products = lax.dot_general(
            rows_ref[head], embedding_ref[...], CONTRACT_LAST, preferred_element_type=F32
        )
        logits = SOFTCAP * jnp.tanh(products * (1.0 / SOFTCAP))
        out_ref[head] = logits.reshape(out_ref.shape[1:])
        terms = jnp.where(allowed, jnp.exp(logits), 0.0)
        part = terms[:, :128]
        for lane in range(128, vocab, 128):
            part = part + terms[:, lane : lane + 128]
        running[head] += part

    @pl.when(step == steps - 1)
    def _():
        for head in range(heads):
            totals_ref[head : head + 1, :] = jnp.sum(
                jnp.transpose(running[head]), axis=0, keepdims=True
            )


def some_logits(place, pieces, bounds, embedding, table):
    heads = HEADS
    count = pieces[0].shape[1]
    vocab_width, depth = embedding.shape
    vocab = min(256, vocab_width)
    spec = pl.BlockSpec
    out_shape = jax.ShapeDtypeStruct((heads, Y, CORE, count // Y, vocab_width), F32)
    given = [place, *pieces, bounds, embedding]
    aliases = {}
    extra_specs = []
    if table is not None:
        given.append(table)
        aliases = {len(given) - 1: 0}
        extra_specs = [spec(memory_space=pl.ANY)]
    return pl.pallas_call(
        logits_kernel,
        out_shape=(out_shape, jax.ShapeDtypeStruct((heads, count), F32)),
        grid_spec=pltpu.PrefetchScalarGridSpec(
            num_scalar_prefetch=1,
            grid=(vocab_width // vocab,),
            in_specs=[spec(memory_space=pl.ANY)] * len(pieces)
            + [
                spec((count, 2), lambda j, p: (0, 0)),
                spec((vocab, depth), lambda j, p: (j, 0)),
            ]
            + extra_specs,
            out_specs=(
                spec((heads, Y, None, count // Y, vocab), lambda j, p: (0, 0, p[0], 0, j)),
                spec((heads, count), lambda j, p: (0, 0)),
            ),
            scratch_shapes=[
                pltpu.VMEM((heads, count, depth), BF),
                pltpu.VMEM((heads, count, 128), F32),
                pltpu.SemaphoreType.DMA((PIECES * Z,)),
            ],
        ),
        input_output_aliases=aliases,
        compiler_params=pltpu.CompilerParams(
            dimension_semantics=("arbitrary",), vmem_limit_bytes=32 << 20
        ),
        cost_estimate=pl.CostEstimate(
            flops=2 * heads * count * vocab_width * depth,
            bytes_accessed=2 * vocab_width * depth + 4 * heads * count * vocab_width,
            transcendentals=2 * heads * count * vocab_width,
        ),
    )(*given)


def finish_kernel(place_ref, table_ref, logs_ref, bounds_ref, out_ref):
    step = pl.program_id(0)
    heads, count, vocab = table_ref.shape
    ids = place_ref[3] + step * vocab + lax.broadcasted_iota(jnp.int32, (count, vocab), 1)
    allowed = (ids >= bounds_ref[:, 0:1]) & (ids < bounds_ref[:, 1:2])
    for head in range(heads):
        values = table_ref[head] - logs_ref[:, head : head + 1]
        out_ref[head] = jnp.where(allowed, values, 0.0).astype(BF)


def finish(place, table, logs, bounds):
    heads, count, vocab_width = table.shape
    vocab = min(256, vocab_width)
    spec = pl.BlockSpec
    return pl.pallas_call(
        finish_kernel,
        out_shape=jax.ShapeDtypeStruct(table.shape, BF),
        grid_spec=pltpu.PrefetchScalarGridSpec(
            num_scalar_prefetch=1,
            grid=(vocab_width // vocab,),
            in_specs=[
                spec((heads, count, vocab), lambda j, p: (0, 0, j)),
                spec((count, heads), lambda j, p: (0, 0)),
                spec((count, 2), lambda j, p: (0, 0)),
            ],
            out_specs=spec((heads, count, vocab), lambda j, p: (0, 0, j)),
        ),
        compiler_params=pltpu.CompilerParams(
            dimension_semantics=("arbitrary",), vmem_limit_bytes=32 << 20
        ),
        cost_estimate=pl.CostEstimate(
            flops=4 * heads * count * vocab_width,
            bytes_accessed=6 * heads * count * vocab_width,
            transcendentals=0,
        ),
    )(place, table, logs, bounds)


def rms_scale(values, gain):
    floats = values.astype(F32)
    return (
        floats
        * lax.rsqrt(jnp.mean(floats * floats, axis=-1, keepdims=True) + EPS)
        * gain.astype(F32)
    )


def after(values, *earlier):
    return lax.optimization_barrier((values, *earlier))[0]


def ring(values, axis, size, shift):
    return lax.ppermute(values, axis, [((i + shift) % size, i) for i in range(size)])


def spread(values, axes, size):
    copies = lax.optimization_barrier(jnp.broadcast_to(values[None], (size,) + values.shape))
    return lax.all_to_all(copies, axes, split_axis=0, concat_axis=0, tiled=True)


def in_order(blocks, index):
    size = len(blocks)
    ordered = []
    for position in range(size):
        shift = (position - index) % size
        block = blocks[0]
        for candidate in range(1, size):
            block = jnp.where(shift == candidate, blocks[candidate], block)
        ordered.append(block)
    return ordered


def out_weights(out_weight):
    half = out_weight.shape[0] // 2
    own = lax.dynamic_slice_in_dim(out_weight, lax.axis_index("core") * half, half, 0)
    own = jnp.concatenate([own] + [ring(own, "x", X, shift) for shift in range(1, X)], axis=1)
    return own, ring(own, "core", CORE, 1)


def out_projection(attended, own_weight, other_weight):
    rows, depth = attended.shape
    half = depth // 2
    core = lax.axis_index("core")
    group = jnp.concatenate(
        [attended] + [ring(attended, "z", Z, shift) for shift in range(1, Z)], axis=0
    )
    own_part = lax.dynamic_slice_in_dim(group, core * half, half, 1)
    other_part = lax.dynamic_slice_in_dim(group, (1 - core) * half, half, 1)
    columns = (
        jnp.dot(own_part, own_weight, preferred_element_type=F32)
        + jnp.dot(other_part, other_weight, preferred_element_type=F32)
    ).astype(BF)
    width = columns.shape[1] // X
    back = [columns[:rows]]
    for shift in range(1, Z):
        slot = (Z - shift) % Z
        back.append(ring(columns[slot * rows : (slot + 1) * rows], "z", Z, shift))
    by_z = in_order(back, lax.axis_index("z"))
    by_x = in_order(
        [
            jnp.concatenate([b[:, d * width : (d + 1) * width] for b in by_z], axis=1)
            for d in range(X)
        ],
        lax.axis_index("x"),
    )
    return jnp.concatenate(by_x, axis=1)


def unit_terms(mlp_rows, weights):
    gate_part = jnp.dot(mlp_rows, weights[0], preferred_element_type=F32)
    upward = jnp.dot(mlp_rows, weights[1], preferred_element_type=F32)
    active = (jax.nn.gelu(gate_part, approximate=True) * upward).astype(BF)
    return lax.dot_general(
        active, weights[2], (((1,), (1,)), ((), ())), preferred_element_type=F32
    ).astype(BF)


def gather_drafts(drafts):
    pieces = []
    firsts = []
    for kind, near in ((0, "z"), (1, "x")):
        part = drafts[2 * kind : 2 * kind + 2]
        ahead, behind = ring(part, near, X, 1), ring(part, near, X, 3)
        firsts.append((part, ahead, behind))
    joined = []
    for (kind, near), (part, ahead, behind) in zip(((0, "z"), (1, "x")), firsts):
        across = ring(ahead, near, X, 1)
        joined.append(jnp.concatenate([part, ahead, across, behind], axis=2))
    seconds = []
    for far, part in zip(("x", "z"), joined):
        seconds.append((part, ring(part, far, X, 1), ring(part, far, X, 3)))
    for far, (part, ahead, behind) in zip(("x", "z"), seconds):
        pieces += [part, ahead, behind, ring(ahead[:1], far, X, 1), ring(behind[1:], far, X, 3)]
    return pieces


def per_device(
    hidden,
    tree_q,
    tree_kv,
    kv_cache,
    cache_lengths,
    tree_parents,
    accepted,
    tenant_ranges,
    out_weight,
    mlp_weights,
    draft_weights,
    embedding,
    attn_post_gain,
    ff_pre_gain,
    ff_post_gain,
    final_gain,
):
    units = X * Z
    rows = units * ACC
    core = lax.axis_index("core")
    y = lax.axis_index("y")
    unit = lax.axis_index(XZ)
    weights = lax.all_gather(mlp_weights, YC, axis=2, tiled=True)
    chosen = (
        accepted[0][:, None] == jnp.arange(hidden.shape[0], dtype=jnp.int32)[None, :]
    ).astype(BF)

    def pick(values):
        return jnp.dot(chosen, values, preferred_element_type=F32).astype(BF)

    path_hidden = spread(pick(hidden), XZ, units).reshape(rows, -1)
    own_weight, other_weight = out_weights(out_weight)
    attended = attention(tree_q, tree_kv, kv_cache, cache_lengths, tree_parents)

    path_attended = spread(pick(attended), XZ, units).reshape(rows, -1)
    path_columns = jnp.dot(path_attended, out_weight, preferred_element_type=F32).astype(BF)
    path_columns = spread(path_columns, XZ, units)
    path_projected = jnp.transpose(path_columns, (1, 0, 2)).reshape(rows, -1)
    path_first = (path_hidden.astype(F32) + rms_scale(path_projected, attn_post_gain)).astype(BF)
    path_rows = rms_scale(path_first, ff_pre_gain).astype(BF)
    path_terms = unit_terms(path_rows, weights)
    path_terms = lax.all_to_all(
        path_terms.reshape(units, ACC, -1), XZ, split_axis=0, concat_axis=0, tiled=True
    )
    path_sum = jnp.sum(path_terms.astype(F32), axis=0)
    own_first = lax.dynamic_slice_in_dim(path_first, unit * ACC, ACC, 0)
    path = (own_first.astype(F32) + rms_scale(path_sum, ff_post_gain)).astype(BF)
    path_normed = rms_scale(path, final_gain).astype(BF)
    group_path = spread(path_normed, XZ, units).reshape(rows, -1)

    width = draft_weights.shape[2]
    before = jnp.einsum("rd,hde->hre", group_path, draft_weights, preferred_element_type=F32)
    own_columns = lax.dynamic_slice_in_dim(group_path, unit * width, width, 1)
    drafts = (own_columns.astype(F32)[None] + jax.nn.silu(before)).astype(BF)
    drafts = in_order([drafts] + [ring(drafts, "y", Y, shift) for shift in range(1, Y)], y)
    drafts = jnp.concatenate(drafts, axis=1)
    pieces = gather_drafts(drafts)

    projected = out_projection(after(attended, path_attended), own_weight, other_weight)
    first = (hidden.astype(F32) + rms_scale(projected, attn_post_gain)).astype(BF)
    normed = rms_scale(first, ff_pre_gain).astype(BF)
    mlp_rows = lax.all_gather(normed, XZ, axis=0, tiled=True)
    partial = unit_terms(after(mlp_rows, drafts), weights)
    mlp_sum = lax.psum_scatter(partial, XZ, scatter_dimension=0, tiled=True).astype(F32)

    vocab_width = embedding.shape[0]
    start = lax.axis_index(ALL) * vocab_width
    bounds = jnp.repeat(tenant_ranges, ACC, axis=0)
    by_core = bounds.reshape(Y, CORE, rows, 2)

    def place_of(which):
        return jnp.stack([which, lax.axis_index("x"), lax.axis_index("z"), start]).astype(jnp.int32)

    def bounds_of(which):
        return lax.dynamic_index_in_dim(by_core, which, 1, keepdims=False).reshape(Y * rows, 2)

    table, own_totals = some_logits(place_of(core), pieces, bounds_of(core), embedding, None)
    other_pieces = [ring(piece, "core", CORE, 1) for piece in pieces]
    table, other_totals = some_logits(
        place_of(1 - core), other_pieces, bounds_of(1 - core), embedding, table
    )
    sums = jnp.stack(
        [
            jnp.sum(spread(own_totals, XZ, units), axis=0),
            jnp.sum(spread(other_totals, XZ, units), axis=0),
        ]
    )
    sums = sums + ring(sums, "y", Y, 1) + ring(sums, "y", Y, 2) + ring(sums, "y", Y, 3)
    swapped = ring(sums, "core", CORE, 1)
    logs = jnp.log(sums + swapped[::-1])
    logs = jnp.where(core == 0, logs, logs[::-1]).reshape(CORE, HEADS, Y, rows)
    logs = jnp.transpose(logs, (2, 0, 3, 1)).reshape(Y * CORE * rows, HEADS)
    draft_logprobs = finish(
        place_of(core), table.reshape(HEADS, Y * CORE * rows, vocab_width), logs, bounds
    )
    mlp_sum = after(mlp_sum, sums)
    tree_out = (first.astype(F32) + rms_scale(mlp_sum, ff_post_gain)).astype(BF)
    return (tree_out, draft_logprobs)


def solution(mesh):
    fine = Mesh(mesh.devices.reshape(Y, CORE, X, Z), ALL)
    return jax.shard_map(
        per_device,
        mesh=fine,
        in_specs=(
            P(ALL, None),
            P(ALL, None),
            P(ALL, None, None),
            P(ALL, None, None, None, None),
            P(ALL),
            P(ALL, None),
            P(ALL, None),
            P(),
            P(None, XZ),
            P(None, None, ALL),
            P(None, None, XZ),
            P(ALL, None),
            P(),
            P(),
            P(),
            P(),
        ),
        out_specs=(P(ALL, None), P(None, None, ALL)),
        check_vma=False,
    )
```

```python
import jax
import jax.numpy as jnp
from jax import lax
from jax.experimental import pallas as pl
from jax.experimental.pallas import tpu as pltpu
from jax.sharding import Mesh, PartitionSpec as P

BF = jnp.bfloat16
F32 = jnp.float32
QH = 8
KVH = 2
HD = 256
HEADS = 4
SOFTCAP = 30.0
Y, CORE, X, Z = 4, 2, 4, 4
TILE = 256
VOCAB_BLOCK = 512
FINISH_BLOCK = 512
HIDDEN = -1e30
EPS = 1e-06
ACC = 4
XZ = ("x", "z")
YC = ("y", "core")
ALL = ("y", "core", "x", "z")
PIECE_PLACES = tuple((kind, d) for kind in range(2) for d in range(X))
PIECES = len(PIECE_PLACES)
CONTRACT_LAST = (((1,), (1,)), ((), ()))


def attention_kernel(length_ref, q_ref, kv_ref, parents_ref, keys_ref, values_ref, out_ref, top, bottom, tree):
    rows = q_ref.shape[0]
    group = QH // KVH
    head, block = pl.program_id(0), pl.program_id(1)
    width = keys_ref.shape[0]
    queries = jnp.concatenate([q_ref[:, g * HD : (g + 1) * HD] for g in range(group)], axis=0)
    scale = HD ** (-0.5)

    @pl.when((head == 0) & (block == 0))
    def _():
        lanes = lax.broadcasted_iota(jnp.int32, (rows, rows), 1)
        subs = lax.broadcasted_iota(jnp.int32, (rows, rows), 0)
        reach = jnp.where((parents_ref[...] == lanes) | (subs == lanes), 1.0, 0.0)
        for _ in range(max(1, (rows - 1).bit_length())):
            half = reach.astype(BF)
            reach = jnp.minimum(jnp.dot(half, half, preferred_element_type=F32), 1.0)
        tree[...] = reach

    @pl.when(block == 0)
    def _():
        keys = kv_ref[0]
        scores = lax.dot_general(queries, keys, CONTRACT_LAST, preferred_element_type=F32)
        reach = tree[...]
        weights = jnp.exp(scores * scale) * jnp.concatenate([reach] * group, axis=0)
        bottom[...] = jnp.sum(weights, axis=1, keepdims=True)
        top[...] = jnp.dot(weights.astype(BF), kv_ref[1], preferred_element_type=F32)

    scores = lax.dot_general(queries, keys_ref[...], CONTRACT_LAST, preferred_element_type=F32)
    slots = block * width + lax.broadcasted_iota(jnp.int32, scores.shape, 1)
    weights = jnp.where(slots < length_ref[0], jnp.exp(scores * scale), 0.0)
    bottom[...] += jnp.sum(weights, axis=1, keepdims=True)
    top[...] += jnp.dot(weights.astype(BF), values_ref[...], preferred_element_type=F32)

    @pl.when(block == pl.num_programs(1) - 1)
    def _():
        attended = (top[...] / bottom[...]).astype(BF)
        for g in range(group):
            out_ref[:, g * HD : (g + 1) * HD] = attended[g * rows : (g + 1) * rows]


def attention(tree_q, tree_kv, kv_cache, cache_lengths, tree_parents):
    rows = tree_q.shape[0]
    group = QH // KVH
    slots = kv_cache.shape[3]
    block = min(1024, slots)
    kv = jnp.transpose(tree_kv, (1, 0, 2))
    spec = pl.BlockSpec
    return pl.pallas_call(
        attention_kernel,
        out_shape=jax.ShapeDtypeStruct((rows, QH * HD), BF),
        grid_spec=pltpu.PrefetchScalarGridSpec(
            num_scalar_prefetch=1,
            grid=(KVH, slots // block),
            in_specs=[
                spec((rows, group * HD), lambda k, b, n: (0, k)),
                spec((2, rows, HD), lambda k, b, n: (0, 0, k)),
                spec((rows, 1), lambda k, b, n: (0, 0)),
                spec((None, None, None, block, HD), lambda k, b, n: (0, 0, k, b, 0)),
                spec((None, None, None, block, HD), lambda k, b, n: (0, 1, k, b, 0)),
            ],
            out_specs=spec((rows, group * HD), lambda k, b, n: (0, k)),
            scratch_shapes=[
                pltpu.VMEM((group * rows, HD), F32),
                pltpu.VMEM((group * rows, 1), F32),
                pltpu.VMEM((rows, rows), F32),
            ],
        ),
        compiler_params=pltpu.CompilerParams(
            dimension_semantics=("arbitrary", "arbitrary"), vmem_limit_bytes=24 << 20
        ),
        cost_estimate=pl.CostEstimate(
            flops=4 * rows * QH * HD * slots,
            bytes_accessed=4 * KVH * slots * HD,
            transcendentals=rows * QH * slots,
        ),
    )(cache_lengths, tree_q, kv, tree_parents.reshape(rows, 1), kv_cache, kv_cache)


def logits_kernel(place_ref, *refs):
    pieces = refs[:PIECES]
    bounds_ref, embedding_ref = refs[PIECES : PIECES + 2]
    out_ref, totals_ref, rows_ref, running, sems = refs[-5:]
    step, steps = pl.program_id(0), pl.num_programs(0)
    heads, depth = rows_ref.shape[0], rows_ref.shape[2]
    count = rows_ref.shape[1]
    width = depth // (X * Z)
    x, z, start = place_ref[1], place_ref[2], place_ref[3]
    vocab = embedding_ref.shape[0]

    def copies():
        found = []
        for piece, (kind, d) in zip(pieces, PIECE_PLACES):
            target = rows_ref.at[2 * kind : 2 * kind + 2]
            if kind == 0:
                column = pl.multiple_of(lax.rem(x + d, X) * Z * width, width)
                parts = [(piece, target.at[:, :, pl.ds(column, Z * width)])]
            else:
                parts = []
                for e in range(X):
                    column = pl.multiple_of((e * Z + lax.rem(z + d, Z)) * width, width)
                    parts.append(
                        (
                            piece.at[:, :, e * width : (e + 1) * width],
                            target.at[:, :, pl.ds(column, width)],
                        )
                    )
            for source, place in parts:
                found.append(pltpu.make_async_copy(source, place, sems.at[len(found)]))
        return found

    @pl.when(step == 0)
    def _():
        started = copies()
        for copy in started:
            copy.start()
        for copy in started:
            copy.wait()
        running[...] = jnp.zeros_like(running)

    every = rows_ref[...].reshape(heads * count, depth)
    ids = start + step * vocab + lax.broadcasted_iota(jnp.int32, (count, TILE), 1)
    for tile in range(0, vocab, TILE):
        products = lax.dot_general(
            every,
            embedding_ref[tile : tile + TILE],
            CONTRACT_LAST,
            preferred_element_type=F32,
        )
        allowed = (ids >= bounds_ref[:, 0:1] - tile) & (ids < bounds_ref[:, 1:2] - tile)
        for head in range(heads):
            bent = jnp.tanh(products[head * count : (head + 1) * count] * (1.0 / SOFTCAP))
            terms = jnp.where(allowed, jnp.exp(bent * SOFTCAP), 0.0)
            kept = jnp.where(allowed, bent * SOFTCAP, HIDDEN).astype(BF)
            out_ref[head, :, :, tile : tile + TILE] = kept.reshape(out_ref.shape[1:3] + (TILE,))
            part = terms[:, :128]
            for lane in range(128, TILE, 128):
                part = part + terms[:, lane : lane + 128]
            running[head] += part

    @pl.when(step == steps - 1)
    def _():
        for head in range(heads):
            totals_ref[head : head + 1, :] = jnp.sum(
                jnp.transpose(running[head]), axis=0, keepdims=True
            )


def some_logits(place, pieces, bounds, embedding, table):
    heads = HEADS
    count = pieces[0].shape[1]
    vocab_width, depth = embedding.shape
    vocab = min(VOCAB_BLOCK, vocab_width)
    spec = pl.BlockSpec
    out_shape = jax.ShapeDtypeStruct((heads, Y, CORE, count // Y, vocab_width), BF)
    given = [place, *pieces, bounds, embedding]
    aliases = {}
    extra_specs = []
    if table is not None:
        given.append(table)
        aliases = {len(given) - 1: 0}
        extra_specs = [spec(memory_space=pl.ANY)]
    return pl.pallas_call(
        logits_kernel,
        out_shape=(out_shape, jax.ShapeDtypeStruct((heads, count), F32)),
        grid_spec=pltpu.PrefetchScalarGridSpec(
            num_scalar_prefetch=1,
            grid=(vocab_width // vocab,),
            in_specs=[spec(memory_space=pl.ANY)] * len(pieces)
            + [
                spec((count, 2), lambda j, p: (0, 0)),
                spec((vocab, depth), lambda j, p: (j, 0)),
            ]
            + extra_specs,
            out_specs=(
                spec((heads, Y, None, count // Y, vocab), lambda j, p: (0, 0, p[0], 0, j)),
                spec((heads, count), lambda j, p: (0, 0)),
            ),
            scratch_shapes=[
                pltpu.VMEM((heads, count, depth), BF),
                pltpu.VMEM((heads, count, 128), F32),
                pltpu.SemaphoreType.DMA((X + X * Z,)),
            ],
        ),
        input_output_aliases=aliases,
        compiler_params=pltpu.CompilerParams(
            dimension_semantics=("arbitrary",), vmem_limit_bytes=56 << 20
        ),
        cost_estimate=pl.CostEstimate(
            flops=2 * heads * count * vocab_width * depth,
            bytes_accessed=2 * vocab_width * depth + 2 * heads * count * vocab_width,
            transcendentals=2 * heads * count * vocab_width,
        ),
    )(*given)


def finish_kernel(table_ref, logs_ref, out_ref):
    for head in range(table_ref.shape[0]):
        values = table_ref[head].astype(F32)
        shifted = values - logs_ref[:, head : head + 1]
        out_ref[head] = jnp.where(values > 0.5 * HIDDEN, shifted, 0.0).astype(BF)


def finish(table, logs):
    heads, count, vocab_width = table.shape
    vocab = min(FINISH_BLOCK, vocab_width)
    spec = pl.BlockSpec
    return pl.pallas_call(
        finish_kernel,
        out_shape=jax.ShapeDtypeStruct(table.shape, BF),
        grid=(vocab_width // vocab,),
        in_specs=[
            spec((heads, count, vocab), lambda j: (0, 0, j)),
            spec((count, heads), lambda j: (0, 0)),
        ],
        out_specs=spec((heads, count, vocab), lambda j: (0, 0, j)),
        compiler_params=pltpu.CompilerParams(
            dimension_semantics=("arbitrary",), vmem_limit_bytes=56 << 20
        ),
        cost_estimate=pl.CostEstimate(
            flops=3 * heads * count * vocab_width,
            bytes_accessed=4 * heads * count * vocab_width,
            transcendentals=0,
        ),
    )(table, logs)


def rms_scale(values, gain):
    floats = values.astype(F32)
    return (
        floats
        * lax.rsqrt(jnp.mean(floats * floats, axis=-1, keepdims=True) + EPS)
        * gain.astype(F32)
    )


def after(values, *earlier):
    return lax.optimization_barrier((values, earlier))[0]


def ring(values, axis, size, shift):
    return lax.ppermute(values, axis, [((i + shift) % size, i) for i in range(size)])


def copies_of(values, size):
    return lax.optimization_barrier(jnp.broadcast_to(values[None], (size,) + values.shape))


def swap(copies, axes):
    return lax.all_to_all(copies, axes, split_axis=0, concat_axis=0, tiled=True)


def spread(values, axes, size):
    return swap(copies_of(values, size), axes)


def in_order(blocks, index):
    size = len(blocks)
    ordered = []
    for position in range(size):
        shift = (position - index) % size
        block = blocks[0]
        for candidate in range(1, size):
            block = jnp.where(shift == candidate, blocks[candidate], block)
        ordered.append(block)
    return ordered


def own_half_of(out_weight):
    half = out_weight.shape[0] // 2
    return lax.dynamic_slice_in_dim(out_weight, lax.axis_index("core") * half, half, 0)


def out_weights(own):
    own = jnp.concatenate([own] + [ring(own, "x", X, shift) for shift in range(1, X)], axis=1)
    return own, ring(own, "core", CORE, 1)


def gather_group(attended):
    return [attended] + [ring(attended, "z", Z, shift) for shift in range(1, Z)]


def out_projection(group, own_weight, other_weight, earlier):
    rows, depth = group[0].shape
    half = depth // 2
    core = lax.axis_index("core")
    group = jnp.concatenate(group, axis=0)
    own_part = lax.dynamic_slice_in_dim(group, core * half, half, 1)
    other_part = lax.dynamic_slice_in_dim(group, (1 - core) * half, half, 1)
    columns = (
        jnp.dot(own_part, own_weight, preferred_element_type=F32)
        + jnp.dot(other_part, other_weight, preferred_element_type=F32)
    ).astype(BF)
    width = columns.shape[1] // X
    back = [columns[:rows]]
    for shift in range(1, Z):
        slot = (Z - shift) % Z
        back.append(ring(columns[slot * rows : (slot + 1) * rows], "z", Z, shift))
    back = after(back, earlier)
    by_z = in_order(back, lax.axis_index("z"))
    by_x = in_order(
        [
            jnp.concatenate([b[:, d * width : (d + 1) * width] for b in by_z], axis=1)
            for d in range(X)
        ],
        lax.axis_index("x"),
    )
    return jnp.concatenate(by_x, axis=1)


def unit_terms(mlp_rows, weights):
    gate_part = jnp.dot(mlp_rows, weights[0], preferred_element_type=F32)
    upward = jnp.dot(mlp_rows, weights[1], preferred_element_type=F32)
    active = (jax.nn.gelu(gate_part, approximate=True) * upward).astype(BF)
    return lax.dot_general(
        active, weights[2], (((1,), (1,)), ((), ())), preferred_element_type=F32
    ).astype(BF)


def gather_drafts(drafts):
    nears, fars = ("z", "x"), ("x", "z")
    parts = [drafts[:2], drafts[2:]]
    near = [
        [part] + [ring(part, axis, X, shift) for shift in (1, 3, 2)]
        for part, axis in zip(parts, nears)
    ]
    near = lax.optimization_barrier(near)
    joined = [
        jnp.concatenate(in_order([b[0], b[1], b[3], b[2]], lax.axis_index(axis)), axis=2)
        for b, axis in zip(near, nears)
    ]
    joined = lax.optimization_barrier(joined)
    pieces = []
    for part, axis in zip(joined, fars):
        moved = {shift: ring(part, axis, X, shift) for shift in (1, 3, 2)}
        pieces += [part, moved[1], moved[2], moved[3]]
    return pieces


def per_device(
    hidden,
    tree_q,
    tree_kv,
    kv_cache,
    cache_lengths,
    tree_parents,
    accepted,
    tenant_ranges,
    out_weight,
    mlp_weights,
    draft_weights,
    embedding,
    attn_post_gain,
    ff_pre_gain,
    ff_post_gain,
    final_gain,
):
    units = X * Z
    rows = units * ACC
    core = lax.axis_index("core")
    y = lax.axis_index("y")
    unit = lax.axis_index(XZ)
    weights = lax.all_gather(mlp_weights, YC, axis=2, tiled=True)
    chosen = (
        accepted[0][:, None] == jnp.arange(hidden.shape[0], dtype=jnp.int32)[None, :]
    ).astype(BF)

    def pick(values):
        return jnp.dot(chosen, values, preferred_element_type=F32).astype(BF)

    own_half = own_half_of(out_weight)
    own_weight, other_weight = out_weights(own_half)
    attended = attention(after(tree_q, own_half), tree_kv, kv_cache, cache_lengths, tree_parents)

    ahead = copies_of(jnp.concatenate([pick(attended), pick(hidden)], axis=1), units)
    depth = attended.shape[1]
    arrived = swap(ahead, XZ).reshape(rows, -1)
    path_attended, path_hidden = arrived[:, :depth], arrived[:, depth:]
    path_columns = jnp.dot(path_attended, out_weight, preferred_element_type=F32).astype(BF)
    path_copies = copies_of(path_columns, units)
    path_projected = jnp.transpose(swap(path_copies, XZ), (1, 0, 2)).reshape(rows, -1)
    path_first = (path_hidden.astype(F32) + rms_scale(path_projected, attn_post_gain)).astype(BF)
    path_rows = rms_scale(path_first, ff_pre_gain).astype(BF)
    path_partial = unit_terms(path_rows, weights)
    path_terms = lax.all_to_all(
        path_partial.reshape(units, ACC, -1), XZ, split_axis=0, concat_axis=0, tiled=True
    )
    path_sum = jnp.sum(path_terms.astype(F32), axis=0)
    own_first = lax.dynamic_slice_in_dim(path_first, unit * ACC, ACC, 0)
    path = (own_first.astype(F32) + rms_scale(path_sum, ff_post_gain)).astype(BF)
    path_normed = rms_scale(path, final_gain).astype(BF)
    group_path = spread(path_normed, XZ, units).reshape(rows, -1)

    width = draft_weights.shape[2]
    before = jnp.einsum("rd,hde->hre", group_path, draft_weights, preferred_element_type=F32)
    own_columns = lax.dynamic_slice_in_dim(group_path, unit * width, width, 1)
    drafts = (own_columns.astype(F32)[None] + jax.nn.silu(before)).astype(BF)
    drafts = in_order([drafts] + [ring(drafts, "y", Y, shift) for shift in range(1, Y)], y)
    drafts = jnp.concatenate(drafts, axis=1)
    pieces = gather_drafts(drafts)

    group = gather_group(after(attended, ahead))
    projected = out_projection(
        after(group, path_copies), own_weight, other_weight, path_partial
    )
    first = (hidden.astype(F32) + rms_scale(projected, attn_post_gain)).astype(BF)
    normed = rms_scale(first, ff_pre_gain).astype(BF)
    mlp_rows = lax.all_gather(normed, XZ, axis=0, tiled=True)
    other_pieces = [ring(piece, "core", CORE, 1) for piece in pieces]
    mlp_rows = after(mlp_rows, other_pieces[0], other_pieces[X])
    mlp_partial = unit_terms(mlp_rows, weights)
    pieces = after(pieces, mlp_partial)
    mlp_sum = lax.psum_scatter(mlp_partial, XZ, scatter_dimension=0, tiled=True)

    vocab_width = embedding.shape[0]
    start = lax.axis_index(ALL) * vocab_width
    bounds = jnp.repeat(tenant_ranges, ACC, axis=0)
    by_core = bounds.reshape(Y, CORE, rows, 2)

    def place_of(which):
        return jnp.stack([which, lax.axis_index("x"), lax.axis_index("z"), start]).astype(jnp.int32)

    def bounds_of(which):
        return lax.dynamic_index_in_dim(by_core, which, 1, keepdims=False).reshape(Y * rows, 2)

    table, own_totals = some_logits(place_of(core), pieces, bounds_of(core), embedding, None)
    table, other_totals = some_logits(
        place_of(1 - core), other_pieces, bounds_of(1 - core), embedding, table
    )
    sums = jnp.sum(spread(jnp.stack([own_totals, other_totals]), XZ, units), axis=0)
    whole = sums + ring(sums, "y", Y, 1) + ring(sums, "y", Y, 2) + ring(sums, "y", Y, 3)
    swapped = ring(whole, "core", CORE, 1)
    logs = jnp.log(whole + swapped[::-1])
    logs = jnp.where(core == 0, logs, logs[::-1]).reshape(CORE, HEADS, Y, rows)
    logs = jnp.transpose(logs, (2, 0, 3, 1)).reshape(Y * CORE * rows, HEADS)
    draft_logprobs = finish(table.reshape(HEADS, Y * CORE * rows, vocab_width), logs)
    mlp_sum = after(mlp_sum, sums)
    tree_out = (first.astype(F32) + rms_scale(mlp_sum, ff_post_gain)).astype(BF)
    return (tree_out, draft_logprobs)


def solution(mesh):
    fine = Mesh(mesh.devices.reshape(Y, CORE, X, Z), ALL)
    return jax.shard_map(
        per_device,
        mesh=fine,
        in_specs=(
            P(ALL, None),
            P(ALL, None),
            P(ALL, None, None),
            P(ALL, None, None, None, None),
            P(ALL),
            P(ALL, None),
            P(ALL, None),
            P(),
            P(None, XZ),
            P(None, None, ALL),
            P(None, None, XZ),
            P(ALL, None),
            P(),
            P(),
            P(),
            P(),
        ),
        out_specs=(P(ALL, None), P(None, None, ALL)),
        check_vma=False,
    )
```

```python
import functools

import jax
import jax.numpy as jnp
from jax import lax
from jax.experimental import pallas as pl
from jax.experimental.pallas import tpu as pltpu
from jax.sharding import Mesh, PartitionSpec as P

BF = jnp.bfloat16
F32 = jnp.float32
QH = 8
KVH = 2
HD = 256
HEADS = 4
SOFTCAP = 30.0
Y, CORE, X, Z = 4, 2, 4, 4
EPS = 1e-06
ACC = 4
XZ = ("x", "z")
YC = ("y", "core")
ALL = ("y", "core", "x", "z")
GROUPS = ((0, 0), (0, 1), (1, 0), (3, 0), (1, 1), (3, 1), (2, 0), (2, 1))
CALLS = ((0, 2), (2, 6), (6, 8))
TILE = 256
VOCAB_BLOCK = 512
HIDDEN = -1e30
CONTRACT_LAST = (((1,), (1,)), ((), ()))


def attention_kernel(length_ref, q_ref, kv_ref, parents_ref, keys_ref, values_ref, out_ref, top, bottom, tree):
    rows = q_ref.shape[0]
    group = QH // KVH
    head, block = pl.program_id(0), pl.program_id(1)
    width = keys_ref.shape[0]
    queries = jnp.concatenate([q_ref[:, g * HD : (g + 1) * HD] for g in range(group)], axis=0)
    scale = HD ** (-0.5)

    @pl.when((head == 0) & (block == 0))
    def _():
        lanes = lax.broadcasted_iota(jnp.int32, (rows, rows), 1)
        subs = lax.broadcasted_iota(jnp.int32, (rows, rows), 0)
        reach = jnp.where((parents_ref[...] == lanes) | (subs == lanes), 1.0, 0.0)
        for _ in range(max(1, (rows - 1).bit_length())):
            half = reach.astype(BF)
            reach = jnp.minimum(jnp.dot(half, half, preferred_element_type=F32), 1.0)
        tree[...] = reach

    @pl.when(block == 0)
    def _():
        keys = kv_ref[0]
        scores = lax.dot_general(queries, keys, CONTRACT_LAST, preferred_element_type=F32)
        reach = tree[...]
        weights = jnp.exp(scores * scale) * jnp.concatenate([reach] * group, axis=0)
        bottom[...] = jnp.sum(weights, axis=1, keepdims=True)
        top[...] = jnp.dot(weights.astype(BF), kv_ref[1], preferred_element_type=F32)

    scores = lax.dot_general(queries, keys_ref[...], CONTRACT_LAST, preferred_element_type=F32)
    slots = block * width + lax.broadcasted_iota(jnp.int32, scores.shape, 1)
    weights = jnp.where(slots < length_ref[0], jnp.exp(scores * scale), 0.0)
    bottom[...] += jnp.sum(weights, axis=1, keepdims=True)
    top[...] += jnp.dot(weights.astype(BF), values_ref[...], preferred_element_type=F32)

    @pl.when(block == pl.num_programs(1) - 1)
    def _():
        attended = (top[...] / bottom[...]).astype(BF)
        for g in range(group):
            out_ref[:, g * HD : (g + 1) * HD] = attended[g * rows : (g + 1) * rows]


def attention(tree_q, tree_kv, kv_cache, cache_lengths, tree_parents):
    rows = tree_q.shape[0]
    group = QH // KVH
    slots = kv_cache.shape[3]
    block = min(1024, slots)
    kv = jnp.transpose(tree_kv, (1, 0, 2))
    spec = pl.BlockSpec
    return pl.pallas_call(
        attention_kernel,
        out_shape=jax.ShapeDtypeStruct((rows, QH * HD), BF),
        grid_spec=pltpu.PrefetchScalarGridSpec(
            num_scalar_prefetch=1,
            grid=(KVH, slots // block),
            in_specs=[
                spec((rows, group * HD), lambda k, b, n: (0, k)),
                spec((2, rows, HD), lambda k, b, n: (0, 0, k)),
                spec((rows, 1), lambda k, b, n: (0, 0)),
                spec((None, None, None, block, HD), lambda k, b, n: (0, 0, k, b, 0)),
                spec((None, None, None, block, HD), lambda k, b, n: (0, 1, k, b, 0)),
            ],
            out_specs=spec((rows, group * HD), lambda k, b, n: (0, k)),
            scratch_shapes=[
                pltpu.VMEM((group * rows, HD), F32),
                pltpu.VMEM((group * rows, 1), F32),
                pltpu.VMEM((rows, rows), F32),
            ],
        ),
        compiler_params=pltpu.CompilerParams(
            dimension_semantics=("arbitrary", "arbitrary"), vmem_limit_bytes=24 << 20
        ),
        cost_estimate=pl.CostEstimate(
            flops=4 * rows * QH * HD * slots,
            bytes_accessed=4 * KVH * slots * HD,
            transcendentals=rows * QH * slots,
        ),
    )(cache_lengths, tree_q, kv, tree_parents.reshape(rows, 1), kv_cache, kv_cache)


def logits_kernel(first, parts, place_ref, *refs):
    pieces = refs[: len(parts)]
    bounds_ref, embedding_ref, out_ref, totals_ref, rows_ref, running, sems = refs[len(parts) :]
    step, steps = pl.program_id(0), pl.num_programs(0)
    groups, heads, count, depth = rows_ref.shape
    vocab = embedding_ref.shape[0]

    @pl.when(step == 0)
    def _():
        copies = [
            pltpu.make_async_copy(
                piece, rows_ref.at[group, low : low + piece.shape[0]], sems.at[number]
            )
            for number, (piece, (group, low)) in enumerate(zip(pieces, parts))
        ]
        for copy in copies:
            copy.start()
        for copy in copies:
            copy.wait()
        running[...] = jnp.zeros_like(running)

    every = rows_ref[...].reshape(groups * heads * count, depth)
    ids = place_ref[0] + step * vocab + lax.broadcasted_iota(jnp.int32, (count, TILE), 1)
    for tile in range(0, vocab, TILE):
        products = lax.dot_general(
            every,
            embedding_ref[tile : tile + TILE],
            CONTRACT_LAST,
            preferred_element_type=F32,
        )
        for group in range(groups):
            bounds = bounds_ref[place_ref[1 + first + group]] - tile
            allowed = (ids >= bounds[:, 0:1]) & (ids < bounds[:, 1:2])
            for head in range(heads):
                low = (group * heads + head) * count
                bent = jnp.tanh(products[low : low + count] * (1.0 / SOFTCAP))
                terms = jnp.where(allowed, jnp.exp(bent * SOFTCAP), 0.0)
                kept = jnp.where(allowed, bent * SOFTCAP, HIDDEN).astype(BF)
                out_ref[group, head, :, tile : tile + TILE] = kept
                part = terms[:, :128]
                for lane in range(128, TILE, 128):
                    part = part + terms[:, lane : lane + 128]
                running[low : low + count] += part

    @pl.when(step == steps - 1)
    def _():
        size = heads * count
        for group in range(groups):
            totals_ref[group : group + 1, :] = jnp.sum(
                jnp.transpose(running[group * size : (group + 1) * size]), axis=0, keepdims=True
            )


def some_logits(call, place, pieces, parts, bounds, embedding):
    first, last = CALLS[call]
    groups = last - first
    count, depth = pieces[0].shape[1:]
    vocab_width = embedding.shape[0]
    vocab = min(VOCAB_BLOCK, vocab_width)
    size = groups * HEADS * count
    spec = pl.BlockSpec
    return pl.pallas_call(
        functools.partial(logits_kernel, first, parts),
        out_shape=(
            jax.ShapeDtypeStruct((groups, HEADS, count, vocab_width), BF),
            jax.ShapeDtypeStruct((groups, HEADS * count), F32),
        ),
        grid_spec=pltpu.PrefetchScalarGridSpec(
            num_scalar_prefetch=1,
            grid=(vocab_width // vocab,),
            in_specs=[spec(memory_space=pl.ANY)] * len(pieces)
            + [
                spec(bounds.shape, lambda j, p: (0, 0, 0)),
                spec((vocab, depth), lambda j, p: (j, 0)),
            ],
            out_specs=(
                spec((groups, HEADS, count, vocab), lambda j, p: (0, 0, 0, j)),
                spec((groups, HEADS * count), lambda j, p: (0, 0)),
            ),
            scratch_shapes=[
                pltpu.VMEM((groups, HEADS, count, depth), BF),
                pltpu.VMEM((size, 128), F32),
                pltpu.SemaphoreType.DMA((len(pieces),)),
            ],
        ),
        compiler_params=pltpu.CompilerParams(
            dimension_semantics=("arbitrary",), vmem_limit_bytes=56 << 20
        ),
        cost_estimate=pl.CostEstimate(
            flops=2 * size * vocab_width * depth,
            bytes_accessed=2 * vocab_width * depth + 2 * size * vocab_width,
            transcendentals=2 * size * vocab_width,
        ),
    )(place, *pieces, bounds, embedding)


def finish_kernel(place_ref, *refs):
    tables, logs_ref, out_ref = refs[: len(CALLS)], refs[-2], refs[-1]
    step = pl.program_id(0)
    for table_ref, (first, last) in zip(tables, CALLS):

        @pl.when((step >= first) & (step < last))
        def _(table_ref=table_ref):
            for head in range(HEADS):
                values = table_ref[head].astype(F32)
                shifted = values - logs_ref[:, head : head + 1]
                out_ref[head] = jnp.where(values > 0.5 * HIDDEN, shifted, 0.0).astype(BF)


def finish(place, tables, logs):
    count, vocab_width = tables[0].shape[2:]
    groups = len(GROUPS)
    spec = pl.BlockSpec

    def table_spec(first, last):
        return spec(
            (None, HEADS, count, vocab_width),
            lambda k, p: (jnp.clip(k - first, 0, last - first - 1), 0, 0, 0),
        )

    return pl.pallas_call(
        finish_kernel,
        out_shape=jax.ShapeDtypeStruct((HEADS, groups, count, vocab_width), BF),
        grid_spec=pltpu.PrefetchScalarGridSpec(
            num_scalar_prefetch=1,
            grid=(groups,),
            in_specs=[table_spec(*call) for call in CALLS]
            + [spec((None, count, HEADS), lambda k, p: (p[1 + k], 0, 0))],
            out_specs=spec((HEADS, None, count, vocab_width), lambda k, p: (0, p[1 + k], 0, 0)),
        ),
        compiler_params=pltpu.CompilerParams(
            dimension_semantics=("arbitrary",), vmem_limit_bytes=56 << 20
        ),
        cost_estimate=pl.CostEstimate(
            flops=3 * groups * HEADS * count * vocab_width,
            bytes_accessed=4 * groups * HEADS * count * vocab_width,
            transcendentals=0,
        ),
    )(place, *tables, logs)


def rms_scale(values, gain):
    floats = values.astype(F32)
    return (
        floats
        * lax.rsqrt(jnp.mean(floats * floats, axis=-1, keepdims=True) + EPS)
        * gain.astype(F32)
    )


def after(values, *earlier):
    return lax.optimization_barrier((values, earlier))[0]


def ring(values, axis, size, shift):
    return lax.ppermute(values, axis, [((i + shift) % size, i) for i in range(size)])


def copies_of(values, size):
    return lax.optimization_barrier(jnp.broadcast_to(values[None], (size,) + values.shape))


def swap(copies, axes):
    return lax.all_to_all(copies, axes, split_axis=0, concat_axis=0, tiled=True)


def spread(values, axes, size):
    return swap(copies_of(values, size), axes)


def in_order(blocks, index):
    size = len(blocks)
    ordered = []
    for position in range(size):
        shift = (position - index) % size
        block = blocks[0]
        for candidate in range(1, size):
            block = jnp.where(shift == candidate, blocks[candidate], block)
        ordered.append(block)
    return ordered


def own_half_of(out_weight):
    half = out_weight.shape[0] // 2
    return lax.dynamic_slice_in_dim(out_weight, lax.axis_index("core") * half, half, 0)


def out_weights(pieces):
    own = jnp.concatenate(pieces, axis=1)
    return own, ring(own, "core", CORE, 1)


def out_projection(attended, own_weight, other_weight):
    rows, depth = attended.shape
    half = depth // 2
    core = lax.axis_index("core")
    group = lax.all_gather(attended, "z", axis=0, tiled=True)
    own_part = lax.dynamic_slice_in_dim(group, core * half, half, 1)
    other_part = lax.dynamic_slice_in_dim(group, (1 - core) * half, half, 1)
    columns = (
        jnp.dot(own_part, own_weight, preferred_element_type=F32)
        + jnp.dot(other_part, other_weight, preferred_element_type=F32)
    ).astype(BF)
    width = columns.shape[1] // X
    back = swap(columns.reshape(Z, rows, X * width), "z")
    by_x = in_order(
        [
            jnp.concatenate([back[z, :, d * width : (d + 1) * width] for z in range(Z)], axis=1)
            for d in range(X)
        ],
        lax.axis_index("x"),
    )
    return jnp.concatenate(by_x, axis=1)


def unit_terms(mlp_rows, weights):
    gate_part = jnp.dot(mlp_rows, weights[0], preferred_element_type=F32)
    upward = jnp.dot(mlp_rows, weights[1], preferred_element_type=F32)
    active = (jax.nn.gelu(gate_part, approximate=True) * upward).astype(BF)
    return lax.dot_general(
        active, weights[2], (((1,), (1,)), ((), ())), preferred_element_type=F32
    ).astype(BF)


def per_device(
    hidden,
    tree_q,
    tree_kv,
    kv_cache,
    cache_lengths,
    tree_parents,
    accepted,
    tenant_ranges,
    out_weight,
    mlp_weights,
    draft_weights,
    embedding,
    attn_post_gain,
    ff_pre_gain,
    ff_post_gain,
    final_gain,
):
    units = X * Z
    rows = units * ACC
    core = lax.axis_index("core")
    y = lax.axis_index("y")
    unit = lax.axis_index(XZ)
    weights = lax.all_gather(mlp_weights, YC, axis=2, tiled=True)
    chosen = (
        accepted[0][:, None] == jnp.arange(hidden.shape[0], dtype=jnp.int32)[None, :]
    ).astype(BF)

    def pick(values):
        return jnp.dot(chosen, values, preferred_element_type=F32).astype(BF)

    own_half = own_half_of(out_weight)
    pieces = [own_half] + [ring(own_half, "x", X, shift) for shift in range(1, X)]
    attended = attention(after(tree_q, own_half), tree_kv, kv_cache, cache_lengths, tree_parents)
    own_weight, other_weight = out_weights(after(pieces, attended))
    projected = out_projection(attended, own_weight, other_weight)
    first = (hidden.astype(F32) + rms_scale(projected, attn_post_gain)).astype(BF)
    normed = rms_scale(first, ff_pre_gain).astype(BF)
    mlp_rows = lax.all_gather(normed, XZ, axis=0, tiled=True)

    path_rows = spread(pick(normed), XZ, units).reshape(rows, -1)
    path_terms = swap(unit_terms(path_rows, weights).reshape(units, ACC, -1), XZ)
    path_sum = jnp.sum(path_terms.astype(F32), axis=0)
    path = (pick(first).astype(F32) + rms_scale(path_sum, ff_post_gain)).astype(BF)
    path_normed = rms_scale(path, final_gain).astype(BF)
    group_path = spread(path_normed, XZ, units).reshape(rows, -1)

    width = draft_weights.shape[2]
    before = jnp.einsum("rd,hde->hre", group_path, draft_weights, preferred_element_type=F32)
    own_columns = lax.dynamic_slice_in_dim(group_path, unit * width, width, 1)
    drafts = (own_columns.astype(F32)[None] + jax.nn.silu(before)).astype(BF)
    draft_copies = copies_of(drafts, units)
    drafts = jnp.transpose(swap(draft_copies, XZ), (1, 2, 0, 3)).reshape(HEADS, rows, -1)

    mlp_partial = unit_terms(after(mlp_rows, drafts), weights)
    mlp_sum = lax.psum_scatter(mlp_partial, XZ, scatter_dimension=0, tiled=True)

    vocab_width = embedding.shape[0]
    start = lax.axis_index(ALL) * vocab_width
    order = [((y + dy) % Y) * CORE + (core + dc) % CORE for dy, dc in GROUPS]
    place = jnp.stack([start] + order).astype(jnp.int32)
    bounds = jnp.repeat(tenant_ranges, ACC, axis=0).reshape(Y * CORE, rows, 2)
    half = HEADS // 2
    next_up, next_down = ring(drafts, "y", Y, 1), ring(drafts, "y", Y, 3)
    beside = ring(drafts, "core", CORE, 1)
    across = [ring(next_up[:half], "y", Y, 1), ring(next_down[half:], "y", Y, 3)]
    beside_up, beside_down = ring(next_up, "core", CORE, 1), ring(next_down, "core", CORE, 1)
    beside_across = [ring(piece, "core", CORE, 1) for piece in across]
    table_a, totals_a = some_logits(
        0, place, [drafts, beside], ((0, 0), (1, 0)), bounds, embedding
    )
    table_b, totals_b = some_logits(
        1,
        place,
        after([next_up, next_down, beside_up, beside_down], totals_a, mlp_partial),
        ((0, 0), (1, 0), (2, 0), (3, 0)),
        bounds,
        embedding,
    )
    table_c, totals_c = some_logits(
        2,
        place,
        after(across + beside_across, totals_b),
        ((0, 0), (0, half), (1, 0), (1, half)),
        bounds,
        embedding,
    )
    sums = jnp.concatenate([totals_a, totals_b, totals_c], axis=0)
    here = place[1:, None] == jnp.arange(Y * CORE, dtype=jnp.int32)[None, :]
    sums = jnp.sum(jnp.where(here[:, :, None], sums[:, None, :], 0.0), axis=0)
    sums = jnp.sum(spread(sums, XZ, units), axis=0)
    whole = sums + ring(sums, "y", Y, 1) + ring(sums, "y", Y, 2) + ring(sums, "y", Y, 3)
    whole = whole + ring(whole, "core", CORE, 1)
    logs = jnp.transpose(jnp.log(whole).reshape(Y * CORE, HEADS, rows), (0, 2, 1))
    draft_logprobs = finish(place, [table_a, table_b, table_c], logs).reshape(
        HEADS, Y * CORE * rows, vocab_width
    )
    mlp_sum = after(mlp_sum, sums)
    tree_out = (first.astype(F32) + rms_scale(mlp_sum, ff_post_gain)).astype(BF)
    return (tree_out, draft_logprobs)


def solution(mesh):
    fine = Mesh(mesh.devices.reshape(Y, CORE, X, Z), ALL)
    return jax.shard_map(
        per_device,
        mesh=fine,
        in_specs=(
            P(ALL, None),
            P(ALL, None),
            P(ALL, None, None),
            P(ALL, None, None, None, None),
            P(ALL),
            P(ALL, None),
            P(ALL, None),
            P(),
            P(None, XZ),
            P(None, None, ALL),
            P(None, None, XZ),
            P(ALL, None),
            P(),
            P(),
            P(),
            P(),
        ),
        out_specs=(P(ALL, None), P(None, None, ALL)),
        check_vma=False,
    )
```

```python
import functools

import jax
import jax.numpy as jnp
from jax import lax
from jax.experimental import pallas as pl
from jax.experimental.pallas import tpu as pltpu
from jax.sharding import Mesh, PartitionSpec as P

BF = jnp.bfloat16
F32 = jnp.float32
QH = 8
KVH = 2
HD = 256
HEADS = 4
SOFTCAP = 30.0
Y, CORE, X, Z = 4, 2, 4, 4
EPS = 1e-06
ACC = 4
XZ = ("x", "z")
YC = ("y", "core")
ALL = ("y", "core", "x", "z")
GROUPS = ((0, 0), (0, 1), (1, 0), (1, 1), (3, 0), (3, 1), (2, 0), (2, 1))
CALLS = ((0, 2), (2, 6), (6, 8))
TILE = 256
VOCAB_BLOCK = 512
HIDDEN = -1e30
CONTRACT_LAST = (((1,), (1,)), ((), ()))


def attention_kernel(length_ref, q_ref, kv_ref, parents_ref, keys_ref, values_ref, out_ref, top, bottom, tree):
    rows = q_ref.shape[0]
    group = QH // KVH
    head, block = pl.program_id(0), pl.program_id(1)
    width = keys_ref.shape[0]
    queries = jnp.concatenate([q_ref[:, g * HD : (g + 1) * HD] for g in range(group)], axis=0)
    scale = HD ** (-0.5)

    @pl.when((head == 0) & (block == 0))
    def _():
        lanes = lax.broadcasted_iota(jnp.int32, (rows, rows), 1)
        subs = lax.broadcasted_iota(jnp.int32, (rows, rows), 0)
        reach = jnp.where((parents_ref[...] == lanes) | (subs == lanes), 1.0, 0.0)
        for _ in range(max(1, (rows - 1).bit_length())):
            half = reach.astype(BF)
            reach = jnp.minimum(jnp.dot(half, half, preferred_element_type=F32), 1.0)
        tree[...] = reach

    @pl.when(block == 0)
    def _():
        keys = kv_ref[0]
        scores = lax.dot_general(queries, keys, CONTRACT_LAST, preferred_element_type=F32)
        reach = tree[...]
        weights = jnp.exp(scores * scale) * jnp.concatenate([reach] * group, axis=0)
        bottom[...] = jnp.sum(weights, axis=1, keepdims=True)
        top[...] = jnp.dot(weights.astype(BF), kv_ref[1], preferred_element_type=F32)

    scores = lax.dot_general(queries, keys_ref[...], CONTRACT_LAST, preferred_element_type=F32)
    slots = block * width + lax.broadcasted_iota(jnp.int32, scores.shape, 1)
    weights = jnp.where(slots < length_ref[0], jnp.exp(scores * scale), 0.0)
    bottom[...] += jnp.sum(weights, axis=1, keepdims=True)
    top[...] += jnp.dot(weights.astype(BF), values_ref[...], preferred_element_type=F32)

    @pl.when(block == pl.num_programs(1) - 1)
    def _():
        attended = (top[...] / bottom[...]).astype(BF)
        for g in range(group):
            out_ref[:, g * HD : (g + 1) * HD] = attended[g * rows : (g + 1) * rows]


def attention(tree_q, tree_kv, kv_cache, cache_lengths, tree_parents):
    rows = tree_q.shape[0]
    group = QH // KVH
    slots = kv_cache.shape[3]
    block = min(1024, slots)
    kv = jnp.transpose(tree_kv, (1, 0, 2))
    spec = pl.BlockSpec
    return pl.pallas_call(
        attention_kernel,
        out_shape=jax.ShapeDtypeStruct((rows, QH * HD), BF),
        grid_spec=pltpu.PrefetchScalarGridSpec(
            num_scalar_prefetch=1,
            grid=(KVH, slots // block),
            in_specs=[
                spec((rows, group * HD), lambda k, b, n: (0, k)),
                spec((2, rows, HD), lambda k, b, n: (0, 0, k)),
                spec((rows, 1), lambda k, b, n: (0, 0)),
                spec((None, None, None, block, HD), lambda k, b, n: (0, 0, k, b, 0)),
                spec((None, None, None, block, HD), lambda k, b, n: (0, 1, k, b, 0)),
            ],
            out_specs=spec((rows, group * HD), lambda k, b, n: (0, k)),
            scratch_shapes=[
                pltpu.VMEM((group * rows, HD), F32),
                pltpu.VMEM((group * rows, 1), F32),
                pltpu.VMEM((rows, rows), F32),
            ],
        ),
        compiler_params=pltpu.CompilerParams(
            dimension_semantics=("arbitrary", "arbitrary"), vmem_limit_bytes=24 << 20
        ),
        cost_estimate=pl.CostEstimate(
            flops=4 * rows * QH * HD * slots,
            bytes_accessed=4 * KVH * slots * HD,
            transcendentals=rows * QH * slots,
        ),
    )(cache_lengths, tree_q, kv, tree_parents.reshape(rows, 1), kv_cache, kv_cache)


def logits_kernel(first, parts, place_ref, *refs):
    pieces = refs[: len(parts)]
    bounds_ref, embedding_ref, out_ref, totals_ref, rows_ref, running, sems = refs[len(parts) :]
    step, steps = pl.program_id(0), pl.num_programs(0)
    groups, heads, count, depth = rows_ref.shape
    vocab = embedding_ref.shape[0]

    @pl.when(step == 0)
    def _():
        copies = [
            pltpu.make_async_copy(
                piece, rows_ref.at[group, low : low + piece.shape[0]], sems.at[number]
            )
            for number, (piece, (group, low)) in enumerate(zip(pieces, parts))
        ]
        for copy in copies:
            copy.start()
        for copy in copies:
            copy.wait()
        running[...] = jnp.zeros_like(running)

    every = rows_ref[...].reshape(groups * heads * count, depth)
    ids = place_ref[0] + step * vocab + lax.broadcasted_iota(jnp.int32, (count, TILE), 1)
    for tile in range(0, vocab, TILE):
        products = lax.dot_general(
            every,
            embedding_ref[tile : tile + TILE],
            CONTRACT_LAST,
            preferred_element_type=F32,
        )
        for group in range(groups):
            bounds = bounds_ref[place_ref[1 + first + group]] - tile
            allowed = (ids >= bounds[:, 0:1]) & (ids < bounds[:, 1:2])
            for head in range(heads):
                low = (group * heads + head) * count
                bent = jnp.tanh(products[low : low + count] * (1.0 / SOFTCAP))
                terms = jnp.where(allowed, jnp.exp(bent * SOFTCAP), 0.0)
                kept = jnp.where(allowed, bent * SOFTCAP, HIDDEN).astype(BF)
                out_ref[group, head, :, tile : tile + TILE] = kept
                part = terms[:, :128]
                for lane in range(128, TILE, 128):
                    part = part + terms[:, lane : lane + 128]
                running[low : low + count] += part

    @pl.when(step == steps - 1)
    def _():
        size = heads * count
        for group in range(groups):
            totals_ref[group : group + 1, :] = jnp.sum(
                jnp.transpose(running[group * size : (group + 1) * size]), axis=0, keepdims=True
            )


def some_logits(call, place, pieces, parts, bounds, embedding):
    first, last = CALLS[call]
    groups = last - first
    count, depth = pieces[0].shape[1:]
    vocab_width = embedding.shape[0]
    vocab = min(VOCAB_BLOCK, vocab_width)
    size = groups * HEADS * count
    spec = pl.BlockSpec
    return pl.pallas_call(
        functools.partial(logits_kernel, first, parts),
        out_shape=(
            jax.ShapeDtypeStruct((groups, HEADS, count, vocab_width), BF),
            jax.ShapeDtypeStruct((groups, HEADS * count), F32),
        ),
        grid_spec=pltpu.PrefetchScalarGridSpec(
            num_scalar_prefetch=1,
            grid=(vocab_width // vocab,),
            in_specs=[spec(memory_space=pl.ANY)] * len(pieces)
            + [
                spec(bounds.shape, lambda j, p: (0, 0, 0)),
                spec((vocab, depth), lambda j, p: (j, 0)),
            ],
            out_specs=(
                spec((groups, HEADS, count, vocab), lambda j, p: (0, 0, 0, j)),
                spec((groups, HEADS * count), lambda j, p: (0, 0)),
            ),
            scratch_shapes=[
                pltpu.VMEM((groups, HEADS, count, depth), BF),
                pltpu.VMEM((size, 128), F32),
                pltpu.SemaphoreType.DMA((len(pieces),)),
            ],
        ),
        compiler_params=pltpu.CompilerParams(
            dimension_semantics=("arbitrary",), vmem_limit_bytes=56 << 20
        ),
        cost_estimate=pl.CostEstimate(
            flops=2 * size * vocab_width * depth,
            bytes_accessed=2 * vocab_width * depth + 2 * size * vocab_width,
            transcendentals=2 * size * vocab_width,
        ),
    )(place, *pieces, bounds, embedding)


def finish_kernel(place_ref, *refs):
    tables, logs_ref, out_ref = refs[: len(CALLS)], refs[-2], refs[-1]
    step = pl.program_id(0)
    core = lax.rem(place_ref[1], CORE)
    for table_ref, (first, last) in zip(tables, CALLS):

        @pl.when((step >= first // CORE) & (step < last // CORE))
        def _(table_ref=table_ref):
            for position in range(CORE):
                source = lax.rem(position + core, CORE)
                for head in range(HEADS):
                    values = table_ref[source, head].astype(F32)
                    shifted = values - logs_ref[position, :, head : head + 1]
                    out_ref[head, position] = jnp.where(
                        values > 0.5 * HIDDEN, shifted, 0.0
                    ).astype(BF)


def finish(place, tables, logs):
    count, vocab_width = tables[0].shape[2:]
    groups = len(GROUPS)
    spec = pl.BlockSpec

    def table_spec(first, last):
        return spec(
            (CORE, HEADS, count, vocab_width),
            lambda k, p: (jnp.clip(k - first // CORE, 0, (last - first) // CORE - 1), 0, 0, 0),
        )

    def pair(k, p):
        return lax.div(p[1 + CORE * k], CORE)

    return pl.pallas_call(
        finish_kernel,
        out_shape=jax.ShapeDtypeStruct((HEADS, groups, count, vocab_width), BF),
        grid_spec=pltpu.PrefetchScalarGridSpec(
            num_scalar_prefetch=1,
            grid=(groups // CORE,),
            in_specs=[table_spec(*call) for call in CALLS]
            + [spec((CORE, count, HEADS), lambda k, p: (pair(k, p), 0, 0))],
            out_specs=spec(
                (HEADS, CORE, count, vocab_width), lambda k, p: (0, pair(k, p), 0, 0)
            ),
        ),
        compiler_params=pltpu.CompilerParams(
            dimension_semantics=("arbitrary",), vmem_limit_bytes=56 << 20
        ),
        cost_estimate=pl.CostEstimate(
            flops=3 * groups * HEADS * count * vocab_width,
            bytes_accessed=4 * groups * HEADS * count * vocab_width,
            transcendentals=0,
        ),
    )(place, *tables, logs)


def rms_scale(values, gain):
    floats = values.astype(F32)
    return (
        floats
        * lax.rsqrt(jnp.mean(floats * floats, axis=-1, keepdims=True) + EPS)
        * gain.astype(F32)
    )


def after(values, *earlier):
    return lax.optimization_barrier((values, earlier))[0]


def ring(values, axis, size, shift):
    return lax.ppermute(values, axis, [((i + shift) % size, i) for i in range(size)])


def copies_of(values, size):
    return lax.optimization_barrier(jnp.broadcast_to(values[None], (size,) + values.shape))


def swap(copies, axes):
    return lax.all_to_all(copies, axes, split_axis=0, concat_axis=0, tiled=True)


def spread(values, axes, size):
    return swap(copies_of(values, size), axes)


def in_order(blocks, index):
    size = len(blocks)
    ordered = []
    for position in range(size):
        shift = (position - index) % size
        block = blocks[0]
        for candidate in range(1, size):
            block = jnp.where(shift == candidate, blocks[candidate], block)
        ordered.append(block)
    return ordered


def own_half_of(out_weight):
    half = out_weight.shape[0] // 2
    return lax.dynamic_slice_in_dim(out_weight, lax.axis_index("core") * half, half, 0)


def out_weights(pieces):
    own = jnp.concatenate(pieces, axis=1)
    return own, ring(own, "core", CORE, 1)


def out_projection(attended, own_weight, other_weight):
    rows, depth = attended.shape
    half = depth // 2
    core = lax.axis_index("core")
    group = lax.all_gather(attended, "z", axis=0, tiled=True)
    own_part = lax.dynamic_slice_in_dim(group, core * half, half, 1)
    other_part = lax.dynamic_slice_in_dim(group, (1 - core) * half, half, 1)
    columns = (
        jnp.dot(own_part, own_weight, preferred_element_type=F32)
        + jnp.dot(other_part, other_weight, preferred_element_type=F32)
    ).astype(BF)
    width = columns.shape[1] // X
    back = swap(columns.reshape(Z, rows, X * width), "z")
    by_x = in_order(
        [
            jnp.concatenate([back[z, :, d * width : (d + 1) * width] for z in range(Z)], axis=1)
            for d in range(X)
        ],
        lax.axis_index("x"),
    )
    return jnp.concatenate(by_x, axis=1)


def unit_terms(mlp_rows, weights):
    gate_part = jnp.dot(mlp_rows, weights[0], preferred_element_type=F32)
    upward = jnp.dot(mlp_rows, weights[1], preferred_element_type=F32)
    active = (jax.nn.gelu(gate_part, approximate=True) * upward).astype(BF)
    return lax.dot_general(
        active, weights[2], (((1,), (1,)), ((), ())), preferred_element_type=F32
    ).astype(BF)


def per_device(
    hidden,
    tree_q,
    tree_kv,
    kv_cache,
    cache_lengths,
    tree_parents,
    accepted,
    tenant_ranges,
    out_weight,
    mlp_weights,
    draft_weights,
    embedding,
    attn_post_gain,
    ff_pre_gain,
    ff_post_gain,
    final_gain,
):
    units = X * Z
    rows = units * ACC
    core = lax.axis_index("core")
    y = lax.axis_index("y")
    unit = lax.axis_index(XZ)
    weights = lax.all_gather(mlp_weights, YC, axis=2, tiled=True)
    chosen = (
        accepted[0][:, None] == jnp.arange(hidden.shape[0], dtype=jnp.int32)[None, :]
    ).astype(BF)

    def pick(values):
        return jnp.dot(chosen, values, preferred_element_type=F32).astype(BF)

    own_half = own_half_of(out_weight)
    pieces = [own_half] + [ring(own_half, "x", X, shift) for shift in range(1, X)]
    attended = attention(after(tree_q, own_half), tree_kv, kv_cache, cache_lengths, tree_parents)
    own_weight, other_weight = out_weights(after(pieces, attended))
    projected = out_projection(attended, own_weight, other_weight)
    first = (hidden.astype(F32) + rms_scale(projected, attn_post_gain)).astype(BF)
    normed = rms_scale(first, ff_pre_gain).astype(BF)
    mlp_rows = lax.all_gather(normed, XZ, axis=0, tiled=True)

    path_rows = spread(pick(normed), XZ, units).reshape(rows, -1)
    path_terms = swap(unit_terms(path_rows, weights).reshape(units, ACC, -1), XZ)
    path_sum = jnp.sum(path_terms.astype(F32), axis=0)
    path = (pick(first).astype(F32) + rms_scale(path_sum, ff_post_gain)).astype(BF)
    path_normed = rms_scale(path, final_gain).astype(BF)
    group_path = spread(path_normed, XZ, units).reshape(rows, -1)

    width = draft_weights.shape[2]
    before = jnp.einsum("rd,hde->hre", group_path, draft_weights, preferred_element_type=F32)
    own_columns = lax.dynamic_slice_in_dim(group_path, unit * width, width, 1)
    drafts = (own_columns.astype(F32)[None] + jax.nn.silu(before)).astype(BF)
    draft_copies = copies_of(drafts, units)
    drafts = jnp.transpose(swap(draft_copies, XZ), (1, 2, 0, 3)).reshape(HEADS, rows, -1)

    mlp_partial = unit_terms(after(mlp_rows, draft_copies), weights)
    mlp_sum = lax.psum_scatter(after(mlp_partial, drafts), XZ, scatter_dimension=0, tiled=True)

    vocab_width = embedding.shape[0]
    start = lax.axis_index(ALL) * vocab_width
    order = [((y + dy) % Y) * CORE + (core + dc) % CORE for dy, dc in GROUPS]
    place = jnp.stack([start] + order).astype(jnp.int32)
    bounds = jnp.repeat(tenant_ranges, ACC, axis=0).reshape(Y * CORE, rows, 2)
    half = HEADS // 2
    next_up, next_down = ring(drafts, "y", Y, 1), ring(drafts, "y", Y, 3)
    beside = ring(drafts, "core", CORE, 1)
    table_a, totals_a = some_logits(
        0, place, [drafts, beside], ((0, 0), (1, 0)), bounds, embedding
    )
    next_up, next_down = after([next_up, next_down], totals_a)
    across = [ring(next_up[:half], "y", Y, 1), ring(next_down[half:], "y", Y, 3)]
    beside_up, beside_down = ring(next_up, "core", CORE, 1), ring(next_down, "core", CORE, 1)
    table_b, totals_b = some_logits(
        1,
        place,
        [next_up, beside_up, next_down, beside_down],
        ((0, 0), (1, 0), (2, 0), (3, 0)),
        bounds,
        embedding,
    )
    across = after(across, totals_b)
    beside_across = [ring(piece, "core", CORE, 1) for piece in across]
    table_c, totals_c = some_logits(
        2,
        place,
        across + beside_across,
        ((0, 0), (0, half), (1, 0), (1, half)),
        bounds,
        embedding,
    )
    sums = jnp.concatenate([totals_a, totals_b, totals_c], axis=0)
    here = place[1:, None] == jnp.arange(Y * CORE, dtype=jnp.int32)[None, :]
    sums = jnp.sum(jnp.where(here[:, :, None], sums[:, None, :], 0.0), axis=0)
    sums = jnp.sum(spread(sums, XZ, units), axis=0)
    whole = sums + ring(sums, "y", Y, 1) + ring(sums, "y", Y, 2) + ring(sums, "y", Y, 3)
    whole = whole + ring(whole, "core", CORE, 1)
    logs = jnp.transpose(jnp.log(whole).reshape(Y * CORE, HEADS, rows), (0, 2, 1))
    draft_logprobs = finish(place, [table_a, table_b, table_c], logs).reshape(
        HEADS, Y * CORE * rows, vocab_width
    )
    mlp_sum = after(mlp_sum, sums)
    tree_out = (first.astype(F32) + rms_scale(mlp_sum, ff_post_gain)).astype(BF)
    return (tree_out, draft_logprobs)


def solution(mesh):
    fine = Mesh(mesh.devices.reshape(Y, CORE, X, Z), ALL)
    return jax.shard_map(
        per_device,
        mesh=fine,
        in_specs=(
            P(ALL, None),
            P(ALL, None),
            P(ALL, None, None),
            P(ALL, None, None, None, None),
            P(ALL),
            P(ALL, None),
            P(ALL, None),
            P(),
            P(None, XZ),
            P(None, None, ALL),
            P(None, None, XZ),
            P(ALL, None),
            P(),
            P(),
            P(),
            P(),
        ),
        out_specs=(P(ALL, None), P(None, None, ALL)),
        check_vma=False,
    )
```

```python
import functools

import jax
import jax.numpy as jnp
from jax import lax
from jax.experimental import pallas as pl
from jax.experimental.pallas import tpu as pltpu
from jax.sharding import Mesh, PartitionSpec as P

BF = jnp.bfloat16
F32 = jnp.float32
QH = 8
KVH = 2
HD = 256
HEADS = 4
SOFTCAP = 30.0
Y, CORE, X, Z = 4, 2, 4, 4
EPS = 1e-06
ACC = 4
XZ = ("x", "z")
YC = ("y", "core")
ALL = ("y", "core", "x", "z")
GROUPS = ((0, 0), (0, 1), (1, 0), (1, 1), (3, 0), (3, 1), (2, 0), (2, 1))
CALLS = ((0, 2), (2, 6), (6, 8))
TILE = 256
VOCAB_BLOCK = 512
HIDDEN = -1e30
CONTRACT_LAST = (((1,), (1,)), ((), ()))


def attention_kernel(length_ref, q_ref, kv_ref, parents_ref, keys_ref, values_ref, out_ref, top, bottom, tree):
    rows = q_ref.shape[0]
    group = QH // KVH
    head, block = pl.program_id(0), pl.program_id(1)
    width = keys_ref.shape[0]
    queries = jnp.concatenate([q_ref[:, g * HD : (g + 1) * HD] for g in range(group)], axis=0)
    scale = HD ** (-0.5)

    @pl.when((head == 0) & (block == 0))
    def _():
        lanes = lax.broadcasted_iota(jnp.int32, (rows, rows), 1)
        subs = lax.broadcasted_iota(jnp.int32, (rows, rows), 0)
        reach = jnp.where((parents_ref[...] == lanes) | (subs == lanes), 1.0, 0.0)
        for _ in range(max(1, (rows - 1).bit_length())):
            half = reach.astype(BF)
            reach = jnp.minimum(jnp.dot(half, half, preferred_element_type=F32), 1.0)
        tree[...] = reach

    @pl.when(block == 0)
    def _():
        keys = kv_ref[0]
        scores = lax.dot_general(queries, keys, CONTRACT_LAST, preferred_element_type=F32)
        reach = tree[...]
        weights = jnp.exp(scores * scale) * jnp.concatenate([reach] * group, axis=0)
        bottom[...] = jnp.sum(weights, axis=1, keepdims=True)
        top[...] = jnp.dot(weights.astype(BF), kv_ref[1], preferred_element_type=F32)

    scores = lax.dot_general(queries, keys_ref[...], CONTRACT_LAST, preferred_element_type=F32)
    slots = block * width + lax.broadcasted_iota(jnp.int32, scores.shape, 1)
    weights = jnp.where(slots < length_ref[0], jnp.exp(scores * scale), 0.0)
    bottom[...] += jnp.sum(weights, axis=1, keepdims=True)
    top[...] += jnp.dot(weights.astype(BF), values_ref[...], preferred_element_type=F32)

    @pl.when(block == pl.num_programs(1) - 1)
    def _():
        attended = (top[...] / bottom[...]).astype(BF)
        for g in range(group):
            out_ref[:, g * HD : (g + 1) * HD] = attended[g * rows : (g + 1) * rows]


def attention(tree_q, tree_kv, kv_cache, cache_lengths, tree_parents):
    rows = tree_q.shape[0]
    group = QH // KVH
    slots = kv_cache.shape[3]
    block = min(1024, slots)
    kv = jnp.transpose(tree_kv, (1, 0, 2))
    spec = pl.BlockSpec
    return pl.pallas_call(
        attention_kernel,
        out_shape=jax.ShapeDtypeStruct((rows, QH * HD), BF),
        grid_spec=pltpu.PrefetchScalarGridSpec(
            num_scalar_prefetch=1,
            grid=(KVH, slots // block),
            in_specs=[
                spec((rows, group * HD), lambda k, b, n: (0, k)),
                spec((2, rows, HD), lambda k, b, n: (0, 0, k)),
                spec((rows, 1), lambda k, b, n: (0, 0)),
                spec((None, None, None, block, HD), lambda k, b, n: (0, 0, k, b, 0)),
                spec((None, None, None, block, HD), lambda k, b, n: (0, 1, k, b, 0)),
            ],
            out_specs=spec((rows, group * HD), lambda k, b, n: (0, k)),
            scratch_shapes=[
                pltpu.VMEM((group * rows, HD), F32),
                pltpu.VMEM((group * rows, 1), F32),
                pltpu.VMEM((rows, rows), F32),
            ],
        ),
        compiler_params=pltpu.CompilerParams(
            dimension_semantics=("arbitrary", "arbitrary"), vmem_limit_bytes=24 << 20
        ),
        cost_estimate=pl.CostEstimate(
            flops=4 * rows * QH * HD * slots,
            bytes_accessed=4 * KVH * slots * HD,
            transcendentals=rows * QH * slots,
        ),
    )(cache_lengths, tree_q, kv, tree_parents.reshape(rows, 1), kv_cache, kv_cache)


def logits_kernel(first, parts, place_ref, *refs):
    pieces = refs[: len(parts)]
    bounds_ref, embedding_ref, out_ref, totals_ref, rows_ref, running, sems = refs[len(parts) :]
    step, steps = pl.program_id(0), pl.num_programs(0)
    groups, heads, count, depth = rows_ref.shape
    vocab = embedding_ref.shape[0]

    @pl.when(step == 0)
    def _():
        copies = [
            pltpu.make_async_copy(
                piece, rows_ref.at[group, low : low + piece.shape[0]], sems.at[number]
            )
            for number, (piece, (group, low)) in enumerate(zip(pieces, parts))
        ]
        for copy in copies:
            copy.start()
        for copy in copies:
            copy.wait()
        running[...] = jnp.zeros_like(running)

    every = rows_ref[...].reshape(groups * heads * count, depth)
    ids = place_ref[0] + step * vocab + lax.broadcasted_iota(jnp.int32, (count, TILE), 1)
    for tile in range(0, vocab, TILE):
        products = lax.dot_general(
            every,
            embedding_ref[tile : tile + TILE],
            CONTRACT_LAST,
            preferred_element_type=F32,
        )
        for group in range(groups):
            bounds = bounds_ref[place_ref[1 + first + group]] - tile
            allowed = (ids >= bounds[:, 0:1]) & (ids < bounds[:, 1:2])
            for head in range(heads):
                low = (group * heads + head) * count
                bent = jnp.tanh(products[low : low + count] * (1.0 / SOFTCAP))
                terms = jnp.where(allowed, jnp.exp(bent * SOFTCAP), 0.0)
                kept = jnp.where(allowed, bent * SOFTCAP, HIDDEN).astype(BF)
                out_ref[group, head, :, tile : tile + TILE] = kept
                part = terms[:, :128]
                for lane in range(128, TILE, 128):
                    part = part + terms[:, lane : lane + 128]
                running[low : low + count] += part

    @pl.when(step == steps - 1)
    def _():
        size = heads * count
        for group in range(groups):
            totals_ref[group : group + 1, :] = jnp.sum(
                jnp.transpose(running[group * size : (group + 1) * size]), axis=0, keepdims=True
            )


def some_logits(call, place, pieces, parts, bounds, embedding):
    first, last = CALLS[call]
    groups = last - first
    count, depth = pieces[0].shape[1:]
    vocab_width = embedding.shape[0]
    vocab = min(VOCAB_BLOCK, vocab_width)
    size = groups * HEADS * count
    spec = pl.BlockSpec
    return pl.pallas_call(
        functools.partial(logits_kernel, first, parts),
        out_shape=(
            jax.ShapeDtypeStruct((groups, HEADS, count, vocab_width), BF),
            jax.ShapeDtypeStruct((groups, HEADS * count), F32),
        ),
        grid_spec=pltpu.PrefetchScalarGridSpec(
            num_scalar_prefetch=1,
            grid=(vocab_width // vocab,),
            in_specs=[spec(memory_space=pl.ANY)] * len(pieces)
            + [
                spec(bounds.shape, lambda j, p: (0, 0, 0)),
                spec((vocab, depth), lambda j, p: (j, 0)),
            ],
            out_specs=(
                spec((groups, HEADS, count, vocab), lambda j, p: (0, 0, 0, j)),
                spec((groups, HEADS * count), lambda j, p: (0, 0)),
            ),
            scratch_shapes=[
                pltpu.VMEM((groups, HEADS, count, depth), BF),
                pltpu.VMEM((size, 128), F32),
                pltpu.SemaphoreType.DMA((len(pieces),)),
            ],
        ),
        compiler_params=pltpu.CompilerParams(
            dimension_semantics=("arbitrary",), vmem_limit_bytes=56 << 20
        ),
        cost_estimate=pl.CostEstimate(
            flops=2 * size * vocab_width * depth,
            bytes_accessed=2 * vocab_width * depth + 2 * size * vocab_width,
            transcendentals=2 * size * vocab_width,
        ),
    )(place, *pieces, bounds, embedding)


def finish_kernel(place_ref, *refs):
    tables, logs_ref, out_ref = refs[: len(CALLS)], refs[-2], refs[-1]
    step = pl.program_id(0)
    core = lax.rem(place_ref[1], CORE)
    for table_ref, (first, last) in zip(tables, CALLS):

        @pl.when((step >= first // CORE) & (step < last // CORE))
        def _(table_ref=table_ref):
            for position in range(CORE):
                source = lax.rem(position + core, CORE)
                for head in range(HEADS):
                    values = table_ref[source, head].astype(F32)
                    shifted = values - logs_ref[position, :, head : head + 1]
                    out_ref[head, position] = jnp.where(
                        values > 0.5 * HIDDEN, shifted, 0.0
                    ).astype(BF)


def finish(place, tables, logs):
    count, vocab_width = tables[0].shape[2:]
    groups = len(GROUPS)
    spec = pl.BlockSpec

    def table_spec(first, last):
        return spec(
            (CORE, HEADS, count, vocab_width),
            lambda k, p: (jnp.clip(k - first // CORE, 0, (last - first) // CORE - 1), 0, 0, 0),
        )

    def pair(k, p):
        return lax.div(p[1 + CORE * k], CORE)

    return pl.pallas_call(
        finish_kernel,
        out_shape=jax.ShapeDtypeStruct((HEADS, groups, count, vocab_width), BF),
        grid_spec=pltpu.PrefetchScalarGridSpec(
            num_scalar_prefetch=1,
            grid=(groups // CORE,),
            in_specs=[table_spec(*call) for call in CALLS]
            + [spec((CORE, count, HEADS), lambda k, p: (pair(k, p), 0, 0))],
            out_specs=spec(
                (HEADS, CORE, count, vocab_width), lambda k, p: (0, pair(k, p), 0, 0)
            ),
        ),
        compiler_params=pltpu.CompilerParams(
            dimension_semantics=("arbitrary",), vmem_limit_bytes=56 << 20
        ),
        cost_estimate=pl.CostEstimate(
            flops=3 * groups * HEADS * count * vocab_width,
            bytes_accessed=4 * groups * HEADS * count * vocab_width,
            transcendentals=0,
        ),
    )(place, *tables, logs)


def rms_scale(values, gain):
    floats = values.astype(F32)
    return (
        floats
        * lax.rsqrt(jnp.mean(floats * floats, axis=-1, keepdims=True) + EPS)
        * gain.astype(F32)
    )


def after(values, *earlier):
    return lax.optimization_barrier((values, earlier))[0]


def ring(values, axis, size, shift):
    return lax.ppermute(values, axis, [((i + shift) % size, i) for i in range(size)])


def copies_of(values, size):
    return lax.optimization_barrier(jnp.broadcast_to(values[None], (size,) + values.shape))


def swap(copies, axes):
    return lax.all_to_all(copies, axes, split_axis=0, concat_axis=0, tiled=True)


def spread(values, axes, size):
    return swap(copies_of(values, size), axes)


def in_order(blocks, index):
    size = len(blocks)
    ordered = []
    for position in range(size):
        shift = (position - index) % size
        block = blocks[0]
        for candidate in range(1, size):
            block = jnp.where(shift == candidate, blocks[candidate], block)
        ordered.append(block)
    return ordered


def own_half_of(out_weight):
    half = out_weight.shape[0] // 2
    return lax.dynamic_slice_in_dim(out_weight, lax.axis_index("core") * half, half, 0)


def out_weights(pieces):
    own = jnp.concatenate(pieces, axis=1)
    return own, ring(own, "core", CORE, 1)


def along(values, axis, size):
    blocks = [values] + [ring(values, axis, size, shift) for shift in range(1, size)]
    return in_order(blocks, lax.axis_index(axis))


def four_columns(group, own_weight, other_weight):
    half = group.shape[1] // 2
    core = lax.axis_index("core")
    own_part = lax.dynamic_slice_in_dim(group, core * half, half, 1)
    other_part = lax.dynamic_slice_in_dim(group, (1 - core) * half, half, 1)
    return (
        jnp.dot(own_part, own_weight, preferred_element_type=F32)
        + jnp.dot(other_part, other_weight, preferred_element_type=F32)
    ).astype(BF)


def all_columns(by_z):
    width = by_z[0].shape[1] // X
    by_x = in_order(
        [
            jnp.concatenate([b[:, d * width : (d + 1) * width] for b in by_z], axis=1)
            for d in range(X)
        ],
        lax.axis_index("x"),
    )
    return jnp.concatenate(by_x, axis=1)


def unit_terms(mlp_rows, weights):
    gate_part = jnp.dot(mlp_rows, weights[0], preferred_element_type=F32)
    upward = jnp.dot(mlp_rows, weights[1], preferred_element_type=F32)
    active = (jax.nn.gelu(gate_part, approximate=True) * upward).astype(BF)
    return lax.dot_general(
        active, weights[2], (((1,), (1,)), ((), ())), preferred_element_type=F32
    ).astype(BF)


def per_device(
    hidden,
    tree_q,
    tree_kv,
    kv_cache,
    cache_lengths,
    tree_parents,
    accepted,
    tenant_ranges,
    out_weight,
    mlp_weights,
    draft_weights,
    embedding,
    attn_post_gain,
    ff_pre_gain,
    ff_post_gain,
    final_gain,
):
    units = X * Z
    rows = units * ACC
    core = lax.axis_index("core")
    y = lax.axis_index("y")
    unit = lax.axis_index(XZ)
    weights = lax.all_gather(mlp_weights, YC, axis=2, tiled=True)
    chosen = (
        accepted[0][:, None] == jnp.arange(hidden.shape[0], dtype=jnp.int32)[None, :]
    ).astype(BF)

    def pick(values):
        return jnp.dot(chosen, values, preferred_element_type=F32).astype(BF)

    own_half = own_half_of(out_weight)
    pieces = [own_half] + [ring(own_half, "x", X, shift) for shift in range(1, X)]
    own_weight, other_weight = out_weights(pieces)
    attended = attention(
        after(tree_q, own_weight), tree_kv, kv_cache, cache_lengths, tree_parents
    )

    depth = attended.shape[1]
    line = jnp.concatenate(
        along(jnp.concatenate([pick(attended), pick(hidden)], axis=1), "z", Z), axis=0
    )
    line_columns = four_columns(line[:, :depth], own_weight, other_weight)
    line_projected = all_columns(along(line_columns, "z", Z))
    line_first = (
        line[:, depth:].astype(F32) + rms_scale(line_projected, attn_post_gain)
    ).astype(BF)
    line_normed = rms_scale(line_first, ff_pre_gain).astype(BF)
    path_rows = jnp.concatenate(along(line_normed, "x", X), axis=0)
    path_partial = unit_terms(path_rows, weights)
    path_terms = swap(path_partial.reshape(units, ACC, -1), XZ)
    path_sum = jnp.sum(path_terms.astype(F32), axis=0)
    own_first = lax.dynamic_slice_in_dim(line_first, lax.axis_index("z") * ACC, ACC, 0)
    path = (own_first.astype(F32) + rms_scale(path_sum, ff_post_gain)).astype(BF)
    path_normed = rms_scale(path, final_gain).astype(BF)
    group_path = spread(path_normed, XZ, units).reshape(rows, -1)

    width = draft_weights.shape[2]
    before = jnp.einsum("rd,hde->hre", group_path, draft_weights, preferred_element_type=F32)
    own_columns = lax.dynamic_slice_in_dim(group_path, unit * width, width, 1)
    drafts = (own_columns.astype(F32)[None] + jax.nn.silu(before)).astype(BF)
    draft_copies = copies_of(drafts, units)
    drafts = jnp.transpose(swap(draft_copies, XZ), (1, 2, 0, 3)).reshape(HEADS, rows, -1)

    bulk = after(attended, line)
    group = [bulk] + [ring(bulk, "z", Z, shift) for shift in range(1, Z)]
    group = jnp.concatenate(after(group, line_normed), axis=0)
    columns = four_columns(group, own_weight, other_weight)
    size = attended.shape[0]
    back = [columns[:size]]
    for shift in range(1, Z):
        slot = Z - shift
        back.append(ring(columns[slot * size : (slot + 1) * size], "z", Z, shift))
    back = after(back, path_partial)
    projected = all_columns(in_order(back, lax.axis_index("z")))
    first = (hidden.astype(F32) + rms_scale(projected, attn_post_gain)).astype(BF)
    normed = rms_scale(first, ff_pre_gain).astype(BF)
    mlp_rows = lax.all_gather(normed, XZ, axis=0, tiled=True)
    mlp_partial = unit_terms(after(mlp_rows, drafts), weights)

    vocab_width = embedding.shape[0]
    start = lax.axis_index(ALL) * vocab_width
    order = [((y + dy) % Y) * CORE + (core + dc) % CORE for dy, dc in GROUPS]
    place = jnp.stack([start] + order).astype(jnp.int32)
    bounds = jnp.repeat(tenant_ranges, ACC, axis=0).reshape(Y * CORE, rows, 2)
    half = HEADS // 2
    next_up, next_down = ring(drafts, "y", Y, 1), ring(drafts, "y", Y, 3)
    beside = ring(drafts, "core", CORE, 1)
    table_a, totals_a = some_logits(
        0, place, [drafts, beside], ((0, 0), (1, 0)), bounds, embedding
    )
    next_up, next_down = after([next_up, next_down], totals_a, mlp_partial)
    mlp_sum = lax.psum_scatter(
        after(mlp_partial, next_up, next_down), XZ, scatter_dimension=0, tiled=True
    )
    across = [ring(next_up[:half], "y", Y, 1), ring(next_down[half:], "y", Y, 3)]
    beside_up, beside_down = ring(next_up, "core", CORE, 1), ring(next_down, "core", CORE, 1)
    table_b, totals_b = some_logits(
        1,
        place,
        [next_up, beside_up, next_down, beside_down],
        ((0, 0), (1, 0), (2, 0), (3, 0)),
        bounds,
        embedding,
    )
    across = after(across, totals_b)
    beside_across = [ring(piece, "core", CORE, 1) for piece in across]
    table_c, totals_c = some_logits(
        2,
        place,
        across + beside_across,
        ((0, 0), (0, half), (1, 0), (1, half)),
        bounds,
        embedding,
    )
    sums = jnp.concatenate([totals_a, totals_b, totals_c], axis=0)
    here = place[1:, None] == jnp.arange(Y * CORE, dtype=jnp.int32)[None, :]
    sums = jnp.sum(jnp.where(here[:, :, None], sums[:, None, :], 0.0), axis=0)
    sums = jnp.sum(spread(sums, XZ, units), axis=0)
    whole = sums + ring(sums, "y", Y, 1) + ring(sums, "y", Y, 2) + ring(sums, "y", Y, 3)
    whole = whole + ring(whole, "core", CORE, 1)
    logs = jnp.transpose(jnp.log(whole).reshape(Y * CORE, HEADS, rows), (0, 2, 1))
    draft_logprobs = finish(place, [table_a, table_b, table_c], logs).reshape(
        HEADS, Y * CORE * rows, vocab_width
    )
    mlp_sum = after(mlp_sum, sums)
    tree_out = (first.astype(F32) + rms_scale(mlp_sum, ff_post_gain)).astype(BF)
    return (tree_out, draft_logprobs)


def solution(mesh):
    fine = Mesh(mesh.devices.reshape(Y, CORE, X, Z), ALL)
    return jax.shard_map(
        per_device,
        mesh=fine,
        in_specs=(
            P(ALL, None),
            P(ALL, None),
            P(ALL, None, None),
            P(ALL, None, None, None, None),
            P(ALL),
            P(ALL, None),
            P(ALL, None),
            P(),
            P(None, XZ),
            P(None, None, ALL),
            P(None, None, XZ),
            P(ALL, None),
            P(),
            P(),
            P(),
            P(),
        ),
        out_specs=(P(ALL, None), P(None, None, ALL)),
        check_vma=False,
    )
```

```python
import functools

import jax
import jax.numpy as jnp
from jax import lax
from jax.experimental import pallas as pl
from jax.experimental.pallas import tpu as pltpu
from jax.sharding import Mesh, PartitionSpec as P

BF = jnp.bfloat16
F32 = jnp.float32
QH = 8
KVH = 2
HD = 256
HEADS = 4
SOFTCAP = 30.0
Y, CORE, X, Z = 4, 2, 4, 4
EPS = 1e-06
ACC = 4
XZ = ("x", "z")
YC = ("y", "core")
ALL = ("y", "core", "x", "z")
GROUPS = ((0, 0), (0, 1), (1, 0), (3, 0), (1, 1), (3, 1), (2, 0), (2, 1))
CALLS = ((0, 2), (2, 4), (4, 8))
TILE = 256
VOCAB_BLOCK = 512
HIDDEN = -1e30
CONTRACT_LAST = (((1,), (1,)), ((), ()))


def attention_kernel(length_ref, q_ref, kv_ref, parents_ref, keys_ref, values_ref, out_ref, top, bottom, tree):
    rows = q_ref.shape[0]
    group = QH // KVH
    head, block = pl.program_id(0), pl.program_id(1)
    width = keys_ref.shape[0]
    queries = jnp.concatenate([q_ref[:, g * HD : (g + 1) * HD] for g in range(group)], axis=0)
    scale = HD ** (-0.5)

    @pl.when((head == 0) & (block == 0))
    def _():
        lanes = lax.broadcasted_iota(jnp.int32, (rows, rows), 1)
        subs = lax.broadcasted_iota(jnp.int32, (rows, rows), 0)
        reach = jnp.where((parents_ref[...] == lanes) | (subs == lanes), 1.0, 0.0)
        for _ in range(max(1, (rows - 1).bit_length())):
            half = reach.astype(BF)
            reach = jnp.minimum(jnp.dot(half, half, preferred_element_type=F32), 1.0)
        tree[...] = reach

    @pl.when(block == 0)
    def _():
        keys = kv_ref[0]
        scores = lax.dot_general(queries, keys, CONTRACT_LAST, preferred_element_type=F32)
        reach = tree[...]
        weights = jnp.exp(scores * scale) * jnp.concatenate([reach] * group, axis=0)
        bottom[...] = jnp.sum(weights, axis=1, keepdims=True)
        top[...] = jnp.dot(weights.astype(BF), kv_ref[1], preferred_element_type=F32)

    scores = lax.dot_general(queries, keys_ref[...], CONTRACT_LAST, preferred_element_type=F32)
    slots = block * width + lax.broadcasted_iota(jnp.int32, scores.shape, 1)
    weights = jnp.where(slots < length_ref[0], jnp.exp(scores * scale), 0.0)
    bottom[...] += jnp.sum(weights, axis=1, keepdims=True)
    top[...] += jnp.dot(weights.astype(BF), values_ref[...], preferred_element_type=F32)

    @pl.when(block == pl.num_programs(1) - 1)
    def _():
        attended = (top[...] / bottom[...]).astype(BF)
        for g in range(group):
            out_ref[:, g * HD : (g + 1) * HD] = attended[g * rows : (g + 1) * rows]


def attention(tree_q, tree_kv, kv_cache, cache_lengths, tree_parents):
    rows = tree_q.shape[0]
    group = QH // KVH
    slots = kv_cache.shape[3]
    block = min(1024, slots)
    kv = jnp.transpose(tree_kv, (1, 0, 2))
    spec = pl.BlockSpec
    return pl.pallas_call(
        attention_kernel,
        out_shape=jax.ShapeDtypeStruct((rows, QH * HD), BF),
        grid_spec=pltpu.PrefetchScalarGridSpec(
            num_scalar_prefetch=1,
            grid=(KVH, slots // block),
            in_specs=[
                spec((rows, group * HD), lambda k, b, n: (0, k)),
                spec((2, rows, HD), lambda k, b, n: (0, 0, k)),
                spec((rows, 1), lambda k, b, n: (0, 0)),
                spec((None, None, None, block, HD), lambda k, b, n: (0, 0, k, b, 0)),
                spec((None, None, None, block, HD), lambda k, b, n: (0, 1, k, b, 0)),
            ],
            out_specs=spec((rows, group * HD), lambda k, b, n: (0, k)),
            scratch_shapes=[
                pltpu.VMEM((group * rows, HD), F32),
                pltpu.VMEM((group * rows, 1), F32),
                pltpu.VMEM((rows, rows), F32),
            ],
        ),
        compiler_params=pltpu.CompilerParams(
            dimension_semantics=("arbitrary", "arbitrary"), vmem_limit_bytes=60 << 20
        ),
        cost_estimate=pl.CostEstimate(
            flops=4 * rows * QH * HD * slots,
            bytes_accessed=4 * KVH * slots * HD,
            transcendentals=rows * QH * slots,
        ),
    )(cache_lengths, tree_q, kv, tree_parents.reshape(rows, 1), kv_cache, kv_cache)


def logits_kernel(first, parts, place_ref, *refs):
    pieces = refs[: len(parts)]
    bounds_ref, embedding_ref, out_ref, totals_ref, rows_ref, running = refs[len(parts) :]
    step, steps = pl.program_id(0), pl.num_programs(0)
    groups, heads, count, depth = rows_ref.shape
    vocab = embedding_ref.shape[0]

    @pl.when(step == 0)
    def _():
        for piece, (group, low) in zip(pieces, parts):
            rows_ref[group, low : low + piece.shape[0]] = piece[...]
        running[...] = jnp.zeros_like(running)

    every = rows_ref[...].reshape(groups * heads * count, depth)
    ids = place_ref[0] + step * vocab + lax.broadcasted_iota(jnp.int32, (count, TILE), 1)
    for tile in range(0, vocab, TILE):
        products = lax.dot_general(
            every,
            embedding_ref[tile : tile + TILE],
            CONTRACT_LAST,
            preferred_element_type=F32,
        )
        for group in range(groups):
            bounds = bounds_ref[place_ref[1 + first + group]] - tile
            allowed = (ids >= bounds[:, 0:1]) & (ids < bounds[:, 1:2])
            for head in range(heads):
                low = (group * heads + head) * count
                bent = jnp.tanh(products[low : low + count] * (1.0 / SOFTCAP))
                terms = jnp.where(allowed, jnp.exp(bent * SOFTCAP), 0.0)
                kept = jnp.where(allowed, bent * SOFTCAP, HIDDEN).astype(BF)
                out_ref[group, head, :, tile : tile + TILE] = kept
                part = terms[:, :128]
                for lane in range(128, TILE, 128):
                    part = part + terms[:, lane : lane + 128]
                running[low : low + count] += part

    @pl.when(step == steps - 1)
    def _():
        size = heads * count
        for group in range(groups):
            totals_ref[group : group + 1, :] = jnp.sum(
                jnp.transpose(running[group * size : (group + 1) * size]), axis=0, keepdims=True
            )


def some_logits(call, place, pieces, parts, bounds, embedding):
    first, last = CALLS[call]
    groups = last - first
    count, depth = pieces[0].shape[1:]
    vocab_width = embedding.shape[0]
    vocab = min(VOCAB_BLOCK, vocab_width)
    size = groups * HEADS * count
    spec = pl.BlockSpec
    return pl.pallas_call(
        functools.partial(logits_kernel, first, parts),
        out_shape=(
            jax.ShapeDtypeStruct((groups, HEADS, count, vocab_width), BF),
            jax.ShapeDtypeStruct((groups, HEADS * count), F32),
        ),
        grid_spec=pltpu.PrefetchScalarGridSpec(
            num_scalar_prefetch=1,
            grid=(vocab_width // vocab,),
            in_specs=[
                spec(piece.shape, lambda j, p: (0, 0, 0), pipeline_mode=pl.Buffered(1))
                for piece in pieces
            ]
            + [
                spec(bounds.shape, lambda j, p: (0, 0, 0)),
                spec((vocab, depth), lambda j, p: (j, 0)),
            ],
            out_specs=(
                spec((groups, HEADS, count, vocab), lambda j, p: (0, 0, 0, j)),
                spec((groups, HEADS * count), lambda j, p: (0, 0)),
            ),
            scratch_shapes=[
                pltpu.VMEM((groups, HEADS, count, depth), BF),
                pltpu.VMEM((size, 128), F32),
            ],
        ),
        compiler_params=pltpu.CompilerParams(
            dimension_semantics=("arbitrary",), vmem_limit_bytes=56 << 20
        ),
        cost_estimate=pl.CostEstimate(
            flops=2 * size * vocab_width * depth,
            bytes_accessed=2 * vocab_width * depth + 2 * size * vocab_width,
            transcendentals=2 * size * vocab_width,
        ),
    )(place, *pieces, bounds, embedding)


def finish_kernel(place_ref, *refs):
    tables, logs_ref, out_ref = refs[: len(CALLS)], refs[-2], refs[-1]
    step = pl.program_id(0)
    for table_ref, (first, last) in zip(tables, CALLS):

        @pl.when((step >= first) & (step < last))
        def _(table_ref=table_ref):
            for head in range(HEADS):
                values = table_ref[head].astype(F32)
                shifted = values - logs_ref[:, head : head + 1]
                out_ref[head] = jnp.where(values > 0.5 * HIDDEN, shifted, 0.0).astype(BF)


def finish(place, tables, logs):
    count, vocab_width = tables[0].shape[2:]
    groups = len(GROUPS)
    spec = pl.BlockSpec

    def table_spec(first, last):
        return spec(
            (None, HEADS, count, vocab_width),
            lambda k, p: (jnp.clip(k - first, 0, last - first - 1), 0, 0, 0),
        )

    return pl.pallas_call(
        finish_kernel,
        out_shape=jax.ShapeDtypeStruct((HEADS, groups, count, vocab_width), BF),
        grid_spec=pltpu.PrefetchScalarGridSpec(
            num_scalar_prefetch=1,
            grid=(groups,),
            in_specs=[table_spec(*call) for call in CALLS]
            + [spec((None, count, HEADS), lambda k, p: (p[1 + k], 0, 0))],
            out_specs=spec((HEADS, None, count, vocab_width), lambda k, p: (0, p[1 + k], 0, 0)),
        ),
        compiler_params=pltpu.CompilerParams(
            dimension_semantics=("arbitrary",), vmem_limit_bytes=56 << 20
        ),
        cost_estimate=pl.CostEstimate(
            flops=3 * groups * HEADS * count * vocab_width,
            bytes_accessed=4 * groups * HEADS * count * vocab_width,
            transcendentals=0,
        ),
    )(place, *tables, logs)


def rms_scale(values, gain):
    floats = values.astype(F32)
    return (
        floats
        * lax.rsqrt(jnp.mean(floats * floats, axis=-1, keepdims=True) + EPS)
        * gain.astype(F32)
    )


def after(values, *earlier):
    return lax.optimization_barrier((values, earlier))[0]


def ring(values, axis, size, shift):
    return lax.ppermute(values, axis, [((i + shift) % size, i) for i in range(size)])


def copies_of(values, size):
    return lax.optimization_barrier(jnp.broadcast_to(values[None], (size,) + values.shape))


def swap(copies, axes):
    return lax.all_to_all(copies, axes, split_axis=0, concat_axis=0, tiled=True)


def spread(values, axes, size):
    return swap(copies_of(values, size), axes)


def in_order(blocks, index):
    size = len(blocks)
    ordered = []
    for position in range(size):
        shift = (position - index) % size
        block = blocks[0]
        for candidate in range(1, size):
            block = jnp.where(shift == candidate, blocks[candidate], block)
        ordered.append(block)
    return ordered


def own_half_of(out_weight):
    half = out_weight.shape[0] // 2
    return lax.dynamic_slice_in_dim(out_weight, lax.axis_index("core") * half, half, 0)


def out_weights(pieces):
    own = jnp.concatenate(pieces, axis=1)
    return own, ring(own, "core", CORE, 1)


def out_projection(group, own_weight, other_weight):
    rows, depth = group[0].shape
    half = depth // 2
    core = lax.axis_index("core")
    group = jnp.concatenate(group, axis=0)
    own_part = lax.dynamic_slice_in_dim(group, core * half, half, 1)
    other_part = lax.dynamic_slice_in_dim(group, (1 - core) * half, half, 1)
    columns = (
        jnp.dot(own_part, own_weight, preferred_element_type=F32)
        + jnp.dot(other_part, other_weight, preferred_element_type=F32)
    ).astype(BF)
    width = columns.shape[1] // X
    columns = [columns[z * rows : (z + 1) * rows] for z in range(Z)]
    columns = jnp.stack(in_order(columns, lax.axis_index("z")))
    back = swap(columns, "z")
    by_x = in_order(
        [
            jnp.concatenate([back[z, :, d * width : (d + 1) * width] for z in range(Z)], axis=1)
            for d in range(X)
        ],
        lax.axis_index("x"),
    )
    return jnp.concatenate(by_x, axis=1)


def unit_terms(mlp_rows, weights):
    gate_part = jnp.dot(mlp_rows, weights[0], preferred_element_type=F32)
    upward = jnp.dot(mlp_rows, weights[1], preferred_element_type=F32)
    active = (jax.nn.gelu(gate_part, approximate=True) * upward).astype(BF)
    return lax.dot_general(
        active, weights[2], (((1,), (1,)), ((), ())), preferred_element_type=F32
    ).astype(BF)


def per_device(
    hidden,
    tree_q,
    tree_kv,
    kv_cache,
    cache_lengths,
    tree_parents,
    accepted,
    tenant_ranges,
    out_weight,
    mlp_weights,
    draft_weights,
    embedding,
    attn_post_gain,
    ff_pre_gain,
    ff_post_gain,
    final_gain,
):
    units = X * Z
    rows = units * ACC
    core = lax.axis_index("core")
    y = lax.axis_index("y")
    unit = lax.axis_index(XZ)
    weights = lax.all_gather(mlp_weights, YC, axis=2, tiled=True)
    chosen = (
        accepted[0][:, None] == jnp.arange(hidden.shape[0], dtype=jnp.int32)[None, :]
    ).astype(BF)

    def pick(values):
        return jnp.dot(chosen, values, preferred_element_type=F32).astype(BF)

    own_half = own_half_of(out_weight)
    pieces = [own_half] + [ring(own_half, "x", X, shift) for shift in range(1, X)]
    attended = attention(after(tree_q, own_half), tree_kv, kv_cache, cache_lengths, tree_parents)
    pieces = after(pieces, attended)
    sent = after(attended, pieces)
    group = [sent] + [ring(sent, "z", Z, shift) for shift in range(1, Z)]
    own_weight, other_weight = out_weights(pieces)
    projected = out_projection(after(group, other_weight), own_weight, other_weight)
    first = (hidden.astype(F32) + rms_scale(projected, attn_post_gain)).astype(BF)
    normed = rms_scale(first, ff_pre_gain).astype(BF)
    mlp_rows = lax.all_gather(normed, XZ, axis=0, tiled=True)

    path_rows = spread(pick(normed), XZ, units).reshape(rows, -1)
    path_terms = swap(unit_terms(path_rows, weights).reshape(units, ACC, -1), XZ)
    path_sum = jnp.sum(path_terms.astype(F32), axis=0)
    path = (pick(first).astype(F32) + rms_scale(path_sum, ff_post_gain)).astype(BF)
    path_normed = rms_scale(path, final_gain).astype(BF)
    group_path = spread(path_normed, XZ, units).reshape(rows, -1)

    width = draft_weights.shape[2]
    before = jnp.einsum("rd,hde->hre", group_path, draft_weights, preferred_element_type=F32)
    own_columns = lax.dynamic_slice_in_dim(group_path, unit * width, width, 1)
    drafts = (own_columns.astype(F32)[None] + jax.nn.silu(before)).astype(BF)
    draft_copies = copies_of(drafts, units)
    drafts = jnp.transpose(swap(draft_copies, XZ), (1, 2, 0, 3)).reshape(HEADS, rows, -1)

    mlp_partial = unit_terms(after(mlp_rows, draft_copies), weights)
    mlp_sum = lax.psum_scatter(after(mlp_partial, drafts), XZ, scatter_dimension=0, tiled=True)

    vocab_width = embedding.shape[0]
    start = lax.axis_index(ALL) * vocab_width
    order = [((y + dy) % Y) * CORE + (core + dc) % CORE for dy, dc in GROUPS]
    place = jnp.stack([start] + order).astype(jnp.int32)
    bounds = jnp.repeat(tenant_ranges, ACC, axis=0).reshape(Y * CORE, rows, 2)
    half = HEADS // 2
    next_up, next_down = ring(drafts, "y", Y, 1), ring(drafts, "y", Y, 3)
    beside = ring(drafts, "core", CORE, 1)
    table_a, totals_a = some_logits(
        0, place, [drafts, beside], ((0, 0), (1, 0)), bounds, embedding
    )
    next_up, next_down = after([next_up, next_down], totals_a)
    across = [ring(next_up[:half], "y", Y, 1), ring(next_down[half:], "y", Y, 3)]
    beside_up, beside_down = ring(next_up, "core", CORE, 1), ring(next_down, "core", CORE, 1)
    table_b, totals_b = some_logits(
        1, place, [next_up, next_down], ((0, 0), (1, 0)), bounds, embedding
    )
    beside_up, beside_down, *across = after([beside_up, beside_down, *across], totals_b)
    beside_across = [ring(piece, "core", CORE, 1) for piece in across]
    table_c, totals_c = some_logits(
        2,
        place,
        [beside_up, beside_down, *across, *beside_across],
        ((0, 0), (1, 0), (2, 0), (2, half), (3, 0), (3, half)),
        bounds,
        embedding,
    )
    sums = jnp.concatenate([totals_a, totals_b, totals_c], axis=0)
    here = place[1:, None] == jnp.arange(Y * CORE, dtype=jnp.int32)[None, :]
    sums = jnp.sum(jnp.where(here[:, :, None], sums[:, None, :], 0.0), axis=0)
    sums = jnp.sum(spread(sums, XZ, units), axis=0)
    whole = sums + ring(sums, "y", Y, 1) + ring(sums, "y", Y, 2) + ring(sums, "y", Y, 3)
    whole = whole + ring(whole, "core", CORE, 1)
    logs = jnp.transpose(jnp.log(whole).reshape(Y * CORE, HEADS, rows), (0, 2, 1))
    mlp_sum = after(mlp_sum, sums)
    tree_out = (first.astype(F32) + rms_scale(mlp_sum, ff_post_gain)).astype(BF)
    draft_logprobs = finish(place, [table_a, table_b, table_c], after(logs, tree_out)).reshape(
        HEADS, Y * CORE * rows, vocab_width
    )
    return (tree_out, draft_logprobs)


def solution(mesh):
    fine = Mesh(mesh.devices.reshape(Y, CORE, X, Z), ALL)
    return jax.shard_map(
        per_device,
        mesh=fine,
        in_specs=(
            P(ALL, None),
            P(ALL, None),
            P(ALL, None, None),
            P(ALL, None, None, None, None),
            P(ALL),
            P(ALL, None),
            P(ALL, None),
            P(),
            P(None, XZ),
            P(None, None, ALL),
            P(None, None, XZ),
            P(ALL, None),
            P(),
            P(),
            P(),
            P(),
        ),
        out_specs=(P(ALL, None), P(None, None, ALL)),
        check_vma=False,
    )
```

```python
import functools

import jax
import jax.numpy as jnp
from jax import lax
from jax.experimental import pallas as pl
from jax.experimental.pallas import tpu as pltpu
from jax.sharding import Mesh, PartitionSpec as P

BF = jnp.bfloat16
F32 = jnp.float32
QH = 8
KVH = 2
HD = 256
HEADS = 4
SOFTCAP = 30.0
Y, CORE, X, Z = 4, 2, 4, 4
EPS = 1e-06
ACC = 4
XZ = ("x", "z")
YC = ("y", "core")
ALL = ("y", "core", "x", "z")
GROUPS = ((0, 0), (0, 1), (1, 0), (1, 1), (3, 0), (3, 1), (2, 0), (2, 1))
CALLS = ((0, 2), (2, 6), (6, 8))
TILE = 256
VOCAB_BLOCK = 512
HIDDEN = -1e30
CONTRACT_LAST = (((1,), (1,)), ((), ()))


def attention_kernel(length_ref, q_ref, kv_ref, parents_ref, keys_ref, values_ref, out_ref, top, bottom, tree):
    rows = q_ref.shape[0]
    group = QH // KVH
    head, block = pl.program_id(0), pl.program_id(1)
    width = keys_ref.shape[0]
    queries = jnp.concatenate([q_ref[:, g * HD : (g + 1) * HD] for g in range(group)], axis=0)
    scale = HD ** (-0.5)

    @pl.when((head == 0) & (block == 0))
    def _():
        lanes = lax.broadcasted_iota(jnp.int32, (rows, rows), 1)
        subs = lax.broadcasted_iota(jnp.int32, (rows, rows), 0)
        reach = jnp.where((parents_ref[...] == lanes) | (subs == lanes), 1.0, 0.0)
        for _ in range(max(1, (rows - 1).bit_length())):
            half = reach.astype(BF)
            reach = jnp.minimum(jnp.dot(half, half, preferred_element_type=F32), 1.0)
        tree[...] = reach

    @pl.when(block == 0)
    def _():
        keys = kv_ref[0]
        scores = lax.dot_general(queries, keys, CONTRACT_LAST, preferred_element_type=F32)
        reach = tree[...]
        weights = jnp.exp(scores * scale) * jnp.concatenate([reach] * group, axis=0)
        bottom[...] = jnp.sum(weights, axis=1, keepdims=True)
        top[...] = jnp.dot(weights.astype(BF), kv_ref[1], preferred_element_type=F32)

    scores = lax.dot_general(queries, keys_ref[...], CONTRACT_LAST, preferred_element_type=F32)
    slots = block * width + lax.broadcasted_iota(jnp.int32, scores.shape, 1)
    weights = jnp.where(slots < length_ref[0], jnp.exp(scores * scale), 0.0)
    bottom[...] += jnp.sum(weights, axis=1, keepdims=True)
    top[...] += jnp.dot(weights.astype(BF), values_ref[...], preferred_element_type=F32)

    @pl.when(block == pl.num_programs(1) - 1)
    def _():
        attended = (top[...] / bottom[...]).astype(BF)
        for g in range(group):
            out_ref[:, g * HD : (g + 1) * HD] = attended[g * rows : (g + 1) * rows]


def attention(tree_q, tree_kv, kv_cache, cache_lengths, tree_parents):
    rows = tree_q.shape[0]
    group = QH // KVH
    slots = kv_cache.shape[3]
    block = min(1024, slots)
    kv = jnp.transpose(tree_kv, (1, 0, 2))
    spec = pl.BlockSpec
    return pl.pallas_call(
        attention_kernel,
        out_shape=jax.ShapeDtypeStruct((rows, QH * HD), BF),
        grid_spec=pltpu.PrefetchScalarGridSpec(
            num_scalar_prefetch=1,
            grid=(KVH, slots // block),
            in_specs=[
                spec((rows, group * HD), lambda k, b, n: (0, k)),
                spec((2, rows, HD), lambda k, b, n: (0, 0, k)),
                spec((rows, 1), lambda k, b, n: (0, 0)),
                spec((None, None, None, block, HD), lambda k, b, n: (0, 0, k, b, 0)),
                spec((None, None, None, block, HD), lambda k, b, n: (0, 1, k, b, 0)),
            ],
            out_specs=spec((rows, group * HD), lambda k, b, n: (0, k)),
            scratch_shapes=[
                pltpu.VMEM((group * rows, HD), F32),
                pltpu.VMEM((group * rows, 1), F32),
                pltpu.VMEM((rows, rows), F32),
            ],
        ),
        compiler_params=pltpu.CompilerParams(
            dimension_semantics=("arbitrary", "arbitrary"), vmem_limit_bytes=24 << 20
        ),
        cost_estimate=pl.CostEstimate(
            flops=4 * rows * QH * HD * slots,
            bytes_accessed=4 * KVH * slots * HD,
            transcendentals=rows * QH * slots,
        ),
    )(cache_lengths, tree_q, kv, tree_parents.reshape(rows, 1), kv_cache, kv_cache)


def logits_kernel(first, parts, place_ref, *refs):
    pieces = refs[: len(parts)]
    bounds_ref, embedding_ref, out_ref, totals_ref, rows_ref, running = refs[len(parts) :]
    step, steps = pl.program_id(0), pl.num_programs(0)
    groups, heads, count, depth = rows_ref.shape
    vocab = embedding_ref.shape[0]

    @pl.when(step == 0)
    def _():
        for piece, (group, low) in zip(pieces, parts):
            rows_ref[group, low : low + piece.shape[0]] = piece[...]
        running[...] = jnp.zeros_like(running)

    every = rows_ref[...].reshape(groups * heads * count, depth)
    ids = place_ref[0] + step * vocab + lax.broadcasted_iota(jnp.int32, (count, TILE), 1)
    for tile in range(0, vocab, TILE):
        products = lax.dot_general(
            every,
            embedding_ref[tile : tile + TILE],
            CONTRACT_LAST,
            preferred_element_type=F32,
        )
        for group in range(groups):
            bounds = bounds_ref[place_ref[1 + first + group]] - tile
            allowed = (ids >= bounds[:, 0:1]) & (ids < bounds[:, 1:2])
            for head in range(heads):
                low = (group * heads + head) * count
                bent = jnp.tanh(products[low : low + count] * (1.0 / SOFTCAP))
                terms = jnp.where(allowed, jnp.exp(bent * SOFTCAP), 0.0)
                kept = jnp.where(allowed, bent * SOFTCAP, HIDDEN).astype(BF)
                out_ref[group, head, :, tile : tile + TILE] = kept
                part = terms[:, :128]
                for lane in range(128, TILE, 128):
                    part = part + terms[:, lane : lane + 128]
                running[low : low + count] += part

    @pl.when(step == steps - 1)
    def _():
        size = heads * count
        for group in range(groups):
            totals_ref[group : group + 1, :] = jnp.sum(
                jnp.transpose(running[group * size : (group + 1) * size]), axis=0, keepdims=True
            )


def some_logits(first, shape, place, pieces, parts, bounds, embedding):
    groups, heads = shape
    count, depth = pieces[0].shape[1:]
    vocab_width = embedding.shape[0]
    vocab = min(VOCAB_BLOCK, vocab_width)
    size = groups * heads * count
    spec = pl.BlockSpec
    return pl.pallas_call(
        functools.partial(logits_kernel, first, parts),
        out_shape=(
            jax.ShapeDtypeStruct((groups, heads, count, vocab_width), BF),
            jax.ShapeDtypeStruct((groups, heads * count), F32),
        ),
        grid_spec=pltpu.PrefetchScalarGridSpec(
            num_scalar_prefetch=1,
            grid=(vocab_width // vocab,),
            in_specs=[
                spec(piece.shape, lambda j, p: (0, 0, 0), pipeline_mode=pl.Buffered(1))
                for piece in pieces
            ]
            + [
                spec(bounds.shape, lambda j, p: (0, 0, 0)),
                spec((vocab, depth), lambda j, p: (j, 0)),
            ],
            out_specs=(
                spec((groups, heads, count, vocab), lambda j, p: (0, 0, 0, j)),
                spec((groups, heads * count), lambda j, p: (0, 0)),
            ),
            scratch_shapes=[
                pltpu.VMEM((groups, heads, count, depth), BF),
                pltpu.VMEM((size, 128), F32),
            ],
        ),
        compiler_params=pltpu.CompilerParams(
            dimension_semantics=("arbitrary",), vmem_limit_bytes=56 << 20
        ),
        cost_estimate=pl.CostEstimate(
            flops=2 * size * vocab_width * depth,
            bytes_accessed=2 * vocab_width * depth + 2 * size * vocab_width,
            transcendentals=2 * size * vocab_width,
        ),
    )(place, *pieces, bounds, embedding)


def finish_kernel(place_ref, *refs):
    logs_ref, out_ref = refs[-2:]
    tables = ((refs[0],), refs[1:3], (refs[3],))
    step = pl.program_id(0)
    core = lax.rem(place_ref[1], CORE)
    for shared, (first, last) in zip(tables, CALLS):

        @pl.when((step >= first // CORE) & (step < last // CORE))
        def _(shared=shared):
            heads = HEADS // len(shared)
            for position in range(CORE):
                source = lax.rem(position + core, CORE)
                for head in range(HEADS):
                    values = shared[head // heads][source, head % heads].astype(F32)
                    shifted = values - logs_ref[position, :, head : head + 1]
                    out_ref[head, position] = jnp.where(
                        values > 0.5 * HIDDEN, shifted, 0.0
                    ).astype(BF)


def finish(place, tables, logs):
    count, vocab_width = tables[0].shape[2:]
    groups = len(GROUPS)
    spec = pl.BlockSpec

    def table_spec(table, first, last):
        return spec(
            (CORE, table.shape[1], count, vocab_width),
            lambda k, p: (jnp.clip(k - first // CORE, 0, (last - first) // CORE - 1), 0, 0, 0),
        )

    def pair(k, p):
        return lax.div(p[1 + CORE * k], CORE)

    calls = (CALLS[0], CALLS[1], CALLS[1], CALLS[2])
    return pl.pallas_call(
        finish_kernel,
        out_shape=jax.ShapeDtypeStruct((HEADS, groups, count, vocab_width), BF),
        grid_spec=pltpu.PrefetchScalarGridSpec(
            num_scalar_prefetch=1,
            grid=(groups // CORE,),
            in_specs=[table_spec(table, *call) for table, call in zip(tables, calls)]
            + [spec((CORE, count, HEADS), lambda k, p: (pair(k, p), 0, 0))],
            out_specs=spec(
                (HEADS, CORE, count, vocab_width), lambda k, p: (0, pair(k, p), 0, 0)
            ),
        ),
        compiler_params=pltpu.CompilerParams(
            dimension_semantics=("arbitrary",), vmem_limit_bytes=56 << 20
        ),
        cost_estimate=pl.CostEstimate(
            flops=3 * groups * HEADS * count * vocab_width,
            bytes_accessed=4 * groups * HEADS * count * vocab_width,
            transcendentals=0,
        ),
    )(place, *tables, logs)


def rms_scale(values, gain):
    floats = values.astype(F32)
    return (
        floats
        * lax.rsqrt(jnp.mean(floats * floats, axis=-1, keepdims=True) + EPS)
        * gain.astype(F32)
    )


def after(values, *earlier):
    return lax.optimization_barrier((values, earlier))[0]


def ring(values, axis, size, shift):
    return lax.ppermute(values, axis, [((i + shift) % size, i) for i in range(size)])


def copies_of(values, size):
    return lax.optimization_barrier(jnp.broadcast_to(values[None], (size,) + values.shape))


def swap(copies, axes):
    return lax.all_to_all(copies, axes, split_axis=0, concat_axis=0, tiled=True)


def spread(values, axes, size):
    return swap(copies_of(values, size), axes)


def in_order(blocks, index):
    size = len(blocks)
    ordered = []
    for position in range(size):
        shift = (position - index) % size
        block = blocks[0]
        for candidate in range(1, size):
            block = jnp.where(shift == candidate, blocks[candidate], block)
        ordered.append(block)
    return ordered


def own_half_of(out_weight):
    half = out_weight.shape[0] // 2
    return lax.dynamic_slice_in_dim(out_weight, lax.axis_index("core") * half, half, 0)


def out_weights(pieces):
    own = jnp.concatenate(pieces, axis=1)
    return own, ring(own, "core", CORE, 1)


def out_projection(attended, own_weight, other_weight):
    rows, depth = attended.shape
    half = depth // 2
    core = lax.axis_index("core")
    group = lax.all_gather(attended, "z", axis=0, tiled=True)
    own_part = lax.dynamic_slice_in_dim(group, core * half, half, 1)
    other_part = lax.dynamic_slice_in_dim(group, (1 - core) * half, half, 1)
    columns = (
        jnp.dot(own_part, own_weight, preferred_element_type=F32)
        + jnp.dot(other_part, other_weight, preferred_element_type=F32)
    ).astype(BF)
    width = columns.shape[1] // X
    back = swap(columns.reshape(Z, rows, X * width), "z")
    by_x = in_order(
        [
            jnp.concatenate([back[z, :, d * width : (d + 1) * width] for z in range(Z)], axis=1)
            for d in range(X)
        ],
        lax.axis_index("x"),
    )
    return jnp.concatenate(by_x, axis=1)


def unit_terms(mlp_rows, weights):
    gate_part = jnp.dot(mlp_rows, weights[0], preferred_element_type=F32)
    upward = jnp.dot(mlp_rows, weights[1], preferred_element_type=F32)
    active = (jax.nn.gelu(gate_part, approximate=True) * upward).astype(BF)
    return lax.dot_general(
        active, weights[2], (((1,), (1,)), ((), ())), preferred_element_type=F32
    ).astype(BF)


def per_device(
    hidden,
    tree_q,
    tree_kv,
    kv_cache,
    cache_lengths,
    tree_parents,
    accepted,
    tenant_ranges,
    out_weight,
    mlp_weights,
    draft_weights,
    embedding,
    attn_post_gain,
    ff_pre_gain,
    ff_post_gain,
    final_gain,
):
    units = X * Z
    rows = units * ACC
    core = lax.axis_index("core")
    y = lax.axis_index("y")
    unit = lax.axis_index(XZ)
    weights = lax.all_gather(mlp_weights, YC, axis=2, tiled=True)
    chosen = (
        accepted[0][:, None] == jnp.arange(hidden.shape[0], dtype=jnp.int32)[None, :]
    ).astype(BF)

    def pick(values):
        return jnp.dot(chosen, values, preferred_element_type=F32).astype(BF)

    own_half = own_half_of(out_weight)
    pieces = [own_half] + [ring(own_half, "x", X, shift) for shift in range(1, X)]
    attended = attention(after(tree_q, own_half), tree_kv, kv_cache, cache_lengths, tree_parents)
    own_weight, other_weight = out_weights(after(pieces, attended))
    projected = out_projection(attended, own_weight, other_weight)
    first = (hidden.astype(F32) + rms_scale(projected, attn_post_gain)).astype(BF)
    normed = rms_scale(first, ff_pre_gain).astype(BF)
    mlp_rows = lax.all_gather(normed, XZ, axis=0, tiled=True)

    path_rows = spread(pick(normed), XZ, units).reshape(rows, -1)
    path_terms = swap(unit_terms(path_rows, weights).reshape(units, ACC, -1), XZ)
    path_sum = jnp.sum(path_terms.astype(F32), axis=0)
    path = (pick(first).astype(F32) + rms_scale(path_sum, ff_post_gain)).astype(BF)
    path_normed = rms_scale(path, final_gain).astype(BF)
    group_path = spread(path_normed, XZ, units).reshape(rows, -1)

    width = draft_weights.shape[2]
    before = jnp.einsum("rd,hde->hre", group_path, draft_weights, preferred_element_type=F32)
    own_columns = lax.dynamic_slice_in_dim(group_path, unit * width, width, 1)
    drafts = (own_columns.astype(F32)[None] + jax.nn.silu(before)).astype(BF)
    draft_copies = copies_of(drafts, units)
    drafts = jnp.transpose(swap(draft_copies, XZ), (1, 2, 0, 3)).reshape(HEADS, rows, -1)

    mlp_partial = unit_terms(after(mlp_rows, draft_copies), weights)
    mlp_sum = lax.psum_scatter(after(mlp_partial, drafts), XZ, scatter_dimension=0, tiled=True)

    vocab_width = embedding.shape[0]
    start = lax.axis_index(ALL) * vocab_width
    order = [((y + dy) % Y) * CORE + (core + dc) % CORE for dy, dc in GROUPS]
    place = jnp.stack([start] + order).astype(jnp.int32)
    bounds = jnp.repeat(tenant_ranges, ACC, axis=0).reshape(Y * CORE, rows, 2)
    half = HEADS // 2
    pair = ((0, 0), (1, 0))
    four = pair + ((2, 0), (3, 0))
    low = drafts[:half]
    up_low, down_low = ring(low, "y", Y, 1), ring(low, "y", Y, 3)
    beside = ring(drafts, "core", CORE, 1)
    high = after(drafts[half:], beside)
    up_high, down_high = ring(high, "y", Y, 1), ring(high, "y", Y, 3)
    table_a, totals_a = some_logits(
        0, (2, HEADS), place, [drafts, beside], pair, bounds, embedding
    )
    up_low, down_low = after([up_low, down_low], totals_a)
    across_low = ring(up_low, "y", Y, 1)
    beside_low = [ring(piece, "core", CORE, 1) for piece in (up_low, down_low)]
    table_b, totals_b = some_logits(
        2,
        (4, half),
        place,
        [up_low, beside_low[0], down_low, beside_low[1]],
        four,
        bounds,
        embedding,
    )
    up_high, down_high = after([up_high, down_high], totals_b)
    across_high = ring(down_high, "y", Y, 3)
    beside_high = [ring(piece, "core", CORE, 1) for piece in (up_high, down_high)]
    table_c, totals_c = some_logits(
        2,
        (4, half),
        place,
        [up_high, beside_high[0], down_high, beside_high[1]],
        four,
        bounds,
        embedding,
    )
    across = after([across_low, across_high], totals_c)
    beside_across = [ring(piece, "core", CORE, 1) for piece in across]
    table_d, totals_d = some_logits(
        6,
        (2, HEADS),
        place,
        across + beside_across,
        ((0, 0), (0, half), (1, 0), (1, half)),
        bounds,
        embedding,
    )
    totals_b = jnp.concatenate([totals_b, totals_c], axis=1)
    sums = jnp.concatenate([totals_a, totals_b, totals_d], axis=0)
    here = place[1:, None] == jnp.arange(Y * CORE, dtype=jnp.int32)[None, :]
    sums = jnp.sum(jnp.where(here[:, :, None], sums[:, None, :], 0.0), axis=0)
    sums = jnp.sum(spread(sums, XZ, units), axis=0)
    around = [ring(sums, "y", Y, shift) for shift in range(1, Y)]
    mlp_sum = after(mlp_sum, sums)
    tree_out = (first.astype(F32) + rms_scale(mlp_sum, ff_post_gain)).astype(BF)
    around = after(around, tree_out)
    whole = sums + around[0] + around[1] + around[2]
    whole = whole + ring(whole, "core", CORE, 1)
    logs = jnp.transpose(jnp.log(whole).reshape(Y * CORE, HEADS, rows), (0, 2, 1))
    draft_logprobs = finish(place, [table_a, table_b, table_c, table_d], logs).reshape(
        HEADS, Y * CORE * rows, vocab_width
    )
    return (tree_out, draft_logprobs)


def solution(mesh):
    fine = Mesh(mesh.devices.reshape(Y, CORE, X, Z), ALL)
    return jax.shard_map(
        per_device,
        mesh=fine,
        in_specs=(
            P(ALL, None),
            P(ALL, None),
            P(ALL, None, None),
            P(ALL, None, None, None, None),
            P(ALL),
            P(ALL, None),
            P(ALL, None),
            P(),
            P(None, XZ),
            P(None, None, ALL),
            P(None, None, XZ),
            P(ALL, None),
            P(),
            P(),
            P(),
            P(),
        ),
        out_specs=(P(ALL, None), P(None, None, ALL)),
        check_vma=False,
    )
```

```python
import functools

import jax
import jax.numpy as jnp
from jax import lax
from jax.experimental import pallas as pl
from jax.experimental.pallas import tpu as pltpu
from jax.sharding import Mesh, PartitionSpec as P

BF = jnp.bfloat16
F32 = jnp.float32
QH = 8
KVH = 2
HD = 256
HEADS = 4
SOFTCAP = 30.0
Y, CORE, X, Z = 4, 2, 4, 4
EPS = 1e-06
ACC = 4
XZ = ("x", "z")
YC = ("y", "core")
ALL = ("y", "core", "x", "z")
GROUPS = ((0, 0), (0, 1), (1, 0), (1, 1), (3, 0), (3, 1), (2, 0), (2, 1))
CALLS = ((0, 2), (2, 6), (6, 8))
TILE = 256
VOCAB_BLOCK = 512
HIDDEN = -1e30
CONTRACT_LAST = (((1,), (1,)), ((), ()))


def attention_kernel(length_ref, q_ref, kv_ref, parents_ref, keys_ref, values_ref, out_ref, top, bottom, tree):
    rows = q_ref.shape[0]
    group = QH // KVH
    head, block = pl.program_id(0), pl.program_id(1)
    width = keys_ref.shape[0]
    queries = jnp.concatenate([q_ref[:, g * HD : (g + 1) * HD] for g in range(group)], axis=0)
    scale = HD ** (-0.5)

    @pl.when((head == 0) & (block == 0))
    def _():
        lanes = lax.broadcasted_iota(jnp.int32, (rows, rows), 1)
        subs = lax.broadcasted_iota(jnp.int32, (rows, rows), 0)
        reach = jnp.where((parents_ref[...] == lanes) | (subs == lanes), 1.0, 0.0)
        for _ in range(max(1, (rows - 1).bit_length())):
            half = reach.astype(BF)
            reach = jnp.minimum(jnp.dot(half, half, preferred_element_type=F32), 1.0)
        tree[...] = reach

    @pl.when(block == 0)
    def _():
        keys = kv_ref[0]
        scores = lax.dot_general(queries, keys, CONTRACT_LAST, preferred_element_type=F32)
        reach = tree[...]
        weights = jnp.exp(scores * scale) * jnp.concatenate([reach] * group, axis=0)
        bottom[...] = jnp.sum(weights, axis=1, keepdims=True)
        top[...] = jnp.dot(weights.astype(BF), kv_ref[1], preferred_element_type=F32)

    scores = lax.dot_general(queries, keys_ref[...], CONTRACT_LAST, preferred_element_type=F32)
    slots = block * width + lax.broadcasted_iota(jnp.int32, scores.shape, 1)
    weights = jnp.where(slots < length_ref[0], jnp.exp(scores * scale), 0.0)
    bottom[...] += jnp.sum(weights, axis=1, keepdims=True)
    top[...] += jnp.dot(weights.astype(BF), values_ref[...], preferred_element_type=F32)

    @pl.when(block == pl.num_programs(1) - 1)
    def _():
        attended = (top[...] / bottom[...]).astype(BF)
        for g in range(group):
            out_ref[:, g * HD : (g + 1) * HD] = attended[g * rows : (g + 1) * rows]


def attention(tree_q, tree_kv, kv_cache, cache_lengths, tree_parents):
    rows = tree_q.shape[0]
    group = QH // KVH
    slots = kv_cache.shape[3]
    block = min(1024, slots)
    kv = jnp.transpose(tree_kv, (1, 0, 2))
    spec = pl.BlockSpec
    return pl.pallas_call(
        attention_kernel,
        out_shape=jax.ShapeDtypeStruct((rows, QH * HD), BF),
        grid_spec=pltpu.PrefetchScalarGridSpec(
            num_scalar_prefetch=1,
            grid=(KVH, slots // block),
            in_specs=[
                spec((rows, group * HD), lambda k, b, n: (0, k)),
                spec((2, rows, HD), lambda k, b, n: (0, 0, k)),
                spec((rows, 1), lambda k, b, n: (0, 0)),
                spec((None, None, None, block, HD), lambda k, b, n: (0, 0, k, b, 0)),
                spec((None, None, None, block, HD), lambda k, b, n: (0, 1, k, b, 0)),
            ],
            out_specs=spec((rows, group * HD), lambda k, b, n: (0, k)),
            scratch_shapes=[
                pltpu.VMEM((group * rows, HD), F32),
                pltpu.VMEM((group * rows, 1), F32),
                pltpu.VMEM((rows, rows), F32),
            ],
        ),
        compiler_params=pltpu.CompilerParams(
            dimension_semantics=("arbitrary", "arbitrary"), vmem_limit_bytes=24 << 20
        ),
        cost_estimate=pl.CostEstimate(
            flops=4 * rows * QH * HD * slots,
            bytes_accessed=4 * KVH * slots * HD,
            transcendentals=rows * QH * slots,
        ),
    )(cache_lengths, tree_q, kv, tree_parents.reshape(rows, 1), kv_cache, kv_cache)


def logits_kernel(first, parts, place_ref, *refs):
    pieces = refs[: len(parts)]
    bounds_ref, embedding_ref, out_ref, totals_ref, rows_ref, running = refs[len(parts) :]
    step, steps = pl.program_id(0), pl.num_programs(0)
    groups, heads, count, depth = rows_ref.shape
    vocab = embedding_ref.shape[0]

    @pl.when(step == 0)
    def _():
        for piece, (group, low) in zip(pieces, parts):
            rows_ref[group, low : low + piece.shape[0]] = piece[...]
        running[...] = jnp.zeros_like(running)

    every = rows_ref[...].reshape(groups * heads * count, depth)
    ids = place_ref[0] + step * vocab + lax.broadcasted_iota(jnp.int32, (count, TILE), 1)
    for tile in range(0, vocab, TILE):
        products = lax.dot_general(
            every,
            embedding_ref[tile : tile + TILE],
            CONTRACT_LAST,
            preferred_element_type=F32,
        )
        for group in range(groups):
            bounds = bounds_ref[place_ref[1 + first + group]] - tile
            allowed = (ids >= bounds[:, 0:1]) & (ids < bounds[:, 1:2])
            for head in range(heads):
                low = (group * heads + head) * count
                bent = jnp.tanh(products[low : low + count] * (1.0 / SOFTCAP))
                terms = jnp.where(allowed, jnp.exp(bent * SOFTCAP), 0.0)
                kept = jnp.where(allowed, bent * SOFTCAP, HIDDEN).astype(BF)
                out_ref[group, head, :, tile : tile + TILE] = kept
                part = terms[:, :128]
                for lane in range(128, TILE, 128):
                    part = part + terms[:, lane : lane + 128]
                running[low : low + count] += part

    @pl.when(step == steps - 1)
    def _():
        size = heads * count
        for group in range(groups):
            totals_ref[group : group + 1, :] = jnp.sum(
                jnp.transpose(running[group * size : (group + 1) * size]), axis=0, keepdims=True
            )


def some_logits(first, shape, place, pieces, parts, bounds, embedding):
    groups, heads = shape
    count, depth = pieces[0].shape[1:]
    vocab_width = embedding.shape[0]
    vocab = min(VOCAB_BLOCK, vocab_width)
    size = groups * heads * count
    spec = pl.BlockSpec
    return pl.pallas_call(
        functools.partial(logits_kernel, first, parts),
        out_shape=(
            jax.ShapeDtypeStruct((groups, heads, count, vocab_width), BF),
            jax.ShapeDtypeStruct((groups, heads * count), F32),
        ),
        grid_spec=pltpu.PrefetchScalarGridSpec(
            num_scalar_prefetch=1,
            grid=(vocab_width // vocab,),
            in_specs=[
                spec(piece.shape, lambda j, p: (0, 0, 0), pipeline_mode=pl.Buffered(1))
                for piece in pieces
            ]
            + [
                spec(bounds.shape, lambda j, p: (0, 0, 0)),
                spec((vocab, depth), lambda j, p: (j, 0)),
            ],
            out_specs=(
                spec((groups, heads, count, vocab), lambda j, p: (0, 0, 0, j)),
                spec((groups, heads * count), lambda j, p: (0, 0)),
            ),
            scratch_shapes=[
                pltpu.VMEM((groups, heads, count, depth), BF),
                pltpu.VMEM((size, 128), F32),
            ],
        ),
        compiler_params=pltpu.CompilerParams(
            dimension_semantics=("arbitrary",), vmem_limit_bytes=50 << 20
        ),
        cost_estimate=pl.CostEstimate(
            flops=2 * size * vocab_width * depth,
            bytes_accessed=2 * vocab_width * depth + 2 * size * vocab_width,
            transcendentals=2 * size * vocab_width,
        ),
    )(place, *pieces, bounds, embedding)


def finish_kernel(place_ref, *refs):
    logs_ref, out_ref = refs[-2:]
    tables = ((refs[0],), refs[1:3], (refs[3],))
    step = pl.program_id(0)
    core = lax.rem(place_ref[1], CORE)
    for shared, (first, last) in zip(tables, CALLS):

        @pl.when((step >= first // CORE) & (step < last // CORE))
        def _(shared=shared):
            heads = HEADS // len(shared)
            for position in range(CORE):
                source = lax.rem(position + core, CORE)
                for head in range(HEADS):
                    values = shared[head // heads][source, head % heads].astype(F32)
                    shifted = values - logs_ref[position, :, head : head + 1]
                    out_ref[head, position] = jnp.where(
                        values > 0.5 * HIDDEN, shifted, 0.0
                    ).astype(BF)


def finish(place, tables, logs):
    count, vocab_width = tables[0].shape[2:]
    groups = len(GROUPS)
    spec = pl.BlockSpec

    def table_spec(table, first, last):
        return spec(
            (CORE, table.shape[1], count, vocab_width),
            lambda k, p: (jnp.clip(k - first // CORE, 0, (last - first) // CORE - 1), 0, 0, 0),
        )

    def pair(k, p):
        return lax.div(p[1 + CORE * k], CORE)

    calls = (CALLS[0], CALLS[1], CALLS[1], CALLS[2])
    return pl.pallas_call(
        finish_kernel,
        out_shape=jax.ShapeDtypeStruct((HEADS, groups, count, vocab_width), BF),
        grid_spec=pltpu.PrefetchScalarGridSpec(
            num_scalar_prefetch=1,
            grid=(groups // CORE,),
            in_specs=[table_spec(table, *call) for table, call in zip(tables, calls)]
            + [spec((CORE, count, HEADS), lambda k, p: (pair(k, p), 0, 0))],
            out_specs=spec(
                (HEADS, CORE, count, vocab_width), lambda k, p: (0, pair(k, p), 0, 0)
            ),
        ),
        compiler_params=pltpu.CompilerParams(
            dimension_semantics=("arbitrary",), vmem_limit_bytes=56 << 20
        ),
        cost_estimate=pl.CostEstimate(
            flops=3 * groups * HEADS * count * vocab_width,
            bytes_accessed=4 * groups * HEADS * count * vocab_width,
            transcendentals=0,
        ),
    )(place, *tables, logs)


def rms_scale(values, gain):
    floats = values.astype(F32)
    return (
        floats
        * lax.rsqrt(jnp.mean(floats * floats, axis=-1, keepdims=True) + EPS)
        * gain.astype(F32)
    )


def after(values, *earlier):
    return lax.optimization_barrier((values, earlier))[0]


def ring(values, axis, size, shift):
    return lax.ppermute(values, axis, [((i + shift) % size, i) for i in range(size)])


def copies_of(values, size):
    return lax.optimization_barrier(jnp.broadcast_to(values[None], (size,) + values.shape))


def swap(copies, axes):
    return lax.all_to_all(copies, axes, split_axis=0, concat_axis=0, tiled=True)


def spread(values, axes, size):
    return swap(copies_of(values, size), axes)


def in_order(blocks, index):
    size = len(blocks)
    ordered = []
    for position in range(size):
        shift = (position - index) % size
        block = blocks[0]
        for candidate in range(1, size):
            block = jnp.where(shift == candidate, blocks[candidate], block)
        ordered.append(block)
    return ordered


def own_half_of(out_weight):
    half = out_weight.shape[0] // 2
    return lax.dynamic_slice_in_dim(out_weight, lax.axis_index("core") * half, half, 0)


def out_weights(pieces):
    own = jnp.concatenate(pieces, axis=1)
    return own, ring(own, "core", CORE, 1)


def out_projection(attended, own_weight, other_weight):
    rows, depth = attended.shape
    half = depth // 2
    core = lax.axis_index("core")
    group = lax.all_gather(attended, "z", axis=0, tiled=True)
    own_part = lax.dynamic_slice_in_dim(group, core * half, half, 1)
    other_part = lax.dynamic_slice_in_dim(group, (1 - core) * half, half, 1)
    columns = (
        jnp.dot(own_part, own_weight, preferred_element_type=F32)
        + jnp.dot(other_part, other_weight, preferred_element_type=F32)
    ).astype(BF)
    width = columns.shape[1] // X
    back = swap(columns.reshape(Z, rows, X * width), "z")
    by_x = in_order(
        [
            jnp.concatenate([back[z, :, d * width : (d + 1) * width] for z in range(Z)], axis=1)
            for d in range(X)
        ],
        lax.axis_index("x"),
    )
    return jnp.concatenate(by_x, axis=1)


def unit_terms(mlp_rows, weights):
    gate_part = jnp.dot(mlp_rows, weights[0], preferred_element_type=F32)
    upward = jnp.dot(mlp_rows, weights[1], preferred_element_type=F32)
    active = (jax.nn.gelu(gate_part, approximate=True) * upward).astype(BF)
    return lax.dot_general(
        active, weights[2], (((1,), (1,)), ((), ())), preferred_element_type=F32
    ).astype(BF)


def per_device(
    hidden,
    tree_q,
    tree_kv,
    kv_cache,
    cache_lengths,
    tree_parents,
    accepted,
    tenant_ranges,
    out_weight,
    mlp_weights,
    draft_weights,
    embedding,
    attn_post_gain,
    ff_pre_gain,
    ff_post_gain,
    final_gain,
):
    units = X * Z
    rows = units * ACC
    core = lax.axis_index("core")
    y = lax.axis_index("y")
    unit = lax.axis_index(XZ)
    weights = lax.all_gather(mlp_weights, YC, axis=2, tiled=True)
    chosen = (
        accepted[0][:, None] == jnp.arange(hidden.shape[0], dtype=jnp.int32)[None, :]
    ).astype(BF)

    def pick(values):
        return jnp.dot(chosen, values, preferred_element_type=F32).astype(BF)

    own_half = own_half_of(out_weight)
    pieces = [own_half] + [ring(own_half, "x", X, shift) for shift in range(1, X)]
    attended = attention(after(tree_q, own_half), tree_kv, kv_cache, cache_lengths, tree_parents)
    own_weight, other_weight = out_weights(after(pieces, attended))
    projected = out_projection(attended, own_weight, other_weight)
    first = (hidden.astype(F32) + rms_scale(projected, attn_post_gain)).astype(BF)
    normed = rms_scale(first, ff_pre_gain).astype(BF)
    mlp_rows = lax.all_gather(normed, XZ, axis=0, tiled=True)

    path_rows = spread(pick(normed), XZ, units).reshape(rows, -1)
    path_terms = swap(unit_terms(path_rows, weights).reshape(units, ACC, -1), XZ)
    path_sum = jnp.sum(path_terms.astype(F32), axis=0)
    path = (pick(first).astype(F32) + rms_scale(path_sum, ff_post_gain)).astype(BF)
    path_normed = rms_scale(path, final_gain).astype(BF)
    group_path = spread(path_normed, XZ, units).reshape(rows, -1)

    width = draft_weights.shape[2]
    before = jnp.einsum("rd,hde->hre", group_path, draft_weights, preferred_element_type=F32)
    own_columns = lax.dynamic_slice_in_dim(group_path, unit * width, width, 1)
    drafts = (own_columns.astype(F32)[None] + jax.nn.silu(before)).astype(BF)
    draft_copies = copies_of(drafts, units)
    drafts = jnp.transpose(swap(draft_copies, XZ), (1, 2, 0, 3)).reshape(HEADS, rows, -1)

    mlp_partial = unit_terms(after(mlp_rows, draft_copies), weights)
    mlp_sum = lax.psum_scatter(after(mlp_partial, drafts), XZ, scatter_dimension=0, tiled=True)

    vocab_width = embedding.shape[0]
    start = lax.axis_index(ALL) * vocab_width
    order = [((y + dy) % Y) * CORE + (core + dc) % CORE for dy, dc in GROUPS]
    place = jnp.stack([start] + order).astype(jnp.int32)
    bounds = jnp.repeat(tenant_ranges, ACC, axis=0).reshape(Y * CORE, rows, 2)
    half = HEADS // 2
    pair = ((0, 0), (1, 0))
    four = pair + ((2, 0), (3, 0))
    low = drafts[:half]
    up_low, down_low = ring(low, "y", Y, 1), ring(low, "y", Y, 3)
    beside = ring(drafts, "core", CORE, 1)
    high = after(drafts[half:], beside)
    up_high, down_high = ring(high, "y", Y, 1), ring(high, "y", Y, 3)
    table_a, totals_a = some_logits(
        0, (2, HEADS), place, [drafts, beside], pair, bounds, embedding
    )
    up_low, down_low = after([up_low, down_low], totals_a)
    across_low = ring(up_low, "y", Y, 1)
    beside_low = [ring(piece, "core", CORE, 1) for piece in (up_low, down_low)]
    table_b, totals_b = some_logits(
        2,
        (4, half),
        place,
        [up_low, beside_low[0], down_low, beside_low[1]],
        four,
        bounds,
        embedding,
    )
    up_high, down_high = after([up_high, down_high], totals_b)
    across_high = ring(down_high, "y", Y, 3)
    beside_high = [ring(piece, "core", CORE, 1) for piece in (up_high, down_high)]
    table_c, totals_c = some_logits(
        2,
        (4, half),
        place,
        [up_high, beside_high[0], down_high, beside_high[1]],
        four,
        bounds,
        embedding,
    )
    across = after([across_low, across_high], totals_c)
    beside_across = [ring(piece, "core", CORE, 1) for piece in across]
    table_d, totals_d = some_logits(
        6,
        (2, HEADS),
        place,
        across + beside_across,
        ((0, 0), (0, half), (1, 0), (1, half)),
        bounds,
        embedding,
    )
    totals_b = jnp.concatenate([totals_b, totals_c], axis=1)
    sums = jnp.concatenate([totals_a, totals_b, totals_d], axis=0)
    here = place[1:, None] == jnp.arange(Y * CORE, dtype=jnp.int32)[None, :]
    sums = jnp.sum(jnp.where(here[:, :, None], sums[:, None, :], 0.0), axis=0)
    sums = jnp.sum(spread(sums, XZ, units), axis=0)
    around = [ring(sums, "y", Y, shift) for shift in range(1, Y)]
    mlp_sum = after(mlp_sum, sums)
    tree_out = (first.astype(F32) + rms_scale(mlp_sum, ff_post_gain)).astype(BF)
    around = after(around, tree_out)
    whole = sums + around[0] + around[1] + around[2]
    whole = whole + ring(whole, "core", CORE, 1)
    logs = jnp.transpose(jnp.log(whole).reshape(Y * CORE, HEADS, rows), (0, 2, 1))
    draft_logprobs = finish(place, [table_a, table_b, table_c, table_d], logs).reshape(
        HEADS, Y * CORE * rows, vocab_width
    )
    return (tree_out, draft_logprobs)


def solution(mesh):
    fine = Mesh(mesh.devices.reshape(Y, CORE, X, Z), ALL)
    return jax.shard_map(
        per_device,
        mesh=fine,
        in_specs=(
            P(ALL, None),
            P(ALL, None),
            P(ALL, None, None),
            P(ALL, None, None, None, None),
            P(ALL),
            P(ALL, None),
            P(ALL, None),
            P(),
            P(None, XZ),
            P(None, None, ALL),
            P(None, None, XZ),
            P(ALL, None),
            P(),
            P(),
            P(),
            P(),
        ),
        out_specs=(P(ALL, None), P(None, None, ALL)),
        check_vma=False,
    )
```

```python
import functools

import jax
import jax.numpy as jnp
from jax import lax
from jax.experimental import pallas as pl
from jax.experimental.pallas import tpu as pltpu
from jax.sharding import Mesh, PartitionSpec as P

BF = jnp.bfloat16
F32 = jnp.float32
QH = 8
KVH = 2
HD = 256
HEADS = 4
SOFTCAP = 30.0
Y, CORE, X, Z = 4, 2, 4, 4
EPS = 1e-06
ACC = 4
XZ = ("x", "z")
YC = ("y", "core")
ALL = ("y", "core", "x", "z")
GROUPS = ((0, 0), (0, 1), (1, 0), (1, 1), (3, 0), (3, 1), (2, 0), (2, 1))
CALLS = ((0, 2), (2, 6), (6, 8))
TILE = 256
VOCAB_BLOCK = 512
HIDDEN = -1e30
CONTRACT_LAST = (((1,), (1,)), ((), ()))


def attention_kernel(length_ref, q_ref, kv_ref, parents_ref, keys_ref, values_ref, out_ref, top, bottom, tree):
    rows = q_ref.shape[0]
    group = QH // KVH
    head, block = pl.program_id(0), pl.program_id(1)
    width = keys_ref.shape[0]
    queries = jnp.concatenate([q_ref[:, g * HD : (g + 1) * HD] for g in range(group)], axis=0)
    scale = HD ** (-0.5)

    @pl.when((head == 0) & (block == 0))
    def _():
        lanes = lax.broadcasted_iota(jnp.int32, (rows, rows), 1)
        subs = lax.broadcasted_iota(jnp.int32, (rows, rows), 0)
        reach = jnp.where((parents_ref[...] == lanes) | (subs == lanes), 1.0, 0.0)
        for _ in range(max(1, (rows - 1).bit_length())):
            half = reach.astype(BF)
            reach = jnp.minimum(jnp.dot(half, half, preferred_element_type=F32), 1.0)
        tree[...] = reach

    @pl.when(block == 0)
    def _():
        keys = kv_ref[0]
        scores = lax.dot_general(queries, keys, CONTRACT_LAST, preferred_element_type=F32)
        reach = tree[...]
        weights = jnp.exp(scores * scale) * jnp.concatenate([reach] * group, axis=0)
        bottom[...] = jnp.sum(weights, axis=1, keepdims=True)
        top[...] = jnp.dot(weights.astype(BF), kv_ref[1], preferred_element_type=F32)

    scores = lax.dot_general(queries, keys_ref[...], CONTRACT_LAST, preferred_element_type=F32)
    slots = block * width + lax.broadcasted_iota(jnp.int32, scores.shape, 1)
    weights = jnp.where(slots < length_ref[0], jnp.exp(scores * scale), 0.0)
    bottom[...] += jnp.sum(weights, axis=1, keepdims=True)
    top[...] += jnp.dot(weights.astype(BF), values_ref[...], preferred_element_type=F32)

    @pl.when(block == pl.num_programs(1) - 1)
    def _():
        attended = (top[...] / bottom[...]).astype(BF)
        for g in range(group):
            out_ref[:, g * HD : (g + 1) * HD] = attended[g * rows : (g + 1) * rows]


def attention(tree_q, tree_kv, kv_cache, cache_lengths, tree_parents):
    rows = tree_q.shape[0]
    group = QH // KVH
    slots = kv_cache.shape[3]
    block = min(1024, slots)
    kv = jnp.transpose(tree_kv, (1, 0, 2))
    spec = pl.BlockSpec
    return pl.pallas_call(
        attention_kernel,
        out_shape=jax.ShapeDtypeStruct((rows, QH * HD), BF),
        grid_spec=pltpu.PrefetchScalarGridSpec(
            num_scalar_prefetch=1,
            grid=(KVH, slots // block),
            in_specs=[
                spec((rows, group * HD), lambda k, b, n: (0, k)),
                spec((2, rows, HD), lambda k, b, n: (0, 0, k)),
                spec((rows, 1), lambda k, b, n: (0, 0)),
                spec((None, None, None, block, HD), lambda k, b, n: (0, 0, k, b, 0)),
                spec((None, None, None, block, HD), lambda k, b, n: (0, 1, k, b, 0)),
            ],
            out_specs=spec((rows, group * HD), lambda k, b, n: (0, k)),
            scratch_shapes=[
                pltpu.VMEM((group * rows, HD), F32),
                pltpu.VMEM((group * rows, 1), F32),
                pltpu.VMEM((rows, rows), F32),
            ],
        ),
        compiler_params=pltpu.CompilerParams(
            dimension_semantics=("arbitrary", "arbitrary"), vmem_limit_bytes=24 << 20
        ),
        cost_estimate=pl.CostEstimate(
            flops=4 * rows * QH * HD * slots,
            bytes_accessed=4 * KVH * slots * HD,
            transcendentals=rows * QH * slots,
        ),
    )(cache_lengths, tree_q, kv, tree_parents.reshape(rows, 1), kv_cache, kv_cache)


def logits_kernel(first, parts, place_ref, *refs):
    pieces = refs[: len(parts)]
    bounds_ref, embedding_ref, out_ref, totals_ref, rows_ref, running = refs[len(parts) :]
    step, steps = pl.program_id(0), pl.num_programs(0)
    groups, heads, count, depth = rows_ref.shape
    vocab = embedding_ref.shape[0]

    @pl.when(step == 0)
    def _():
        for piece, (group, low) in zip(pieces, parts):
            rows_ref[group, low : low + piece.shape[0]] = piece[...]
        running[...] = jnp.zeros_like(running)

    every = rows_ref[...].reshape(groups * heads * count, depth)
    ids = place_ref[0] + step * vocab + lax.broadcasted_iota(jnp.int32, (count, TILE), 1)
    for tile in range(0, vocab, TILE):
        products = lax.dot_general(
            every,
            embedding_ref[tile : tile + TILE],
            CONTRACT_LAST,
            preferred_element_type=F32,
        )
        for group in range(groups):
            bounds = bounds_ref[place_ref[1 + first + group]] - tile
            allowed = (ids >= bounds[:, 0:1]) & (ids < bounds[:, 1:2])
            for head in range(heads):
                low = (group * heads + head) * count
                bent = jnp.tanh(products[low : low + count] * (1.0 / SOFTCAP))
                terms = jnp.where(allowed, jnp.exp(bent * SOFTCAP), 0.0)
                kept = jnp.where(allowed, bent * SOFTCAP, HIDDEN).astype(BF)
                out_ref[group, head, :, tile : tile + TILE] = kept
                part = terms[:, :128]
                for lane in range(128, TILE, 128):
                    part = part + terms[:, lane : lane + 128]
                running[low : low + count] += part

    @pl.when(step == steps - 1)
    def _():
        size = heads * count
        for group in range(groups):
            totals_ref[group : group + 1, :] = jnp.sum(
                jnp.transpose(running[group * size : (group + 1) * size]), axis=0, keepdims=True
            )


def some_logits(first, shape, place, pieces, parts, bounds, embedding):
    groups, heads = shape
    count, depth = pieces[0].shape[1:]
    vocab_width = embedding.shape[0]
    vocab = min(VOCAB_BLOCK, vocab_width)
    size = groups * heads * count
    spec = pl.BlockSpec
    return pl.pallas_call(
        functools.partial(logits_kernel, first, parts),
        out_shape=(
            jax.ShapeDtypeStruct((groups, heads, count, vocab_width), BF),
            jax.ShapeDtypeStruct((groups, heads * count), F32),
        ),
        grid_spec=pltpu.PrefetchScalarGridSpec(
            num_scalar_prefetch=1,
            grid=(vocab_width // vocab,),
            in_specs=[
                spec(piece.shape, lambda j, p: (0, 0, 0), pipeline_mode=pl.Buffered(1))
                for piece in pieces
            ]
            + [
                spec(bounds.shape, lambda j, p: (0, 0, 0)),
                spec((vocab, depth), lambda j, p: (j, 0)),
            ],
            out_specs=(
                spec((groups, heads, count, vocab), lambda j, p: (0, 0, 0, j)),
                spec((groups, heads * count), lambda j, p: (0, 0)),
            ),
            scratch_shapes=[
                pltpu.VMEM((groups, heads, count, depth), BF),
                pltpu.VMEM((size, 128), F32),
            ],
        ),
        compiler_params=pltpu.CompilerParams(
            dimension_semantics=("arbitrary",), vmem_limit_bytes=50 << 20
        ),
        cost_estimate=pl.CostEstimate(
            flops=2 * size * vocab_width * depth,
            bytes_accessed=2 * vocab_width * depth + 2 * size * vocab_width,
            transcendentals=2 * size * vocab_width,
        ),
    )(place, *pieces, bounds, embedding)


def finish_kernel(place_ref, *refs):
    logs_ref, out_ref = refs[-2:]
    tables = ((refs[0],), refs[1:3], (refs[3],))
    step = pl.program_id(0)
    core = lax.rem(place_ref[1], CORE)
    for shared, (first, last) in zip(tables, CALLS):

        @pl.when((step >= first // CORE) & (step < last // CORE))
        def _(shared=shared):
            heads = HEADS // len(shared)
            for position in range(CORE):
                source = lax.rem(position + core, CORE)
                for head in range(HEADS):
                    values = shared[head // heads][source, head % heads].astype(F32)
                    shifted = values - logs_ref[position, :, head : head + 1]
                    out_ref[head, position] = jnp.where(
                        values > 0.5 * HIDDEN, shifted, 0.0
                    ).astype(BF)


def finish(place, tables, logs):
    count, vocab_width = tables[0].shape[2:]
    groups = len(GROUPS)
    spec = pl.BlockSpec

    def table_spec(table, first, last):
        return spec(
            (CORE, table.shape[1], count, vocab_width),
            lambda k, p: (jnp.clip(k - first // CORE, 0, (last - first) // CORE - 1), 0, 0, 0),
        )

    def pair(k, p):
        return lax.div(p[1 + CORE * k], CORE)

    calls = (CALLS[0], CALLS[1], CALLS[1], CALLS[2])
    return pl.pallas_call(
        finish_kernel,
        out_shape=jax.ShapeDtypeStruct((HEADS, groups, count, vocab_width), BF),
        grid_spec=pltpu.PrefetchScalarGridSpec(
            num_scalar_prefetch=1,
            grid=(groups // CORE,),
            in_specs=[table_spec(table, *call) for table, call in zip(tables, calls)]
            + [spec((CORE, count, HEADS), lambda k, p: (pair(k, p), 0, 0))],
            out_specs=spec(
                (HEADS, CORE, count, vocab_width), lambda k, p: (0, pair(k, p), 0, 0)
            ),
        ),
        compiler_params=pltpu.CompilerParams(
            dimension_semantics=("arbitrary",), vmem_limit_bytes=56 << 20
        ),
        cost_estimate=pl.CostEstimate(
            flops=3 * groups * HEADS * count * vocab_width,
            bytes_accessed=4 * groups * HEADS * count * vocab_width,
            transcendentals=0,
        ),
    )(place, *tables, logs)


def rms_scale(values, gain):
    floats = values.astype(F32)
    return (
        floats
        * lax.rsqrt(jnp.mean(floats * floats, axis=-1, keepdims=True) + EPS)
        * gain.astype(F32)
    )


def after(values, *earlier):
    return lax.optimization_barrier((values, earlier))[0]


def ring(values, axis, size, shift):
    return lax.ppermute(values, axis, [((i + shift) % size, i) for i in range(size)])


def copies_of(values, size):
    return lax.optimization_barrier(jnp.broadcast_to(values[None], (size,) + values.shape))


def swap(copies, axes):
    return lax.all_to_all(copies, axes, split_axis=0, concat_axis=0, tiled=True)


def spread(values, axes, size):
    return swap(copies_of(values, size), axes)


def in_order(blocks, index):
    size = len(blocks)
    ordered = []
    for position in range(size):
        shift = (position - index) % size
        block = blocks[0]
        for candidate in range(1, size):
            block = jnp.where(shift == candidate, blocks[candidate], block)
        ordered.append(block)
    return ordered


def out_projection(group, weights):
    rows = group.shape[0] // Z
    columns = jnp.concatenate(
        [jnp.dot(group, w, preferred_element_type=F32).astype(BF) for w in weights], axis=1
    )
    width = columns.shape[1] // X
    back = swap(columns.reshape(Z, rows, X * width), "z")
    by_x = in_order(
        [
            jnp.concatenate([back[z, :, d * width : (d + 1) * width] for z in range(Z)], axis=1)
            for d in range(X)
        ],
        lax.axis_index("x"),
    )
    return jnp.concatenate(by_x, axis=1)


def unit_terms(mlp_rows, weights):
    gate_part = jnp.dot(mlp_rows, weights[0], preferred_element_type=F32)
    upward = jnp.dot(mlp_rows, weights[1], preferred_element_type=F32)
    active = (jax.nn.gelu(gate_part, approximate=True) * upward).astype(BF)
    return lax.dot_general(
        active, weights[2], (((1,), (1,)), ((), ())), preferred_element_type=F32
    ).astype(BF)


def per_device(
    hidden,
    tree_q,
    tree_kv,
    kv_cache,
    cache_lengths,
    tree_parents,
    accepted,
    tenant_ranges,
    out_weight,
    mlp_weights,
    draft_weights,
    embedding,
    attn_post_gain,
    ff_pre_gain,
    ff_post_gain,
    final_gain,
):
    units = X * Z
    rows = units * ACC
    core = lax.axis_index("core")
    y = lax.axis_index("y")
    unit = lax.axis_index(XZ)
    weights = lax.all_gather(mlp_weights, YC, axis=2, tiled=True)
    chosen = (
        accepted[0][:, None] == jnp.arange(hidden.shape[0], dtype=jnp.int32)[None, :]
    ).astype(BF)

    def pick(values):
        return jnp.dot(chosen, values, preferred_element_type=F32).astype(BF)

    pieces = [ring(out_weight, "x", X, shift) for shift in range(1, X)]
    attended = attention(tree_q, tree_kv, kv_cache, cache_lengths, tree_parents)
    group = lax.all_gather(attended, "z", axis=0, tiled=True)
    projected = out_projection(group, [out_weight] + after(pieces, group))
    first = (hidden.astype(F32) + rms_scale(projected, attn_post_gain)).astype(BF)
    normed = rms_scale(first, ff_pre_gain).astype(BF)
    mlp_rows = lax.all_gather(normed, XZ, axis=0, tiled=True)

    path_rows = spread(pick(normed), XZ, units).reshape(rows, -1)
    path_terms = swap(unit_terms(path_rows, weights).reshape(units, ACC, -1), XZ)
    path_sum = jnp.sum(path_terms.astype(F32), axis=0)
    path = (pick(first).astype(F32) + rms_scale(path_sum, ff_post_gain)).astype(BF)
    path_normed = rms_scale(path, final_gain).astype(BF)
    group_path = spread(path_normed, XZ, units).reshape(rows, -1)

    width = draft_weights.shape[2]
    before = jnp.einsum("rd,hde->hre", group_path, draft_weights, preferred_element_type=F32)
    own_columns = lax.dynamic_slice_in_dim(group_path, unit * width, width, 1)
    drafts = (own_columns.astype(F32)[None] + jax.nn.silu(before)).astype(BF)
    draft_copies = copies_of(drafts, units)
    drafts = jnp.transpose(swap(draft_copies, XZ), (1, 2, 0, 3)).reshape(HEADS, rows, -1)

    mlp_partial = unit_terms(after(mlp_rows, draft_copies), weights)
    mlp_sum = lax.psum_scatter(after(mlp_partial, drafts), XZ, scatter_dimension=0, tiled=True)

    vocab_width = embedding.shape[0]
    start = lax.axis_index(ALL) * vocab_width
    order = [((y + dy) % Y) * CORE + (core + dc) % CORE for dy, dc in GROUPS]
    place = jnp.stack([start] + order).astype(jnp.int32)
    bounds = jnp.repeat(tenant_ranges, ACC, axis=0).reshape(Y * CORE, rows, 2)
    half = HEADS // 2
    pair = ((0, 0), (1, 0))
    four = pair + ((2, 0), (3, 0))
    low = drafts[:half]
    up_low, down_low = ring(low, "y", Y, 1), ring(low, "y", Y, 3)
    beside = ring(drafts, "core", CORE, 1)
    high = after(drafts[half:], beside)
    up_high, down_high = ring(high, "y", Y, 1), ring(high, "y", Y, 3)
    table_a, totals_a = some_logits(
        0, (2, HEADS), place, [drafts, beside], pair, bounds, embedding
    )
    up_low, down_low = after([up_low, down_low], totals_a)
    across_low = ring(up_low, "y", Y, 1)
    beside_low = [ring(piece, "core", CORE, 1) for piece in (up_low, down_low)]
    table_b, totals_b = some_logits(
        2,
        (4, half),
        place,
        [up_low, beside_low[0], down_low, beside_low[1]],
        four,
        bounds,
        embedding,
    )
    up_high, down_high = after([up_high, down_high], totals_b)
    across_high = ring(down_high, "y", Y, 3)
    beside_high = [ring(piece, "core", CORE, 1) for piece in (up_high, down_high)]
    table_c, totals_c = some_logits(
        2,
        (4, half),
        place,
        [up_high, beside_high[0], down_high, beside_high[1]],
        four,
        bounds,
        embedding,
    )
    across = after([across_low, across_high], totals_c)
    beside_across = [ring(piece, "core", CORE, 1) for piece in across]
    table_d, totals_d = some_logits(
        6,
        (2, HEADS),
        place,
        across + beside_across,
        ((0, 0), (0, half), (1, 0), (1, half)),
        bounds,
        embedding,
    )
    totals_b = jnp.concatenate([totals_b, totals_c], axis=1)
    sums = jnp.concatenate([totals_a, totals_b, totals_d], axis=0)
    here = place[1:, None] == jnp.arange(Y * CORE, dtype=jnp.int32)[None, :]
    sums = jnp.sum(jnp.where(here[:, :, None], sums[:, None, :], 0.0), axis=0)
    sums = jnp.sum(spread(sums, XZ, units), axis=0)
    around = [ring(sums, "y", Y, shift) for shift in range(1, Y)]
    mlp_sum = after(mlp_sum, sums)
    tree_out = (first.astype(F32) + rms_scale(mlp_sum, ff_post_gain)).astype(BF)
    around = after(around, tree_out)
    whole = sums + around[0] + around[1] + around[2]
    whole = whole + ring(whole, "core", CORE, 1)
    logs = jnp.transpose(jnp.log(whole).reshape(Y * CORE, HEADS, rows), (0, 2, 1))
    draft_logprobs = finish(place, [table_a, table_b, table_c, table_d], logs).reshape(
        HEADS, Y * CORE * rows, vocab_width
    )
    return (tree_out, draft_logprobs)


def solution(mesh):
    fine = Mesh(mesh.devices.reshape(Y, CORE, X, Z), ALL)
    return jax.shard_map(
        per_device,
        mesh=fine,
        in_specs=(
            P(ALL, None),
            P(ALL, None),
            P(ALL, None, None),
            P(ALL, None, None, None, None),
            P(ALL),
            P(ALL, None),
            P(ALL, None),
            P(),
            P(None, XZ),
            P(None, None, ALL),
            P(None, None, XZ),
            P(ALL, None),
            P(),
            P(),
            P(),
            P(),
        ),
        out_specs=(P(ALL, None), P(None, None, ALL)),
        check_vma=False,
    )
```

```python
import functools

import jax
import jax.numpy as jnp
from jax import lax
from jax.experimental import pallas as pl
from jax.experimental.pallas import tpu as pltpu
from jax.sharding import Mesh, PartitionSpec as P

BF = jnp.bfloat16
F32 = jnp.float32
QH = 8
KVH = 2
HD = 256
HEADS = 4
SOFTCAP = 30.0
Y, CORE, X, Z = 4, 2, 4, 4
EPS = 1e-06
ACC = 4
XZ = ("x", "z")
YC = ("y", "core")
ALL = ("y", "core", "x", "z")
GROUPS = ((0, 0), (0, 1), (1, 0), (1, 1), (3, 0), (3, 1), (2, 0), (2, 1))
CALLS = ((0, 2), (2, 6), (6, 8))
TILE = 256
VOCAB_BLOCK = 512
HIDDEN = -1e30
CONTRACT_LAST = (((1,), (1,)), ((), ()))


def attention_kernel(length_ref, q_ref, kv_ref, parents_ref, keys_ref, values_ref, out_ref, top, bottom, tree):
    rows = q_ref.shape[0]
    group = QH // KVH
    head, block = pl.program_id(0), pl.program_id(1)
    width = keys_ref.shape[0]
    queries = jnp.concatenate([q_ref[:, g * HD : (g + 1) * HD] for g in range(group)], axis=0)
    scale = HD ** (-0.5)

    @pl.when((head == 0) & (block == 0))
    def _():
        lanes = lax.broadcasted_iota(jnp.int32, (rows, rows), 1)
        subs = lax.broadcasted_iota(jnp.int32, (rows, rows), 0)
        reach = jnp.where((parents_ref[...] == lanes) | (subs == lanes), 1.0, 0.0)
        for _ in range(max(1, (rows - 1).bit_length())):
            half = reach.astype(BF)
            reach = jnp.minimum(jnp.dot(half, half, preferred_element_type=F32), 1.0)
        tree[...] = reach

    @pl.when(block == 0)
    def _():
        keys = kv_ref[0]
        scores = lax.dot_general(queries, keys, CONTRACT_LAST, preferred_element_type=F32)
        reach = tree[...]
        weights = jnp.exp(scores * scale) * jnp.concatenate([reach] * group, axis=0)
        bottom[...] = jnp.sum(weights, axis=1, keepdims=True)
        top[...] = jnp.dot(weights.astype(BF), kv_ref[1], preferred_element_type=F32)

    scores = lax.dot_general(queries, keys_ref[...], CONTRACT_LAST, preferred_element_type=F32)
    slots = block * width + lax.broadcasted_iota(jnp.int32, scores.shape, 1)
    weights = jnp.where(slots < length_ref[0], jnp.exp(scores * scale), 0.0)
    bottom[...] += jnp.sum(weights, axis=1, keepdims=True)
    top[...] += jnp.dot(weights.astype(BF), values_ref[...], preferred_element_type=F32)

    @pl.when(block == pl.num_programs(1) - 1)
    def _():
        attended = (top[...] / bottom[...]).astype(BF)
        for g in range(group):
            out_ref[:, g * HD : (g + 1) * HD] = attended[g * rows : (g + 1) * rows]


def attention(tree_q, tree_kv, kv_cache, cache_lengths, tree_parents):
    rows = tree_q.shape[0]
    group = QH // KVH
    slots = kv_cache.shape[3]
    block = min(1024, slots)
    kv = jnp.transpose(tree_kv, (1, 0, 2))
    spec = pl.BlockSpec
    return pl.pallas_call(
        attention_kernel,
        out_shape=jax.ShapeDtypeStruct((rows, QH * HD), BF),
        grid_spec=pltpu.PrefetchScalarGridSpec(
            num_scalar_prefetch=1,
            grid=(KVH, slots // block),
            in_specs=[
                spec((rows, group * HD), lambda k, b, n: (0, k)),
                spec((2, rows, HD), lambda k, b, n: (0, 0, k)),
                spec((rows, 1), lambda k, b, n: (0, 0)),
                spec((None, None, None, block, HD), lambda k, b, n: (0, 0, k, b, 0)),
                spec((None, None, None, block, HD), lambda k, b, n: (0, 1, k, b, 0)),
            ],
            out_specs=spec((rows, group * HD), lambda k, b, n: (0, k)),
            scratch_shapes=[
                pltpu.VMEM((group * rows, HD), F32),
                pltpu.VMEM((group * rows, 1), F32),
                pltpu.VMEM((rows, rows), F32),
            ],
        ),
        compiler_params=pltpu.CompilerParams(
            dimension_semantics=("arbitrary", "arbitrary"), vmem_limit_bytes=24 << 20
        ),
        cost_estimate=pl.CostEstimate(
            flops=4 * rows * QH * HD * slots,
            bytes_accessed=4 * KVH * slots * HD,
            transcendentals=rows * QH * slots,
        ),
    )(cache_lengths, tree_q, kv, tree_parents.reshape(rows, 1), kv_cache, kv_cache)


def logits_kernel(first, parts, place_ref, *refs):
    pieces = refs[: len(parts)]
    bounds_ref, embedding_ref, out_ref, totals_ref, rows_ref, running = refs[len(parts) :]
    step, steps = pl.program_id(0), pl.num_programs(0)
    groups, heads, count, depth = rows_ref.shape
    vocab = embedding_ref.shape[0]

    @pl.when(step == 0)
    def _():
        for piece, (group, low) in zip(pieces, parts):
            rows_ref[group, low : low + piece.shape[0]] = piece[...]
        running[...] = jnp.zeros_like(running)

    every = rows_ref[...].reshape(groups * heads * count, depth)
    ids = place_ref[0] + step * vocab + lax.broadcasted_iota(jnp.int32, (count, TILE), 1)
    for tile in range(0, vocab, TILE):
        products = lax.dot_general(
            every,
            embedding_ref[tile : tile + TILE],
            CONTRACT_LAST,
            preferred_element_type=F32,
        )
        for group in range(groups):
            bounds = bounds_ref[place_ref[1 + first + group]] - tile
            allowed = (ids >= bounds[:, 0:1]) & (ids < bounds[:, 1:2])
            for head in range(heads):
                low = (group * heads + head) * count
                bent = jnp.tanh(products[low : low + count] * (1.0 / SOFTCAP))
                terms = jnp.where(allowed, jnp.exp(bent * SOFTCAP), 0.0)
                kept = jnp.where(allowed, bent * SOFTCAP, HIDDEN).astype(BF)
                out_ref[group, head, :, tile : tile + TILE] = kept
                part = terms[:, :128]
                for lane in range(128, TILE, 128):
                    part = part + terms[:, lane : lane + 128]
                running[low : low + count] += part

    @pl.when(step == steps - 1)
    def _():
        size = heads * count
        for group in range(groups):
            totals_ref[group : group + 1, :] = jnp.sum(
                jnp.transpose(running[group * size : (group + 1) * size]), axis=0, keepdims=True
            )


def some_logits(first, shape, place, pieces, parts, bounds, embedding):
    groups, heads = shape
    count, depth = pieces[0].shape[1:]
    vocab_width = embedding.shape[0]
    vocab = min(VOCAB_BLOCK, vocab_width)
    size = groups * heads * count
    spec = pl.BlockSpec
    return pl.pallas_call(
        functools.partial(logits_kernel, first, parts),
        out_shape=(
            jax.ShapeDtypeStruct((groups, heads, count, vocab_width), BF),
            jax.ShapeDtypeStruct((groups, heads * count), F32),
        ),
        grid_spec=pltpu.PrefetchScalarGridSpec(
            num_scalar_prefetch=1,
            grid=(vocab_width // vocab,),
            in_specs=[
                spec(piece.shape, lambda j, p: (0, 0, 0), pipeline_mode=pl.Buffered(1))
                for piece in pieces
            ]
            + [
                spec(bounds.shape, lambda j, p: (0, 0, 0)),
                spec((vocab, depth), lambda j, p: (j, 0)),
            ],
            out_specs=(
                spec((groups, heads, count, vocab), lambda j, p: (0, 0, 0, j)),
                spec((groups, heads * count), lambda j, p: (0, 0)),
            ),
            scratch_shapes=[
                pltpu.VMEM((groups, heads, count, depth), BF),
                pltpu.VMEM((size, 128), F32),
            ],
        ),
        compiler_params=pltpu.CompilerParams(
            dimension_semantics=("arbitrary",), vmem_limit_bytes=50 << 20
        ),
        cost_estimate=pl.CostEstimate(
            flops=2 * size * vocab_width * depth,
            bytes_accessed=2 * vocab_width * depth + 2 * size * vocab_width,
            transcendentals=2 * size * vocab_width,
        ),
    )(place, *pieces, bounds, embedding)


def finish_kernel(place_ref, *refs):
    logs_ref, out_ref = refs[-2:]
    tables = ((refs[0],), refs[1:3], (refs[3],))
    step = pl.program_id(0)
    core = lax.rem(place_ref[1], CORE)
    for shared, (first, last) in zip(tables, CALLS):

        @pl.when((step >= first // CORE) & (step < last // CORE))
        def _(shared=shared):
            heads = HEADS // len(shared)
            for position in range(CORE):
                source = lax.rem(position + core, CORE)
                for head in range(HEADS):
                    values = shared[head // heads][source, head % heads].astype(F32)
                    shifted = values - logs_ref[position, :, head : head + 1]
                    out_ref[head, position] = jnp.where(
                        values > 0.5 * HIDDEN, shifted, 0.0
                    ).astype(BF)


def finish(place, tables, logs):
    count, vocab_width = tables[0].shape[2:]
    groups = len(GROUPS)
    spec = pl.BlockSpec

    def table_spec(table, first, last):
        return spec(
            (CORE, table.shape[1], count, vocab_width),
            lambda k, p: (jnp.clip(k - first // CORE, 0, (last - first) // CORE - 1), 0, 0, 0),
        )

    def pair(k, p):
        return lax.div(p[1 + CORE * k], CORE)

    calls = (CALLS[0], CALLS[1], CALLS[1], CALLS[2])
    return pl.pallas_call(
        finish_kernel,
        out_shape=jax.ShapeDtypeStruct((HEADS, groups, count, vocab_width), BF),
        grid_spec=pltpu.PrefetchScalarGridSpec(
            num_scalar_prefetch=1,
            grid=(groups // CORE,),
            in_specs=[table_spec(table, *call) for table, call in zip(tables, calls)]
            + [spec((CORE, count, HEADS), lambda k, p: (pair(k, p), 0, 0))],
            out_specs=spec(
                (HEADS, CORE, count, vocab_width), lambda k, p: (0, pair(k, p), 0, 0)
            ),
        ),
        compiler_params=pltpu.CompilerParams(
            dimension_semantics=("arbitrary",), vmem_limit_bytes=56 << 20
        ),
        cost_estimate=pl.CostEstimate(
            flops=3 * groups * HEADS * count * vocab_width,
            bytes_accessed=4 * groups * HEADS * count * vocab_width,
            transcendentals=0,
        ),
    )(place, *tables, logs)


def rms_scale(values, gain):
    floats = values.astype(F32)
    return (
        floats
        * lax.rsqrt(jnp.mean(floats * floats, axis=-1, keepdims=True) + EPS)
        * gain.astype(F32)
    )


def after(values, *earlier):
    return lax.optimization_barrier((values, earlier))[0]


def ring(values, axis, size, shift):
    return lax.ppermute(values, axis, [((i + shift) % size, i) for i in range(size)])


def copies_of(values, size):
    return lax.optimization_barrier(jnp.broadcast_to(values[None], (size,) + values.shape))


def swap(copies, axes):
    return lax.all_to_all(copies, axes, split_axis=0, concat_axis=0, tiled=True)


def spread(values, axes, size):
    return swap(copies_of(values, size), axes)


def in_order(blocks, index):
    size = len(blocks)
    ordered = []
    for position in range(size):
        shift = (position - index) % size
        block = blocks[0]
        for candidate in range(1, size):
            block = jnp.where(shift == candidate, blocks[candidate], block)
        ordered.append(block)
    return ordered


def out_projection(group, weights):
    rows = group.shape[0] // Z
    columns = jnp.concatenate(
        [jnp.dot(group, w, preferred_element_type=F32).astype(BF) for w in weights], axis=1
    )
    width = columns.shape[1] // X
    back = swap(columns.reshape(Z, rows, X * width), "z")
    by_x = in_order(
        [
            jnp.concatenate([back[z, :, d * width : (d + 1) * width] for z in range(Z)], axis=1)
            for d in range(X)
        ],
        lax.axis_index("x"),
    )
    return jnp.concatenate(by_x, axis=1)


def unit_terms(mlp_rows, weights):
    gate_part = jnp.dot(mlp_rows, weights[0], preferred_element_type=F32)
    upward = jnp.dot(mlp_rows, weights[1], preferred_element_type=F32)
    active = (jax.nn.gelu(gate_part, approximate=True) * upward).astype(BF)
    return lax.dot_general(
        active, weights[2], (((1,), (1,)), ((), ())), preferred_element_type=F32
    ).astype(BF)


def per_device(
    hidden,
    tree_q,
    tree_kv,
    kv_cache,
    cache_lengths,
    tree_parents,
    accepted,
    tenant_ranges,
    out_weight,
    mlp_weights,
    draft_weights,
    embedding,
    attn_post_gain,
    ff_pre_gain,
    ff_post_gain,
    final_gain,
):
    units = X * Z
    rows = units * ACC
    core = lax.axis_index("core")
    y = lax.axis_index("y")
    unit = lax.axis_index(XZ)
    weights = lax.all_gather(mlp_weights, YC, axis=2, tiled=True)
    chosen = (
        accepted[0][:, None] == jnp.arange(hidden.shape[0], dtype=jnp.int32)[None, :]
    ).astype(BF)

    def pick(values):
        return jnp.dot(chosen, values, preferred_element_type=F32).astype(BF)

    pieces = [ring(out_weight, "x", X, shift) for shift in range(1, X)]
    attended = attention(tree_q, tree_kv, kv_cache, cache_lengths, tree_parents)
    group = lax.all_gather(attended, "z", axis=0, tiled=True)
    projected = out_projection(group, [out_weight] + after(pieces, group))
    first = (hidden.astype(F32) + rms_scale(projected, attn_post_gain)).astype(BF)
    normed = rms_scale(first, ff_pre_gain).astype(BF)
    mlp_rows = lax.all_gather(normed, XZ, axis=0, tiled=True)

    path_rows = spread(pick(normed), XZ, units).reshape(rows, -1)
    path_terms = swap(unit_terms(path_rows, weights).reshape(units, ACC, -1), XZ)
    path_sum = jnp.sum(path_terms.astype(F32), axis=0)
    path = (pick(first).astype(F32) + rms_scale(path_sum, ff_post_gain)).astype(BF)
    path_normed = rms_scale(path, final_gain).astype(BF)
    group_path = spread(path_normed, XZ, units).reshape(rows, -1)

    width = draft_weights.shape[2]
    before = jnp.einsum("rd,hde->hre", group_path, draft_weights, preferred_element_type=F32)
    own_columns = lax.dynamic_slice_in_dim(group_path, unit * width, width, 1)
    drafts = (own_columns.astype(F32)[None] + jax.nn.silu(before)).astype(BF)
    draft_copies = copies_of(drafts, units)
    drafts = jnp.transpose(swap(draft_copies, XZ), (1, 2, 0, 3)).reshape(HEADS, rows, -1)

    mlp_partial = unit_terms(after(mlp_rows, draft_copies), weights)
    mlp_sum = lax.psum_scatter(after(mlp_partial, drafts), XZ, scatter_dimension=0, tiled=True)

    vocab_width = embedding.shape[0]
    start = lax.axis_index(ALL) * vocab_width
    order = [((y + dy) % Y) * CORE + (core + dc) % CORE for dy, dc in GROUPS]
    place = jnp.stack([start] + order).astype(jnp.int32)
    bounds = jnp.repeat(tenant_ranges, ACC, axis=0).reshape(Y * CORE, rows, 2)
    half = HEADS // 2
    pair = ((0, 0), (1, 0))
    four = pair + ((2, 0), (3, 0))
    low = drafts[:half]
    up_low, down_low = ring(low, "y", Y, 1), ring(low, "y", Y, 3)
    beside = ring(drafts, "core", CORE, 1)
    high = drafts[half:]
    up_high, down_high = ring(high, "y", Y, 1), ring(high, "y", Y, 3)
    table_a, totals_a = some_logits(
        0, (2, HEADS), place, [drafts, beside], pair, bounds, embedding
    )
    up_low, down_low = after([up_low, down_low], totals_a)
    across_low = ring(up_low, "y", Y, 1)
    beside_low = [ring(piece, "core", CORE, 1) for piece in (up_low, down_low)]
    table_b, totals_b = some_logits(
        2,
        (4, half),
        place,
        [up_low, beside_low[0], down_low, beside_low[1]],
        four,
        bounds,
        embedding,
    )
    up_high, down_high = after([up_high, down_high], totals_b)
    across_high = ring(down_high, "y", Y, 3)
    beside_high = [ring(piece, "core", CORE, 1) for piece in (up_high, down_high)]
    table_c, totals_c = some_logits(
        2,
        (4, half),
        place,
        [up_high, beside_high[0], down_high, beside_high[1]],
        four,
        bounds,
        embedding,
    )
    across = after([across_low, across_high], totals_c)
    beside_across = [ring(piece, "core", CORE, 1) for piece in across]
    table_d, totals_d = some_logits(
        6,
        (2, HEADS),
        place,
        across + beside_across,
        ((0, 0), (0, half), (1, 0), (1, half)),
        bounds,
        embedding,
    )
    totals_b = jnp.concatenate([totals_b, totals_c], axis=1)
    sums = jnp.concatenate([totals_a, totals_b, totals_d], axis=0)
    here = place[1:, None] == jnp.arange(Y * CORE, dtype=jnp.int32)[None, :]
    sums = jnp.sum(jnp.where(here[:, :, None], sums[:, None, :], 0.0), axis=0)
    sums = jnp.sum(spread(sums, XZ, units), axis=0)
    around = [ring(sums, "y", Y, shift) for shift in range(1, Y)]
    mlp_sum = after(mlp_sum, sums)
    tree_out = (first.astype(F32) + rms_scale(mlp_sum, ff_post_gain)).astype(BF)
    around = after(around, tree_out)
    whole = sums + around[0] + around[1] + around[2]
    whole = whole + ring(whole, "core", CORE, 1)
    logs = jnp.transpose(jnp.log(whole).reshape(Y * CORE, HEADS, rows), (0, 2, 1))
    draft_logprobs = finish(place, [table_a, table_b, table_c, table_d], logs).reshape(
        HEADS, Y * CORE * rows, vocab_width
    )
    return (tree_out, draft_logprobs)


def solution(mesh):
    fine = Mesh(mesh.devices.reshape(Y, CORE, X, Z), ALL)
    return jax.shard_map(
        per_device,
        mesh=fine,
        in_specs=(
            P(ALL, None),
            P(ALL, None),
            P(ALL, None, None),
            P(ALL, None, None, None, None),
            P(ALL),
            P(ALL, None),
            P(ALL, None),
            P(),
            P(None, XZ),
            P(None, None, ALL),
            P(None, None, XZ),
            P(ALL, None),
            P(),
            P(),
            P(),
            P(),
        ),
        out_specs=(P(ALL, None), P(None, None, ALL)),
        check_vma=False,
    )
```
